512 devices in a mesh: gx: 16 (over y_lo, x), gy: 16 (over z, core), gz: 2 (over y_hi).
Axes of the slice: x: 4, y: 8 (y_hi: 2, y_lo: 4; y = y_hi * 4 + y_lo), z: 8, core: 2. Of those that a mesh axis runs over, the one named last changes fastest.
Arguments:
- droplets: float32 [2, 16, 16, 8, 8192], P('gz', 'gx', 'gy'), as said below
- cell_index: int32 [2, 16, 16, 8192], P('gz', 'gx', 'gy'), may hold values from 0 to 16383
- crossing: int32 [2, 16, 16, 4, 512], P('gz', 'gx', 'gy'), may hold values from 0 to 8191, as said below
- crossing_count: int32 [2, 16, 16, 4], P('gz', 'gx', 'gy'), may hold values from 128 to 512, as said below
- saturation: float32 [128, 16, 16, 256], P('gz', 'gx', 'gy'), may hold values from -4 to 4
- velocity: float32 [128, 16, 16, 256], P('gz', 'gx', 'gy'), may hold values from -6 to 6
- pressure: float32 [128, 16, 16, 256], P('gz', 'gx', 'gy'), may hold values from -6 to 6
- block_inverse: float32 [4, 128], replicated
- forward_map: float32 [4, 128], replicated
- backward_map: float32 [4, 128], replicated
Outputs:
- residents: float32 [2, 16, 16, 8, 8192], P('gz', 'gx', 'gy')
- arrivals: float32 [2, 16, 16, 4, 8, 512], P('gz', 'gx', 'gy')
- new_velocity: float32 [128, 16, 16, 256], P('gz', 'gx', 'gy')
- new_pressure: float32 [128, 16, 16, 256], P('gz', 'gx', 'gy')
The draws below stay inside these ranges and needn't reach their ends.
Inputs may be any that keep to these rules, and one draw needn't show every extreme that they name: `droplets`: multiplicity (value 1) is positive and radius (value 0) at least 0.5 in every record. `crossing`: indices into the tile's droplets; no droplet appears twice among a tile's four faces, padding slots included. `crossing_count`: some face of every tile uses all 512 slots.
All inputs are finite; a program needn't handle non-finite values.
Results may differ from the reference program's by a relative error of at most 0.0003.
Values sent between devices are 32-bit elements; how exact they have to be, the bound alone decides.
No kernel may reach another device: no remote copies, remote signals or barrier semaphores. Data moves between devices by JAX's collectives and lax.ppermute only.
A program may use at most 64 MiB of HBM per device.

```python
import jax
import jax.numpy as jnp
from jax import lax

CX = 8
CY = 32
CZ = 64
REC = 8
DROP_DEV = 8192
SLOTS = 512
NZ = 128
N_GX = 16
N_GY = 16
N_GZ = 2


def uniform_at(key, index, array_dims):
    return jax.random.uniform(jax.random.fold_in(key, index), array_dims, jnp.float32)


def draw_droplets(key, part):
    array_dims = (N_GZ, N_GX, N_GY, DROP_DEV)
    radius = 0.5 + uniform_at(key, 1, array_dims)
    multiplicity = 0.3 * jnp.exp(jnp.log(10.0) * uniform_at(key, 2, array_dims))
    dry_radius = 0.05 + 0.25 * uniform_at(key, 3, array_dims)
    solute = 0.1 + 1.1 * uniform_at(key, 4, array_dims)
    rows = [radius, multiplicity, dry_radius, solute, uniform_at(key, 5, array_dims), uniform_at(key, 6, array_dims), uniform_at(key, 7, array_dims), 0.2 + 0.8 * uniform_at(key, 8, array_dims)]
    return jnp.stack(rows, axis=3)


def draw_crossing(key, part):
    device_keys = jax.random.split(jax.random.fold_in(key, 21), N_GZ * N_GX * N_GY)
    shuffled = jax.vmap(lambda one_key: jax.random.permutation(one_key, DROP_DEV)[:4 * SLOTS])(device_keys)
    return shuffled.reshape(N_GZ, N_GX, N_GY, 4, SLOTS).astype(jnp.int32)


def draw_crossing_count(key, part):
    base_counts = jax.random.randint(jax.random.fold_in(key, 31), (N_GZ, N_GX, N_GY, 4), SLOTS // 4, SLOTS + 1)
    full_face = jax.random.randint(jax.random.fold_in(key, 32), (N_GZ, N_GX, N_GY), 0, 4)
    face_ids = jnp.arange(4, dtype=jnp.int32)
    return jnp.where(face_ids == full_face[..., None], SLOTS, base_counts).astype(jnp.int32)


def draw_block_inverse(key, part):
    array_dims = (N_GZ * CZ,)
    first = 0.05 * jnp.exp(jnp.log(3.0) * uniform_at(key, 41, array_dims))
    second = 0.05 * jnp.exp(jnp.log(3.0) * uniform_at(key, 42, array_dims))
    middle = jnp.sqrt(first * second)
    upper_sign = jnp.where(uniform_at(key, 43, array_dims) < 0.5, -1.0, 1.0)
    lower_sign = jnp.where(uniform_at(key, 44, array_dims) < 0.5, -1.0, 1.0)
    upper_off = upper_sign * middle * (0.2 + 0.2 * uniform_at(key, 45, array_dims))
    lower_off = lower_sign * middle * (0.2 + 0.2 * uniform_at(key, 46, array_dims))
    return jnp.stack([first, upper_off, lower_off, second])


def rotation_blocks(key, spectral):
    array_dims = spectral.shape
    flipped = jnp.where(uniform_at(key, 51, array_dims) < 0.5, -1.0, 1.0)
    rotation = flipped * (0.25 + 0.35 * uniform_at(key, 52, array_dims))
    return jnp.stack([spectral * jnp.cos(rotation), -spectral * jnp.sin(rotation), spectral * jnp.sin(rotation), spectral * jnp.cos(rotation)])


def draw_forward_map(key, part):
    array_dims = (N_GZ * CZ,)
    spectral = 0.95 + 0.035 * uniform_at(key, 53, array_dims)
    return rotation_blocks(key, spectral)


def draw_backward_map(key, part):
    array_dims = (N_GZ * CZ,)
    spectral = 0.9 + 0.08 * uniform_at(key, 54, array_dims)
    return rotation_blocks(jax.random.fold_in(key, 55), spectral)


def set_ends(result, own_key, least, high):
    longest = result.shape.index(max(result.shape))
    spots = []
    for shift in (0, 1):
        where = [jax.random.randint(jax.random.fold_in(own_key, axis), (), 0, length) for axis, length in enumerate(result.shape)]
        where[longest] = (where[longest] + shift) % result.shape[longest]
        spots.append(tuple(where))
    return result.at[spots[0]].set(least).at[spots[1]].set(high)


def block_scale(stream_key, extent, cuts, least, high):
    level = 1.0
    for dim, parts in cuts:
        draws = jax.random.uniform(jax.random.fold_in(jax.random.fold_in(stream_key, 6), dim), (parts,), jnp.float32, least / len(cuts), high / len(cuts))
        level = level * jnp.repeat(jnp.exp(draws), extent[dim] // parts).reshape((-1,) + (1,) * (len(extent) - 1 - dim))
    return level


def centred(own_key, shape, scale, bound, cuts=(), kind=jnp.bfloat16):
    gain = block_scale(own_key, shape, cuts, -0.22, 0.18) if cuts else 1.0
    drawn = jax.random.normal(own_key, shape, jnp.float32) * scale * gain
    return jnp.minimum(jnp.maximum(drawn, -bound), bound).astype(kind)


def setup_inputs(seed: int = 0) -> dict:
    key_of = jax.random.split(jax.random.key(seed), 11)
    droplets = draw_droplets(jax.random.fold_in(key_of[10], 71), 0)
    cell_index = set_ends(jax.random.randint(key_of[1], (N_GZ, N_GX, N_GY, DROP_DEV), 0, CZ * CX * CY), jax.random.fold_in(key_of[1], 1), 0, (CZ * CX * CY) - 1).astype(jnp.int32)
    crossing = draw_crossing(jax.random.fold_in(key_of[10], 71), 0)
    crossing_count = draw_crossing_count(jax.random.fold_in(key_of[10], 71), 0)
    saturation = centred(key_of[4], (NZ, N_GX, N_GY, CX * CY), 0.6, 4.0, ((0, 2), (1, 16), (2, 16)), jnp.float32)
    velocity = centred(key_of[5], (NZ, N_GX, N_GY, CX * CY), 1.0, 6.0, ((0, 2), (1, 16), (2, 16)), jnp.float32)
    pressure = centred(key_of[6], (NZ, N_GX, N_GY, CX * CY), 1.0, 6.0, ((0, 2), (1, 16), (2, 16)), jnp.float32)
    block_inverse = draw_block_inverse(jax.random.fold_in(key_of[10], 71), 0)
    forward_map = draw_forward_map(jax.random.fold_in(key_of[10], 71), 0)
    backward_map = draw_backward_map(jax.random.fold_in(key_of[10], 71), 0)
    return {"droplets": droplets, "cell_index": cell_index, "crossing": crossing, "crossing_count": crossing_count, "saturation": saturation, "velocity": velocity, "pressure": pressure, "block_inverse": block_inverse, "forward_map": forward_map, "backward_map": backward_map}


GROW = 0.4
CURVATURE = 0.05
FLOOR_SQ = 0.09
BUOYANCY = 0.5

def compose(latter, former):
    return jnp.stack([latter[0] * former[0] + latter[1] * former[2], latter[0] * former[1] + latter[1] * former[3], latter[2] * former[0] + latter[3] * former[2], latter[2] * former[1] + latter[3] * former[3]])

def apply_pair(matrix, vector):
    return jnp.stack([matrix[0] * vector[0] + matrix[1] * vector[1], matrix[2] * vector[0] + matrix[3] * vector[1]])

def condense(records, flat_field, target, occupied):
    excess = flat_field[target]
    radius = jnp.where(occupied, records[..., 0, :], 1.0)
    dry_radius = records[..., 2, :]
    solute = records[..., 3, :]
    radius_cubed = radius * radius * radius
    squared = jnp.maximum(radius * radius + GROW * (excess - CURVATURE / radius + solute * dry_radius * dry_radius * dry_radius / radius_cubed), FLOOR_SQ)
    grown_radius = jnp.sqrt(squared)
    condensed = jnp.where(occupied, records[..., 1, :] * (grown_radius * grown_radius * grown_radius - radius_cubed), 0.0)
    updated = jnp.concatenate([grown_radius[..., None, :], records[..., 1:, :]], axis=-2)
    updated = jnp.where(occupied[..., None, :], updated, 0.0)
    return (updated, condensed)

def emit_packets(records, cell_ids, leavers, live_count):
    slot_count = leavers.shape[1]
    slot_ids = lax.broadcasted_iota(jnp.int32, (4, slot_count), 1)
    face_ids = lax.broadcasted_iota(jnp.int32, (4, slot_count), 0)
    in_use = slot_ids < live_count[:, None]
    picked = jnp.moveaxis(jnp.take(records, leavers, axis=1), 1, 0)
    source = cell_ids[leavers]
    height = source // (CX * CY)
    cell_x = source // CY % CX
    cell_y = source % CY
    new_x = jnp.where(face_ids == 0, 0, jnp.where(face_ids == 1, CX - 1, cell_x))
    new_y = jnp.where(face_ids == 2, 0, jnp.where(face_ids == 3, CY - 1, cell_y))
    target = (height * (CX * CY) + new_x * CY + new_y).astype(jnp.int32)
    packet = jnp.concatenate([picked, target.astype(records.dtype)[:, None, :]], axis=1)
    packet = jnp.where(in_use[:, None, :], packet, 0.0)
    departed = jnp.zeros((records.shape[1],), jnp.int32).at[leavers.reshape(-1)].add(in_use.reshape(-1).astype(jnp.int32))
    return (packet, departed == 0)

def settle(records, cell_ids, staying, packet_in, sat_tile, vel_tile, pres_tile):
    flat_field = sat_tile.reshape(-1)
    resident, res_mass = condense(records, flat_field, cell_ids, staying)
    incoming = packet_in[:, :REC]
    target = packet_in[:, REC].astype(jnp.int32)
    occupied = incoming[:, 1] > 0
    arrived, arr_mass = condense(incoming, flat_field, target, occupied)
    heating = jax.ops.segment_sum(jnp.concatenate([res_mass, arr_mass.reshape(-1)]), jnp.concatenate([cell_ids, target.reshape(-1)]), num_segments=flat_field.shape[0])
    forcing = jnp.stack([vel_tile + BUOYANCY * heating.reshape(vel_tile.shape), pres_tile])
    return (resident, arrived, forcing)

def over_devices(device_fn):
    return jax.vmap(jax.vmap(jax.vmap(device_fn)))

def to_tiles(grid_field):
    return grid_field.reshape(N_GZ, CZ, N_GX, N_GY, CX * CY).transpose(0, 2, 3, 1, 4)

def solve_columns(columns, block_inverse, forward_map, backward_map):
    driven = apply_pair(block_inverse[:, :, None], columns)

    def advance(carried, inputs):
        coupling, source = inputs
        carried = source + apply_pair(coupling, carried)
        return (carried, carried)
    start = jnp.zeros((2, columns.shape[2]), columns.dtype)
    _, upward = lax.scan(advance, start, (forward_map.T, jnp.moveaxis(driven, 1, 0)))
    _, downward = lax.scan(advance, start, (backward_map.T, upward), reverse=True)
    return jnp.moveaxis(downward, 0, 1)

def reference(droplets, cell_index, crossing, crossing_count, saturation, velocity, pressure, block_inverse, forward_map, backward_map):
    packets, staying = over_devices(emit_packets)(droplets, cell_index, crossing, crossing_count)
    incoming = jnp.stack([jnp.roll(packets[:, :, :, 0], 1, axis=1), jnp.roll(packets[:, :, :, 1], -1, axis=1), jnp.roll(packets[:, :, :, 2], 1, axis=2), jnp.roll(packets[:, :, :, 3], -1, axis=2)], axis=3)
    residents, arrivals, forcing = over_devices(settle)(droplets, cell_index, staying, incoming, to_tiles(saturation), to_tiles(velocity), to_tiles(pressure))
    columns = forcing.transpose(3, 0, 4, 1, 2, 5).reshape(2, N_GZ * CZ, -1)
    solved = solve_columns(columns, block_inverse, forward_map, backward_map)
    new_velocity = solved[0].reshape(N_GZ * CZ, N_GX, N_GY, CX * CY)
    new_pressure = solved[1].reshape(N_GZ * CZ, N_GX, N_GY, CX * CY)
    return (residents, arrivals, new_velocity, new_pressure)
```

```python
import math

import jax
import jax.numpy as jnp
from jax import lax
from jax.sharding import PartitionSpec as P
from jax.experimental import pallas as pl
from jax.experimental.pallas import tpu as pltpu

CX = 8
CY = 32


GROW = 0.4
CURVATURE = 0.05
FLOOR_SQ = 0.09
BUOYANCY = 0.5
EXACT = lax.Precision.HIGHEST


def shifted(value, axis, steps):
    count = lax.axis_size(axis)
    pairs = [(source, (source + steps) % count) for source in range(count)]
    return lax.ppermute(value, axis, pairs)


def compose(latter, former):
    return jnp.stack(
        [
            latter[0] * former[0] + latter[1] * former[2],
            latter[0] * former[1] + latter[1] * former[3],
            latter[2] * former[0] + latter[3] * former[2],
            latter[2] * former[1] + latter[3] * former[3],
        ]
    )


def apply_pair(matrix, vector):
    return jnp.stack(
        [
            matrix[0] * vector[0] + matrix[1] * vector[1],
            matrix[2] * vector[0] + matrix[3] * vector[1],
        ]
    )


def linear_scan(matrices, vectors):

    def combine(former, latter):
        return (compose(latter[0], former[0]), apply_pair(latter[0], former[1]) + latter[1])

    return lax.associative_scan(combine, (matrices, vectors), axis=1)


def one_hot_of(index, width, dtype):
    return (index[:, None] == lax.broadcasted_iota(jnp.int32, (1, width), 1)).astype(dtype)


def read_cells(field, cell_ids):
    level_count, column_count = field.shape
    total = cell_ids.shape[0]
    block_rows = math.gcd(total, 2048)

    def read_one_block(ids_block):
        levels = one_hot_of(ids_block // column_count, level_count, jnp.float32)
        rows = jnp.dot(levels, field, precision=EXACT, preferred_element_type=jnp.float32)
        return jnp.sum(
            rows * one_hot_of(ids_block % column_count, column_count, jnp.float32), axis=1
        )

    return lax.map(read_one_block, cell_ids.reshape(-1, block_rows)).reshape(-1)


def add_cells(values, cell_ids, level_count, column_count):
    total = cell_ids.shape[0]
    block_rows = math.gcd(total, 2048)

    def add_one_block(carried, inputs):
        ids_block, value_block = inputs
        levels = (
            one_hot_of(ids_block // column_count, level_count, jnp.float32) * value_block[:, None]
        )
        columns = one_hot_of(ids_block % column_count, column_count, jnp.float32)
        return (
            carried
            + jnp.einsum(
                "nl,nc->lc", levels, columns, precision=EXACT, preferred_element_type=jnp.float32
            ),
            None,
        )

    start = jnp.zeros((level_count, column_count), jnp.float32)
    summed, _ = lax.scan(
        add_one_block, start, (cell_ids.reshape(-1, block_rows), values.reshape(-1, block_rows))
    )
    return summed


def condense(records, excess, occupied):
    radius = jnp.where(occupied, records[..., 0, :], 1.0)
    dry_radius = records[..., 2, :]
    solute = records[..., 3, :]
    radius_cubed = radius * radius * radius
    squared = jnp.maximum(
        radius * radius
        + GROW
        * (
            excess
            - CURVATURE / radius
            + solute * dry_radius * dry_radius * dry_radius / radius_cubed
        ),
        FLOOR_SQ,
    )
    grown_radius = jnp.sqrt(squared)
    condensed = jnp.where(
        occupied,
        records[..., 1, :] * (grown_radius * grown_radius * grown_radius - radius_cubed),
        0.0,
    )
    updated = jnp.concatenate([grown_radius[..., None, :], records[..., 1:, :]], axis=-2)
    updated = jnp.where(occupied[..., None, :], updated, 0.0)
    return (updated, condensed)


def emit_packets(records, cell_ids, leavers, live_count, width_x, width_y):
    record_width, drop_count = records.shape
    slot_count = leavers.shape[1]
    slot_ids = lax.broadcasted_iota(jnp.int32, (4, slot_count), 1)
    face_ids = lax.broadcasted_iota(jnp.int32, (4, slot_count), 0)
    in_use = slot_ids < live_count[:, None]
    inner = min(128, drop_count)
    outer = drop_count // inner
    table = jnp.concatenate([records, cell_ids.astype(jnp.float32)[None, :]], axis=0).reshape(
        record_width + 1, outer, inner
    )
    flat_leavers = leavers.reshape(-1)
    flat_use = in_use.reshape(-1).astype(jnp.bfloat16)
    block_rows = math.gcd(4 * slot_count, 1024)

    def pick_block(inputs):
        ids_block, use_block = inputs
        upper = one_hot_of(ids_block // inner, outer, jnp.float32)
        lower = one_hot_of(ids_block % inner, inner, jnp.float32)
        rows = jnp.einsum(
            "nh,rhl->nrl", upper, table, precision=EXACT, preferred_element_type=jnp.float32
        )
        picked_block = jnp.sum(rows * lower[:, None, :], axis=2)
        upper_used = upper.astype(jnp.bfloat16) * use_block[:, None]
        counts = jnp.einsum(
            "nh,nl->hl", upper_used, lower.astype(jnp.bfloat16), preferred_element_type=jnp.float32
        )
        return (picked_block, counts)

    picked_blocks, count_blocks = lax.map(
        pick_block, (flat_leavers.reshape(-1, block_rows), flat_use.reshape(-1, block_rows))
    )
    picked_all = picked_blocks.reshape(4, slot_count, record_width + 1)
    departed = jnp.sum(count_blocks, axis=0).reshape(-1)
    picked = jnp.moveaxis(picked_all[:, :, :record_width], 2, 1)
    source = (picked_all[:, :, record_width] + 0.5).astype(jnp.int32)
    height = source // (width_x * width_y)
    cell_x = source // width_y % width_x
    cell_y = source % width_y
    new_x = jnp.where(face_ids == 0, 0, jnp.where(face_ids == 1, width_x - 1, cell_x))
    new_y = jnp.where(face_ids == 2, 0, jnp.where(face_ids == 3, width_y - 1, cell_y))
    target = height * (width_x * width_y) + new_x * width_y + new_y
    packet = jnp.concatenate([picked, target.astype(records.dtype)[:, None, :]], axis=1)
    packet = jnp.where(in_use[:, None, :], packet, 0.0)
    return (packet, departed == 0.0)


def settle(records, cell_ids, staying, packet_in, sat_tile, vel_tile, pres_tile):
    level_count, column_count = sat_tile.shape
    record_width = records.shape[0]
    incoming = packet_in[:, :record_width]
    target = (packet_in[:, record_width] + 0.5).astype(jnp.int32)
    occupied = incoming[:, 1] > 0
    all_ids = jnp.concatenate([cell_ids, target.reshape(-1)])
    excess = read_cells(sat_tile, all_ids)
    drop_count = cell_ids.shape[0]
    resident, res_mass = condense(records, excess[:drop_count], staying)
    arrived, arr_mass = condense(incoming, excess[drop_count:].reshape(target.shape), occupied)
    heating = add_cells(
        jnp.concatenate([res_mass, arr_mass.reshape(-1)]), all_ids, level_count, column_count
    )
    forcing = jnp.stack([vel_tile + BUOYANCY * heating, pres_tile])
    return (resident, arrived, forcing)


def along_x(packet_face, offset):
    return shifted(packet_face, "gx", offset)


def along_y(packet_face, offset):
    return shifted(packet_face, "gy", offset)


def solve_kernel(
    off_ref, maps_ref, fv_ref, fp_ref, sv_ref, sp_ref, last_ref, first_ref, ex_ref, xv_ref, xp_ref
):
    levels = fv_ref.shape[0]
    off = off_ref[0]
    upper = jnp.where(off > 0, 1.0, 0.0).astype(jnp.float32)
    lane = lax.broadcasted_iota(jnp.int32, (1, 128), 1)
    e0 = jnp.where(lane == 0, 1.0, 0.0).astype(jnp.float32)
    e1 = jnp.where(lane == 1, 1.0, 0.0).astype(jnp.float32)
    zero = jnp.zeros(fv_ref.shape[1:], jnp.float32)[None, :]

    def forward(k, carry):
        uv, up, xv, xp = carry
        level = off + k
        b0 = maps_ref[0, level]
        b1 = maps_ref[1, level]
        b2 = maps_ref[2, level]
        b3 = maps_ref[3, level]
        f0 = maps_ref[4, level]
        f1 = maps_ref[5, level]
        f2 = maps_ref[6, level]
        f3 = maps_ref[7, level]
        gv = fv_ref[pl.ds(k, 1), :]
        gp = fp_ref[pl.ds(k, 1), :]
        nuv = (b0 * gv + b1 * gp) + (f0 * uv + f1 * up)
        nup = (b2 * gv + b3 * gp) + (f2 * uv + f3 * up)
        nxv = f0 * xv + f1 * xp
        nxp = f2 * xv + f3 * xp
        sv_ref[pl.ds(k, 1), :] = nuv
        sp_ref[pl.ds(k, 1), :] = nup
        xv_ref[pl.ds(k, 1), :] = nxv
        xp_ref[pl.ds(k, 1), :] = nxp
        return (nuv, nup, nxv, nxp)

    uv, up, xv, xp = lax.fori_loop(
        0, levels, forward, (zero, zero, upper * e0, upper * e1)
    )
    last_ref[0:1, :] = uv
    last_ref[1:2, :] = up
    last_ref[2:4, :] = jnp.zeros((2, uv.shape[1]), jnp.float32)
    last_ref[2:3, 0:128] = xv
    last_ref[3:4, 0:128] = xp

    def backward(step, carry):
        sv, sp, yv, yp = carry
        k = levels - 1 - step
        level = off + k
        c0 = maps_ref[8, level]
        c1 = maps_ref[9, level]
        c2 = maps_ref[10, level]
        c3 = maps_ref[11, level]
        nsv = sv_ref[pl.ds(k, 1), :] + (c0 * sv + c1 * sp)
        nsp = sp_ref[pl.ds(k, 1), :] + (c2 * sv + c3 * sp)
        nyv = xv_ref[pl.ds(k, 1), :] + (c0 * yv + c1 * yp)
        nyp = xp_ref[pl.ds(k, 1), :] + (c2 * yv + c3 * yp)
        sv_ref[pl.ds(k, 1), :] = nsv
        sp_ref[pl.ds(k, 1), :] = nsp
        ex_ref[0, pl.ds(k, 1), :] = nyv
        ex_ref[1, pl.ds(k, 1), :] = nyp
        return (nsv, nsp, nyv, nyp)

    lower = 1.0 - upper
    sv, sp, yv, yp = lax.fori_loop(
        0, levels, backward, (zero, zero, lower * e0, lower * e1)
    )
    first_ref[0:1, :] = sv
    first_ref[1:2, :] = sp
    first_ref[2:4, :] = jnp.zeros((2, sv.shape[1]), jnp.float32)
    first_ref[2:3, 0:128] = yv
    first_ref[3:4, 0:128] = yp


def solve_local(forcing, block_inverse, forward_map, backward_map):
    _, levels, columns = forcing.shape
    offset = jnp.full((1,), lax.axis_index("gz") * levels, jnp.int32)
    maps = jnp.concatenate([block_inverse, forward_map, backward_map], axis=0)
    smem = pl.BlockSpec(memory_space=pltpu.SMEM)
    vmem = pl.BlockSpec(memory_space=pltpu.VMEM)
    return pl.pallas_call(
        solve_kernel,
        out_shape=(
            jax.ShapeDtypeStruct((levels, columns), jnp.float32),
            jax.ShapeDtypeStruct((levels, columns), jnp.float32),
            jax.ShapeDtypeStruct((4, columns), jnp.float32),
            jax.ShapeDtypeStruct((4, columns), jnp.float32),
            jax.ShapeDtypeStruct((2, levels, 128), jnp.float32),
        ),
        in_specs=[smem, smem, vmem, vmem],
        out_specs=(vmem, vmem, vmem, vmem, vmem),
        scratch_shapes=[
            pltpu.VMEM((levels, 128), jnp.float32),
            pltpu.VMEM((levels, 128), jnp.float32),
        ],
        cost_estimate=pl.CostEstimate(
            flops=40 * levels * columns, bytes_accessed=24 * levels * columns, transcendentals=0
        ),
    )(offset, maps, forcing[0], forcing[1])


def solve_split(forcing, block_inverse, forward_map, backward_map):
    assert lax.axis_size("gz") == 2
    sv, sp, last, first, extra = solve_local(forcing, block_inverse, forward_map, backward_map)
    lower = lax.axis_index("gz") == 0
    message = jnp.where(lower, last, first)
    received = lax.ppermute(message, "gz", [(0, 1), (1, 0)])
    r0 = received[0] + received[2, 0] * last[0] + received[2, 1] * last[1]
    r1 = received[1] + received[3, 0] * last[0] + received[3, 1] * last[1]
    new_v = sv + extra[0, :, 0:1] * r0[None, :] + extra[0, :, 1:2] * r1[None, :]
    new_p = sp + extra[1, :, 0:1] * r0[None, :] + extra[1, :, 1:2] * r1[None, :]
    return new_v, new_p


def body(
    droplets,
    cell_index,
    crossing,
    crossing_count,
    saturation,
    velocity,
    pressure,
    block_inverse,
    forward_map,
    backward_map,
):
    records = droplets[0, 0, 0]
    cell_ids = cell_index[0, 0, 0]
    sat_tile = saturation[:, 0, 0, :]
    packet, staying = emit_packets(
        records, cell_ids, crossing[0, 0, 0], crossing_count[0, 0, 0], CX, CY
    )
    from_west = along_x(packet[0], 1)
    from_east = along_x(packet[1], -1)
    from_south = along_y(packet[2], 1)
    from_north = along_y(packet[3], -1)
    packet_in = jnp.stack([from_west, from_east, from_south, from_north])
    resident, arrived, forcing = settle(
        records, cell_ids, staying, packet_in, sat_tile, velocity[:, 0, 0, :], pressure[:, 0, 0, :]
    )
    solved_v, solved_p = solve_split(forcing, block_inverse, forward_map, backward_map)
    new_velocity = solved_v[:, None, None, :]
    new_pressure = solved_p[:, None, None, :]
    return (resident[None, None, None], arrived[None, None, None], new_velocity, new_pressure)


def solution(mesh):
    return jax.shard_map(
        body,
        mesh=mesh,
        in_specs=(
            P("gz", "gx", "gy", None, None),
            P("gz", "gx", "gy", None),
            P("gz", "gx", "gy", None, None),
            P("gz", "gx", "gy", None),
            P("gz", "gx", "gy", None),
            P("gz", "gx", "gy", None),
            P("gz", "gx", "gy", None),
            P(),
            P(),
            P(),
        ),
        out_specs=(
            P("gz", "gx", "gy", None, None),
            P("gz", "gx", "gy", None, None, None),
            P("gz", "gx", "gy", None),
            P("gz", "gx", "gy", None),
        ),
        check_vma=False,
    )
```

```python
import math

import jax
import jax.numpy as jnp
from jax import lax
from jax.sharding import PartitionSpec as P
from jax.experimental import pallas as pl
from jax.experimental.pallas import tpu as pltpu

CX = 8
CY = 32


GROW = 0.4
CURVATURE = 0.05
FLOOR_SQ = 0.09
BUOYANCY = 0.5
EXACT = lax.Precision.HIGHEST


def shifted(value, axis, steps):
    count = lax.axis_size(axis)
    pairs = [(source, (source + steps) % count) for source in range(count)]
    return lax.ppermute(value, axis, pairs)


def compose(latter, former):
    return jnp.stack(
        [
            latter[0] * former[0] + latter[1] * former[2],
            latter[0] * former[1] + latter[1] * former[3],
            latter[2] * former[0] + latter[3] * former[2],
            latter[2] * former[1] + latter[3] * former[3],
        ]
    )


def apply_pair(matrix, vector):
    return jnp.stack(
        [
            matrix[0] * vector[0] + matrix[1] * vector[1],
            matrix[2] * vector[0] + matrix[3] * vector[1],
        ]
    )


def linear_scan(matrices, vectors):

    def combine(former, latter):
        return (compose(latter[0], former[0]), apply_pair(latter[0], former[1]) + latter[1])

    return lax.associative_scan(combine, (matrices, vectors), axis=1)


def one_hot_of(index, width, dtype):
    return (index[:, None] == lax.broadcasted_iota(jnp.int32, (1, width), 1)).astype(dtype)


def read_cells(field, cell_ids):
    level_count, column_count = field.shape
    total = cell_ids.shape[0]
    block_rows = math.gcd(total, 2048)

    def read_one_block(ids_block):
        levels = one_hot_of(ids_block // column_count, level_count, jnp.float32)
        rows = jnp.dot(levels, field, precision=EXACT, preferred_element_type=jnp.float32)
        return jnp.sum(
            rows * one_hot_of(ids_block % column_count, column_count, jnp.float32), axis=1
        )

    return lax.map(read_one_block, cell_ids.reshape(-1, block_rows)).reshape(-1)


def add_cells(values, cell_ids, level_count, column_count):
    total = cell_ids.shape[0]
    block_rows = math.gcd(total, 2048)

    def add_one_block(carried, inputs):
        ids_block, value_block = inputs
        levels = (
            one_hot_of(ids_block // column_count, level_count, jnp.float32) * value_block[:, None]
        )
        columns = one_hot_of(ids_block % column_count, column_count, jnp.float32)
        return (
            carried
            + jnp.einsum(
                "nl,nc->lc", levels, columns, precision=EXACT, preferred_element_type=jnp.float32
            ),
            None,
        )

    start = jnp.zeros((level_count, column_count), jnp.float32)
    summed, _ = lax.scan(
        add_one_block, start, (cell_ids.reshape(-1, block_rows), values.reshape(-1, block_rows))
    )
    return summed


def condense(records, excess, occupied):
    radius = jnp.where(occupied, records[..., 0, :], 1.0)
    dry_radius = records[..., 2, :]
    solute = records[..., 3, :]
    radius_cubed = radius * radius * radius
    squared = jnp.maximum(
        radius * radius
        + GROW
        * (
            excess
            - CURVATURE / radius
            + solute * dry_radius * dry_radius * dry_radius / radius_cubed
        ),
        FLOOR_SQ,
    )
    grown_radius = jnp.sqrt(squared)
    condensed = jnp.where(
        occupied,
        records[..., 1, :] * (grown_radius * grown_radius * grown_radius - radius_cubed),
        0.0,
    )
    updated = jnp.concatenate([grown_radius[..., None, :], records[..., 1:, :]], axis=-2)
    updated = jnp.where(occupied[..., None, :], updated, 0.0)
    return (updated, condensed)


def emit_packets(records, cell_ids, leavers, live_count, width_x, width_y):
    record_width, drop_count = records.shape
    slot_count = leavers.shape[1]
    slot_ids = lax.broadcasted_iota(jnp.int32, (4, slot_count), 1)
    face_ids = lax.broadcasted_iota(jnp.int32, (4, slot_count), 0)
    in_use = slot_ids < live_count[:, None]
    inner = min(128, drop_count)
    outer = drop_count // inner
    table = jnp.concatenate([records, cell_ids.astype(jnp.float32)[None, :]], axis=0).reshape(
        record_width + 1, outer, inner
    )
    flat_leavers = leavers.reshape(-1)
    flat_use = in_use.reshape(-1).astype(jnp.bfloat16)
    block_rows = math.gcd(4 * slot_count, 1024)

    def pick_block(inputs):
        ids_block, use_block = inputs
        upper = one_hot_of(ids_block // inner, outer, jnp.float32)
        lower = one_hot_of(ids_block % inner, inner, jnp.float32)
        rows = jnp.einsum(
            "nh,rhl->nrl", upper, table, precision=EXACT, preferred_element_type=jnp.float32
        )
        picked_block = jnp.sum(rows * lower[:, None, :], axis=2)
        upper_used = upper.astype(jnp.bfloat16) * use_block[:, None]
        counts = jnp.einsum(
            "nh,nl->hl", upper_used, lower.astype(jnp.bfloat16), preferred_element_type=jnp.float32
        )
        return (picked_block, counts)

    picked_blocks, count_blocks = lax.map(
        pick_block, (flat_leavers.reshape(-1, block_rows), flat_use.reshape(-1, block_rows))
    )
    picked_all = picked_blocks.reshape(4, slot_count, record_width + 1)
    departed = jnp.sum(count_blocks, axis=0).reshape(-1)
    picked = jnp.moveaxis(picked_all[:, :, :record_width], 2, 1)
    source = (picked_all[:, :, record_width] + 0.5).astype(jnp.int32)
    height = source // (width_x * width_y)
    cell_x = source // width_y % width_x
    cell_y = source % width_y
    new_x = jnp.where(face_ids == 0, 0, jnp.where(face_ids == 1, width_x - 1, cell_x))
    new_y = jnp.where(face_ids == 2, 0, jnp.where(face_ids == 3, width_y - 1, cell_y))
    target = height * (width_x * width_y) + new_x * width_y + new_y
    packet = jnp.concatenate([picked, target.astype(records.dtype)[:, None, :]], axis=1)
    packet = jnp.where(in_use[:, None, :], packet, 0.0)
    return (packet, departed == 0.0)


def settle(records, cell_ids, staying, packet_in, sat_tile, vel_tile, pres_tile):
    level_count, column_count = sat_tile.shape
    record_width = records.shape[0]
    incoming = packet_in[:, :record_width]
    target = (packet_in[:, record_width] + 0.5).astype(jnp.int32)
    occupied = incoming[:, 1] > 0
    all_ids = jnp.concatenate([cell_ids, target.reshape(-1)])
    excess = read_cells(sat_tile, all_ids)
    drop_count = cell_ids.shape[0]
    resident, res_mass = condense(records, excess[:drop_count], staying)
    arrived, arr_mass = condense(incoming, excess[drop_count:].reshape(target.shape), occupied)
    heating = add_cells(
        jnp.concatenate([res_mass, arr_mass.reshape(-1)]), all_ids, level_count, column_count
    )
    forcing = jnp.stack([vel_tile + BUOYANCY * heating, pres_tile])
    return (resident, arrived, forcing)


def split_pieces(value):
    high = value.astype(jnp.bfloat16)
    rest = value - high.astype(jnp.float32)
    middle = rest.astype(jnp.bfloat16)
    low = (rest - middle.astype(jnp.float32)).astype(jnp.bfloat16)
    return (high, middle, low)


def condense_chunk(records, cells, occupied, sat_pieces):
    level_count = sat_pieces[0].shape[0]
    column_count = sat_pieces[0].shape[1]
    width = cells.shape[1]
    shift = column_count.bit_length() - 1
    levels = lax.shift_right_logical(cells, shift)
    columns = jnp.bitwise_and(cells, column_count - 1)
    col_hot = jnp.where(
        lax.broadcasted_iota(jnp.int32, (column_count, width), 0) == columns, 1.0, 0.0
    ).astype(jnp.bfloat16)
    level_mask = lax.broadcasted_iota(jnp.int32, (level_count, width), 0) == levels
    rows = None
    for piece in sat_pieces:
        part = jnp.dot(piece, col_hot, preferred_element_type=jnp.float32)
        rows = part if rows is None else rows + part
    excess = jnp.sum(jnp.where(level_mask, rows, 0.0), axis=0, keepdims=True)
    radius = jnp.where(occupied, records[0:1], 1.0)
    dry_radius = records[2:3]
    solute = records[3:4]
    radius_cubed = radius * radius * radius
    squared = jnp.maximum(
        radius * radius
        + GROW
        * (
            excess
            - CURVATURE / radius
            + solute * dry_radius * dry_radius * dry_radius / radius_cubed
        ),
        FLOOR_SQ,
    )
    grown = jnp.sqrt(squared)
    condensed = jnp.where(occupied, records[1:2] * (grown * grown * grown - radius_cubed), 0.0)
    heat = None
    for piece in split_pieces(condensed):
        spread = jnp.where(level_mask, piece.astype(jnp.float32), 0.0).astype(jnp.bfloat16)
        part = lax.dot_general(
            spread, col_hot, (((1,), (1,)), ((), ())), preferred_element_type=jnp.float32
        )
        heat = part if heat is None else heat + part
    updated = jnp.concatenate([grown, records[1:]], axis=0)
    updated = jnp.where(occupied, updated, 0.0)
    return (updated, heat)


def resident_kernel(rec_ref, cell_ref, stay_ref, sat_ref, out_ref, heat_ref):
    step = pl.program_id(0)
    sat_pieces = split_pieces(sat_ref[...])
    updated, heat = condense_chunk(rec_ref[...], cell_ref[...], stay_ref[...] > 0.0, sat_pieces)
    out_ref[...] = updated

    @pl.when(step == 0)
    def _():
        heat_ref[...] = heat

    @pl.when(step > 0)
    def _():
        heat_ref[...] += heat


def arrival_kernel(in_ref, sat_ref, res_ref, vel_ref, out_ref, force_ref, heat_acc):
    step = pl.program_id(0)
    record_width = out_ref.shape[0]
    packet = in_ref[...]
    records = packet[:record_width]
    cells = (packet[record_width : record_width + 1] + 0.5).astype(jnp.int32)
    occupied = records[1:2] > 0.0
    updated, heat = condense_chunk(records, cells, occupied, split_pieces(sat_ref[...]))
    out_ref[...] = updated

    @pl.when(step == 0)
    def _():
        heat_acc[...] = res_ref[...] + heat

    @pl.when(step > 0)
    def _():
        heat_acc[...] += heat

    @pl.when(step == pl.num_programs(0) - 1)
    def _():
        force_ref[...] = vel_ref[...] + BUOYANCY * heat_acc[...]


def settle_residents(records, cell_ids, staying, sat_tile):
    record_width, drop_count = records.shape
    level_count, column_count = sat_tile.shape
    chunk = min(1024, drop_count)
    whole = lambda j: (0, 0)
    by_chunk = lambda j: (0, j)
    return pl.pallas_call(
        resident_kernel,
        grid=(drop_count // chunk,),
        out_shape=(
            jax.ShapeDtypeStruct((record_width, drop_count), jnp.float32),
            jax.ShapeDtypeStruct((level_count, column_count), jnp.float32),
        ),
        in_specs=[
            pl.BlockSpec((record_width, chunk), by_chunk),
            pl.BlockSpec((1, chunk), by_chunk),
            pl.BlockSpec((1, chunk), by_chunk),
            pl.BlockSpec((level_count, column_count), whole),
        ],
        out_specs=(
            pl.BlockSpec((record_width, chunk), by_chunk),
            pl.BlockSpec((level_count, column_count), whole),
        ),
        cost_estimate=pl.CostEstimate(
            flops=12 * level_count * column_count * drop_count,
            bytes_accessed=4 * (2 * record_width + 2) * drop_count,
            transcendentals=drop_count,
        ),
    )(records, cell_ids.reshape(1, drop_count), staying.astype(jnp.float32).reshape(1, drop_count), sat_tile)


def settle_arrivals(packet_in, sat_tile, heat_res, vel_tile):
    faces, packet_width, slot_count = packet_in.shape
    record_width = packet_width - 1
    level_count, column_count = sat_tile.shape
    whole = lambda f: (0, 0)
    return pl.pallas_call(
        arrival_kernel,
        grid=(faces,),
        out_shape=(
            jax.ShapeDtypeStruct((faces, record_width, slot_count), jnp.float32),
            jax.ShapeDtypeStruct((level_count, column_count), jnp.float32),
        ),
        in_specs=[
            pl.BlockSpec((None, packet_width, slot_count), lambda f: (f, 0, 0)),
            pl.BlockSpec((level_count, column_count), whole),
            pl.BlockSpec((level_count, column_count), whole),
            pl.BlockSpec((level_count, column_count), whole),
        ],
        out_specs=(
            pl.BlockSpec((None, record_width, slot_count), lambda f: (f, 0, 0)),
            pl.BlockSpec((level_count, column_count), whole),
        ),
        scratch_shapes=[pltpu.VMEM((level_count, column_count), jnp.float32)],
        cost_estimate=pl.CostEstimate(
            flops=12 * level_count * column_count * faces * slot_count,
            bytes_accessed=4 * (2 * packet_width) * faces * slot_count,
            transcendentals=faces * slot_count,
        ),
    )(packet_in, sat_tile, heat_res, vel_tile)


def along_x(packet_face, offset):
    return shifted(packet_face, "gx", offset)


def along_y(packet_face, offset):
    return shifted(packet_face, "gy", offset)


def solve_kernel(
    off_ref, maps_ref, fv_ref, fp_ref, sv_ref, sp_ref, last_ref, first_ref, ex_ref, xv_ref, xp_ref
):
    levels = fv_ref.shape[0]
    off = off_ref[0]
    upper = jnp.where(off > 0, 1.0, 0.0).astype(jnp.float32)
    lane = lax.broadcasted_iota(jnp.int32, (1, 128), 1)
    e0 = jnp.where(lane == 0, 1.0, 0.0).astype(jnp.float32)
    e1 = jnp.where(lane == 1, 1.0, 0.0).astype(jnp.float32)
    zero = jnp.zeros(fv_ref.shape[1:], jnp.float32)[None, :]

    def forward(k, carry):
        uv, up, xv, xp = carry
        level = off + k
        b0 = maps_ref[0, level]
        b1 = maps_ref[1, level]
        b2 = maps_ref[2, level]
        b3 = maps_ref[3, level]
        f0 = maps_ref[4, level]
        f1 = maps_ref[5, level]
        f2 = maps_ref[6, level]
        f3 = maps_ref[7, level]
        gv = fv_ref[pl.ds(k, 1), :]
        gp = fp_ref[pl.ds(k, 1), :]
        nuv = (b0 * gv + b1 * gp) + (f0 * uv + f1 * up)
        nup = (b2 * gv + b3 * gp) + (f2 * uv + f3 * up)
        nxv = f0 * xv + f1 * xp
        nxp = f2 * xv + f3 * xp
        sv_ref[pl.ds(k, 1), :] = nuv
        sp_ref[pl.ds(k, 1), :] = nup
        xv_ref[pl.ds(k, 1), :] = nxv
        xp_ref[pl.ds(k, 1), :] = nxp
        return (nuv, nup, nxv, nxp)

    uv, up, xv, xp = lax.fori_loop(
        0, levels, forward, (zero, zero, upper * e0, upper * e1)
    )
    last_ref[0:1, :] = uv
    last_ref[1:2, :] = up
    last_ref[2:4, :] = jnp.zeros((2, uv.shape[1]), jnp.float32)
    last_ref[2:3, 0:128] = xv
    last_ref[3:4, 0:128] = xp

    def backward(step, carry):
        sv, sp, yv, yp = carry
        k = levels - 1 - step
        level = off + k
        c0 = maps_ref[8, level]
        c1 = maps_ref[9, level]
        c2 = maps_ref[10, level]
        c3 = maps_ref[11, level]
        nsv = sv_ref[pl.ds(k, 1), :] + (c0 * sv + c1 * sp)
        nsp = sp_ref[pl.ds(k, 1), :] + (c2 * sv + c3 * sp)
        nyv = xv_ref[pl.ds(k, 1), :] + (c0 * yv + c1 * yp)
        nyp = xp_ref[pl.ds(k, 1), :] + (c2 * yv + c3 * yp)
        sv_ref[pl.ds(k, 1), :] = nsv
        sp_ref[pl.ds(k, 1), :] = nsp
        ex_ref[0, pl.ds(k, 1), :] = nyv
        ex_ref[1, pl.ds(k, 1), :] = nyp
        return (nsv, nsp, nyv, nyp)

    lower = 1.0 - upper
    sv, sp, yv, yp = lax.fori_loop(
        0, levels, backward, (zero, zero, lower * e0, lower * e1)
    )
    first_ref[0:1, :] = sv
    first_ref[1:2, :] = sp
    first_ref[2:4, :] = jnp.zeros((2, sv.shape[1]), jnp.float32)
    first_ref[2:3, 0:128] = yv
    first_ref[3:4, 0:128] = yp


def solve_local(forcing, block_inverse, forward_map, backward_map):
    _, levels, columns = forcing.shape
    offset = jnp.full((1,), lax.axis_index("gz") * levels, jnp.int32)
    maps = jnp.concatenate([block_inverse, forward_map, backward_map], axis=0)
    smem = pl.BlockSpec(memory_space=pltpu.SMEM)
    vmem = pl.BlockSpec(memory_space=pltpu.VMEM)
    return pl.pallas_call(
        solve_kernel,
        out_shape=(
            jax.ShapeDtypeStruct((levels, columns), jnp.float32),
            jax.ShapeDtypeStruct((levels, columns), jnp.float32),
            jax.ShapeDtypeStruct((4, columns), jnp.float32),
            jax.ShapeDtypeStruct((4, columns), jnp.float32),
            jax.ShapeDtypeStruct((2, levels, 128), jnp.float32),
        ),
        in_specs=[smem, smem, vmem, vmem],
        out_specs=(vmem, vmem, vmem, vmem, vmem),
        scratch_shapes=[
            pltpu.VMEM((levels, 128), jnp.float32),
            pltpu.VMEM((levels, 128), jnp.float32),
        ],
        cost_estimate=pl.CostEstimate(
            flops=40 * levels * columns, bytes_accessed=24 * levels * columns, transcendentals=0
        ),
    )(offset, maps, forcing[0], forcing[1])


def solve_split(forcing, block_inverse, forward_map, backward_map):
    assert lax.axis_size("gz") == 2
    sv, sp, last, first, extra = solve_local(forcing, block_inverse, forward_map, backward_map)
    lower = lax.axis_index("gz") == 0
    message = jnp.where(lower, last, first)
    received = lax.ppermute(message, "gz", [(0, 1), (1, 0)])
    r0 = received[0] + received[2, 0] * last[0] + received[2, 1] * last[1]
    r1 = received[1] + received[3, 0] * last[0] + received[3, 1] * last[1]
    new_v = sv + extra[0, :, 0:1] * r0[None, :] + extra[0, :, 1:2] * r1[None, :]
    new_p = sp + extra[1, :, 0:1] * r0[None, :] + extra[1, :, 1:2] * r1[None, :]
    return new_v, new_p


def body(
    droplets,
    cell_index,
    crossing,
    crossing_count,
    saturation,
    velocity,
    pressure,
    block_inverse,
    forward_map,
    backward_map,
):
    records = droplets[0, 0, 0]
    cell_ids = cell_index[0, 0, 0]
    sat_tile = saturation[:, 0, 0, :]
    packet, staying = emit_packets(
        records, cell_ids, crossing[0, 0, 0], crossing_count[0, 0, 0], CX, CY
    )
    from_west = along_x(packet[0], 1)
    from_east = along_x(packet[1], -1)
    from_south = along_y(packet[2], 1)
    from_north = along_y(packet[3], -1)
    resident, heat_res = settle_residents(records, cell_ids, staying, sat_tile)
    packet_in = jnp.stack([from_west, from_east, from_south, from_north])
    arrived, force_v = settle_arrivals(packet_in, sat_tile, heat_res, velocity[:, 0, 0, :])
    forcing = jnp.stack([force_v, pressure[:, 0, 0, :]])
    solved_v, solved_p = solve_split(forcing, block_inverse, forward_map, backward_map)
    new_velocity = solved_v[:, None, None, :]
    new_pressure = solved_p[:, None, None, :]
    return (resident[None, None, None], arrived[None, None, None], new_velocity, new_pressure)


def solution(mesh):
    return jax.shard_map(
        body,
        mesh=mesh,
        in_specs=(
            P("gz", "gx", "gy", None, None),
            P("gz", "gx", "gy", None),
            P("gz", "gx", "gy", None, None),
            P("gz", "gx", "gy", None),
            P("gz", "gx", "gy", None),
            P("gz", "gx", "gy", None),
            P("gz", "gx", "gy", None),
            P(),
            P(),
            P(),
        ),
        out_specs=(
            P("gz", "gx", "gy", None, None),
            P("gz", "gx", "gy", None, None, None),
            P("gz", "gx", "gy", None),
            P("gz", "gx", "gy", None),
        ),
        check_vma=False,
    )
```

```python
import math

import jax
import jax.numpy as jnp
from jax import lax
from jax.sharding import PartitionSpec as P
from jax.experimental import pallas as pl
from jax.experimental.pallas import tpu as pltpu

CX = 8
CY = 32


GROW = 0.4
CURVATURE = 0.05
FLOOR_SQ = 0.09
BUOYANCY = 0.5
EXACT = lax.Precision.HIGHEST


def shifted(value, axis, steps):
    count = lax.axis_size(axis)
    pairs = [(source, (source + steps) % count) for source in range(count)]
    return lax.ppermute(value, axis, pairs)


def one_hot_of(index, width, dtype):
    return (index[:, None] == lax.broadcasted_iota(jnp.int32, (1, width), 1)).astype(dtype)


def emit_packets(records, cell_ids, leavers, live_count, width_x, width_y):
    record_width, drop_count = records.shape
    slot_count = leavers.shape[1]
    slot_ids = lax.broadcasted_iota(jnp.int32, (4, slot_count), 1)
    face_ids = lax.broadcasted_iota(jnp.int32, (4, slot_count), 0)
    in_use = slot_ids < live_count[:, None]
    inner = min(128, drop_count)
    outer = drop_count // inner
    table = jnp.concatenate([records, cell_ids.astype(jnp.float32)[None, :]], axis=0).reshape(
        record_width + 1, outer, inner
    )
    flat_leavers = leavers.reshape(-1)
    flat_use = in_use.reshape(-1).astype(jnp.bfloat16)
    block_rows = math.gcd(4 * slot_count, 1024)

    def pick_block(inputs):
        ids_block, use_block = inputs
        upper = one_hot_of(ids_block // inner, outer, jnp.float32)
        lower = one_hot_of(ids_block % inner, inner, jnp.float32)
        rows = jnp.einsum(
            "nh,rhl->nrl", upper, table, precision=EXACT, preferred_element_type=jnp.float32
        )
        picked_block = jnp.sum(rows * lower[:, None, :], axis=2)
        upper_used = upper.astype(jnp.bfloat16) * use_block[:, None]
        counts = jnp.einsum(
            "nh,nl->hl", upper_used, lower.astype(jnp.bfloat16), preferred_element_type=jnp.float32
        )
        return (picked_block, counts)

    picked_blocks, count_blocks = lax.map(
        pick_block, (flat_leavers.reshape(-1, block_rows), flat_use.reshape(-1, block_rows))
    )
    picked_all = picked_blocks.reshape(4, slot_count, record_width + 1)
    departed = jnp.sum(count_blocks, axis=0).reshape(-1)
    picked = jnp.moveaxis(picked_all[:, :, :record_width], 2, 1)
    source = (picked_all[:, :, record_width] + 0.5).astype(jnp.int32)
    height = source // (width_x * width_y)
    cell_x = source // width_y % width_x
    cell_y = source % width_y
    new_x = jnp.where(face_ids == 0, 0, jnp.where(face_ids == 1, width_x - 1, cell_x))
    new_y = jnp.where(face_ids == 2, 0, jnp.where(face_ids == 3, width_y - 1, cell_y))
    target = height * (width_x * width_y) + new_x * width_y + new_y
    packet = jnp.concatenate([picked, target.astype(records.dtype)[:, None, :]], axis=1)
    packet = jnp.where(in_use[:, None, :], packet, 0.0)
    return (packet, departed == 0.0)


def split_pieces(value):
    high = value.astype(jnp.bfloat16)
    rest = value - high.astype(jnp.float32)
    middle = rest.astype(jnp.bfloat16)
    low = (rest - middle.astype(jnp.float32)).astype(jnp.bfloat16)
    return (high, middle, low)


def stacked_pieces(value):
    return jnp.concatenate(split_pieces(value), axis=0)


def condense_chunk(records, cells, occupied, sat_stack):
    rows = sat_stack.shape[0] // 3
    lanes = sat_stack.shape[1]
    width = cells.shape[1]
    shift = lanes.bit_length() - 1
    row_of = lax.shift_right_logical(cells, shift)
    lane_of = jnp.bitwise_and(cells, lanes - 1)
    lane_mask = lax.broadcasted_iota(jnp.int32, (lanes, width), 0) == lane_of
    lane_hot = jnp.where(lane_mask, 1.0, 0.0).astype(jnp.bfloat16)
    row_mask = lax.broadcasted_iota(jnp.int32, (rows, width), 0) == row_of
    row_hot = jnp.where(row_mask, 1.0, 0.0).astype(jnp.bfloat16)
    picked = jnp.dot(sat_stack, lane_hot, preferred_element_type=jnp.float32)
    picked = picked[:rows] + picked[rows : 2 * rows] + picked[2 * rows :]
    excess = jnp.sum(jnp.where(row_mask, picked, 0.0), axis=0, keepdims=True)
    radius = jnp.where(occupied, records[0:1], 1.0)
    dry_radius = records[2:3]
    solute = records[3:4]
    radius_cubed = radius * radius * radius
    squared = jnp.maximum(
        radius * radius
        + GROW
        * (
            excess
            - CURVATURE / radius
            + solute * dry_radius * dry_radius * dry_radius / radius_cubed
        ),
        FLOOR_SQ,
    )
    grown = jnp.sqrt(squared)
    condensed = jnp.where(occupied, records[1:2] * (grown * grown * grown - radius_cubed), 0.0)
    spread = jnp.concatenate([row_hot * piece for piece in split_pieces(condensed)], axis=0)
    heat = lax.dot_general(
        spread, lane_hot, (((1,), (1,)), ((), ())), preferred_element_type=jnp.float32
    )
    heat = heat[:rows] + heat[rows : 2 * rows] + heat[2 * rows :]
    updated = jnp.concatenate([grown, records[1:]], axis=0)
    updated = jnp.where(occupied, updated, 0.0)
    return (updated, heat)


def resident_kernel(rec_ref, cell_ref, stay_ref, sat_ref, out_ref, heat_ref):
    step = pl.program_id(0)
    updated, heat = condense_chunk(
        rec_ref[...], cell_ref[...], stay_ref[...] > 0.0, stacked_pieces(sat_ref[...])
    )
    out_ref[...] = updated

    @pl.when(step == 0)
    def _():
        heat_ref[...] = heat

    @pl.when(step > 0)
    def _():
        heat_ref[...] += heat


def arrival_kernel(w_ref, e_ref, s_ref, n_ref, sat_ref, res_ref, vel_ref, out_ref, force_ref):
    record_width = out_ref.shape[1]
    sat_stack = stacked_pieces(sat_ref[...])
    total = res_ref[...]
    for face, in_ref in enumerate((w_ref, e_ref, s_ref, n_ref)):
        packet = in_ref[...]
        records = packet[:record_width]
        cells = (packet[record_width : record_width + 1] + 0.5).astype(jnp.int32)
        occupied = records[1:2] > 0.0
        updated, heat = condense_chunk(records, cells, occupied, sat_stack)
        out_ref[face] = updated
        total = total + heat
    force_ref[...] = vel_ref[...] + BUOYANCY * total


def settle_residents(records, cell_row, staying_row, sat_view):
    record_width, drop_count = records.shape
    rows, lanes = sat_view.shape
    chunk = min(4096, drop_count)
    whole = lambda j: (0, 0)
    by_chunk = lambda j: (0, j)
    return pl.pallas_call(
        resident_kernel,
        grid=(drop_count // chunk,),
        out_shape=(
            jax.ShapeDtypeStruct((record_width, drop_count), jnp.float32),
            jax.ShapeDtypeStruct((rows, lanes), jnp.float32),
        ),
        in_specs=[
            pl.BlockSpec((record_width, chunk), by_chunk),
            pl.BlockSpec((1, chunk), by_chunk),
            pl.BlockSpec((1, chunk), by_chunk),
            pl.BlockSpec((rows, lanes), whole),
        ],
        out_specs=(
            pl.BlockSpec((record_width, chunk), by_chunk),
            pl.BlockSpec((rows, lanes), whole),
        ),
        cost_estimate=pl.CostEstimate(
            flops=12 * rows * lanes * drop_count,
            bytes_accessed=4 * (2 * record_width + 2) * drop_count,
            transcendentals=drop_count,
        ),
    )(records, cell_row, staying_row, sat_view)


def settle_arrivals(faces_in, sat_view, heat_res, vel_view):
    packet_width, slot_count = faces_in[0].shape
    record_width = packet_width - 1
    vmem = pl.BlockSpec(memory_space=pltpu.VMEM)
    return pl.pallas_call(
        arrival_kernel,
        out_shape=(
            jax.ShapeDtypeStruct((len(faces_in), record_width, slot_count), jnp.float32),
            jax.ShapeDtypeStruct(sat_view.shape, jnp.float32),
        ),
        in_specs=[vmem] * (len(faces_in) + 3),
        out_specs=(vmem, vmem),
        cost_estimate=pl.CostEstimate(
            flops=12 * sat_view.size * len(faces_in) * slot_count,
            bytes_accessed=4 * (2 * packet_width) * len(faces_in) * slot_count,
            transcendentals=len(faces_in) * slot_count,
        ),
    )(*faces_in, sat_view, heat_res, vel_view)


def solve_kernel(
    off_ref, bi_ref, fm_ref, bm_ref, fv_ref, fp_ref, sv_ref, sp_ref, msg_ref, coef_ref, xs_ref
):
    rows = fv_ref.shape[0]
    levels = coef_ref.shape[1]
    per = rows // levels
    off = off_ref[0]
    upper = jnp.where(off > 0, 1.0, 0.0).astype(jnp.float32)
    lower = 1.0 - upper
    zero = jnp.zeros((per, fv_ref.shape[1]), jnp.float32)

    def forward(k, carry):
        uv, up, x0, x1, x2, x3 = carry
        level = off + k
        b0 = bi_ref[0, level]
        b1 = bi_ref[1, level]
        b2 = bi_ref[2, level]
        b3 = bi_ref[3, level]
        f0 = fm_ref[0, level]
        f1 = fm_ref[1, level]
        f2 = fm_ref[2, level]
        f3 = fm_ref[3, level]
        at = pl.ds(pl.multiple_of(k * per, per), per)
        gv = fv_ref[at, :]
        gp = fp_ref[at, :]
        nuv = (b0 * gv + b1 * gp) + (f0 * uv + f1 * up)
        nup = (b2 * gv + b3 * gp) + (f2 * uv + f3 * up)
        sv_ref[at, :] = nuv
        sp_ref[at, :] = nup
        y0 = f0 * x0 + f1 * x2
        y1 = f0 * x1 + f1 * x3
        y2 = f2 * x0 + f3 * x2
        y3 = f2 * x1 + f3 * x3
        xs_ref[0, k] = y0
        xs_ref[1, k] = y1
        xs_ref[2, k] = y2
        xs_ref[3, k] = y3
        return (nuv, nup, y0, y1, y2, y3)

    uv, up, _, _, _, _ = lax.fori_loop(
        0, levels, forward, (zero, zero, upper, 0.0 * upper, 0.0 * upper, upper), unroll=4
    )

    def backward(step, carry):
        sv, sp, c0, c1, c2, c3 = carry
        k = levels - 1 - step
        level = off + k
        m0 = bm_ref[0, level]
        m1 = bm_ref[1, level]
        m2 = bm_ref[2, level]
        m3 = bm_ref[3, level]
        at = pl.ds(pl.multiple_of(k * per, per), per)
        nsv = sv_ref[at, :] + (m0 * sv + m1 * sp)
        nsp = sp_ref[at, :] + (m2 * sv + m3 * sp)
        sv_ref[at, :] = nsv
        sp_ref[at, :] = nsp
        d0 = xs_ref[0, k] + (m0 * c0 + m1 * c2)
        d1 = xs_ref[1, k] + (m0 * c1 + m1 * c3)
        d2 = xs_ref[2, k] + (m2 * c0 + m3 * c2)
        d3 = xs_ref[3, k] + (m2 * c1 + m3 * c3)
        coef_ref[0, k] = d0
        coef_ref[1, k] = d1
        coef_ref[2, k] = d2
        coef_ref[3, k] = d3
        return (nsv, nsp, d0, d1, d2, d3)

    sv, sp, d0, d1, d2, d3 = lax.fori_loop(
        0, levels, backward, (zero, zero, lower, 0.0 * lower, 0.0 * lower, lower), unroll=4
    )
    lanes = fv_ref.shape[1]
    msg_ref[0:per, :] = lower * uv + upper * sv
    msg_ref[per : 2 * per, :] = lower * up + upper * sp
    for index, value in enumerate((d0, d1, d2, d3)):
        msg_ref[2 * per + index : 2 * per + index + 1, :] = jnp.full((1, lanes), upper * value, jnp.float32)


def correct_kernel(coef_ref, own_ref, recv_ref, sv_ref, sp_ref, nv_ref, np_ref):
    rows = sv_ref.shape[0]
    levels = coef_ref.shape[1]
    per = rows // levels
    own0 = own_ref[0:per, :]
    own1 = own_ref[per : 2 * per, :]
    extra = [recv_ref[2 * per + i : 2 * per + i + 1, :] for i in range(4)]
    v0 = recv_ref[0:per, :] + extra[0] * own0 + extra[1] * own1
    v1 = recv_ref[per : 2 * per, :] + extra[2] * own0 + extra[3] * own1

    def fix(k, carry):
        at = pl.ds(pl.multiple_of(k * per, per), per)
        nv_ref[at, :] = sv_ref[at, :] + (coef_ref[0, k] * v0 + coef_ref[1, k] * v1)
        np_ref[at, :] = sp_ref[at, :] + (coef_ref[2, k] * v0 + coef_ref[3, k] * v1)
        return carry

    lax.fori_loop(0, levels, fix, 0, unroll=8)


def solve_split(force_view, pres_view, levels, block_inverse, forward_map, backward_map):
    assert lax.axis_size("gz") == 2
    rows, lanes = force_view.shape
    per = rows // levels
    offset = jnp.full((1,), lax.axis_index("gz") * levels, jnp.int32)
    smem = pl.BlockSpec(memory_space=pltpu.SMEM)
    vmem = pl.BlockSpec(memory_space=pltpu.VMEM)
    sv, sp, message, coef = pl.pallas_call(
        solve_kernel,
        out_shape=(
            jax.ShapeDtypeStruct((rows, lanes), jnp.float32),
            jax.ShapeDtypeStruct((rows, lanes), jnp.float32),
            jax.ShapeDtypeStruct((2 * per + 4, lanes), jnp.float32),
            jax.ShapeDtypeStruct((4, levels), jnp.float32),
        ),
        in_specs=[smem, smem, smem, smem, vmem, vmem],
        out_specs=(vmem, vmem, vmem, smem),
        scratch_shapes=[pltpu.SMEM((4, levels), jnp.float32)],
        cost_estimate=pl.CostEstimate(
            flops=40 * rows * lanes, bytes_accessed=24 * rows * lanes, transcendentals=0
        ),
    )(offset, block_inverse, forward_map, backward_map, force_view, pres_view)
    received = lax.ppermute(message, "gz", [(0, 1), (1, 0)])
    return pl.pallas_call(
        correct_kernel,
        out_shape=(
            jax.ShapeDtypeStruct((rows, lanes), jnp.float32),
            jax.ShapeDtypeStruct((rows, lanes), jnp.float32),
        ),
        in_specs=[smem, vmem, vmem, vmem, vmem],
        out_specs=(vmem, vmem),
        cost_estimate=pl.CostEstimate(
            flops=8 * rows * lanes, bytes_accessed=16 * rows * lanes, transcendentals=0
        ),
    )(coef, message, received, sv, sp)


def along_x(packet_face, offset):
    return shifted(packet_face, "gx", offset)


def along_y(packet_face, offset):
    return shifted(packet_face, "gy", offset)


def body(
    droplets,
    cell_index,
    crossing,
    crossing_count,
    saturation,
    velocity,
    pressure,
    block_inverse,
    forward_map,
    backward_map,
):
    records = droplets[0, 0, 0]
    cell_ids = cell_index[0, 0, 0]
    levels = saturation.shape[0]
    view = (saturation.size // 128, 128)
    sat_view = saturation.reshape(view)
    packet, staying = emit_packets(
        records, cell_ids, crossing[0, 0, 0], crossing_count[0, 0, 0], CX, CY
    )
    from_west = along_x(packet[0], 1)
    from_east = along_x(packet[1], -1)
    from_south = along_y(packet[2], 1)
    from_north = along_y(packet[3], -1)
    resident, heat_res = settle_residents(
        records,
        cell_index.reshape(1, -1),
        staying.astype(jnp.float32).reshape(1, -1),
        sat_view,
    )
    arrived, force_view = settle_arrivals(
        (from_west, from_east, from_south, from_north), sat_view, heat_res, velocity.reshape(view)
    )
    solved_v, solved_p = solve_split(
        force_view, pressure.reshape(view), levels, block_inverse, forward_map, backward_map
    )
    new_velocity = solved_v.reshape(velocity.shape)
    new_pressure = solved_p.reshape(pressure.shape)
    return (resident[None, None, None], arrived[None, None, None], new_velocity, new_pressure)


def solution(mesh):
    return jax.shard_map(
        body,
        mesh=mesh,
        in_specs=(
            P("gz", "gx", "gy", None, None),
            P("gz", "gx", "gy", None),
            P("gz", "gx", "gy", None, None),
            P("gz", "gx", "gy", None),
            P("gz", "gx", "gy", None),
            P("gz", "gx", "gy", None),
            P("gz", "gx", "gy", None),
            P(),
            P(),
            P(),
        ),
        out_specs=(
            P("gz", "gx", "gy", None, None),
            P("gz", "gx", "gy", None, None, None),
            P("gz", "gx", "gy", None),
            P("gz", "gx", "gy", None),
        ),
        check_vma=False,
    )
```

```python
import math

import jax
import jax.numpy as jnp
from jax import lax
from jax.sharding import PartitionSpec as P
from jax.experimental import pallas as pl
from jax.experimental.pallas import tpu as pltpu

CX = 8
CY = 32


GROW = 0.4
CURVATURE = 0.05
FLOOR_SQ = 0.09
BUOYANCY = 0.5
EXACT = lax.Precision.HIGHEST


def shifted(value, axis, steps):
    count = lax.axis_size(axis)
    pairs = [(source, (source + steps) % count) for source in range(count)]
    return lax.ppermute(value, axis, pairs)


def one_hot_of(index, width, dtype):
    return (index[:, None] == lax.broadcasted_iota(jnp.int32, (1, width), 1)).astype(dtype)


def emit_packets(records, cell_ids, leavers, live_count, width_x, width_y):
    record_width, drop_count = records.shape
    slot_count = leavers.shape[1]
    slot_ids = lax.broadcasted_iota(jnp.int32, (4, slot_count), 1)
    face_ids = lax.broadcasted_iota(jnp.int32, (4, slot_count), 0)
    in_use = slot_ids < live_count[:, None]
    inner = min(128, drop_count)
    outer = drop_count // inner
    table = jnp.concatenate([records, cell_ids.astype(jnp.float32)[None, :]], axis=0).reshape(
        record_width + 1, outer, inner
    )
    flat_leavers = leavers.reshape(-1)
    flat_use = in_use.reshape(-1).astype(jnp.bfloat16)
    block_rows = 4 * slot_count

    def pick_block(inputs):
        ids_block, use_block = inputs
        upper = one_hot_of(ids_block // inner, outer, jnp.float32)
        lower = one_hot_of(ids_block % inner, inner, jnp.float32)
        rows = jnp.einsum(
            "nh,rhl->nrl", upper, table, precision=EXACT, preferred_element_type=jnp.float32
        )
        picked_block = jnp.sum(rows * lower[:, None, :], axis=2)
        upper_used = upper.astype(jnp.bfloat16) * use_block[:, None]
        counts = jnp.einsum(
            "nh,nl->hl", upper_used, lower.astype(jnp.bfloat16), preferred_element_type=jnp.float32
        )
        return (picked_block, counts)

    picked_blocks, count_blocks = lax.map(
        pick_block, (flat_leavers.reshape(-1, block_rows), flat_use.reshape(-1, block_rows))
    )
    picked_all = picked_blocks.reshape(4, slot_count, record_width + 1)
    departed = jnp.sum(count_blocks, axis=0).reshape(-1)
    picked = jnp.moveaxis(picked_all[:, :, :record_width], 2, 1)
    source = (picked_all[:, :, record_width] + 0.5).astype(jnp.int32)
    height = source // (width_x * width_y)
    cell_x = source // width_y % width_x
    cell_y = source % width_y
    new_x = jnp.where(face_ids == 0, 0, jnp.where(face_ids == 1, width_x - 1, cell_x))
    new_y = jnp.where(face_ids == 2, 0, jnp.where(face_ids == 3, width_y - 1, cell_y))
    target = height * (width_x * width_y) + new_x * width_y + new_y
    packet = jnp.concatenate([picked, target.astype(records.dtype)[:, None, :]], axis=1)
    packet = jnp.where(in_use[:, None, :], packet, 0.0)
    return (packet, departed == 0.0)


def split_pieces(value):
    high = value.astype(jnp.bfloat16)
    low = (value - high.astype(jnp.float32)).astype(jnp.bfloat16)
    return (high, low)


def stacked_pieces(value):
    return jnp.concatenate(split_pieces(value), axis=0)


def condense_chunk(records, cells, occupied, sat_stack):
    rows = sat_stack.shape[0] // 2
    lanes = sat_stack.shape[1]
    width = cells.shape[1]
    shift = lanes.bit_length() - 1
    row_of = lax.shift_right_logical(cells, shift)
    lane_of = jnp.bitwise_and(cells, lanes - 1)
    lane_mask = lax.broadcasted_iota(jnp.int32, (lanes, width), 0) == lane_of
    lane_hot = jnp.where(lane_mask, 1.0, 0.0).astype(jnp.bfloat16)
    row_mask = lax.broadcasted_iota(jnp.int32, (rows, width), 0) == row_of
    row_hot = jnp.where(row_mask, 1.0, 0.0).astype(jnp.bfloat16)
    picked = jnp.dot(sat_stack, lane_hot, preferred_element_type=jnp.float32)
    picked = picked[:rows] + picked[rows:]
    excess = jnp.sum(jnp.where(row_mask, picked, 0.0), axis=0, keepdims=True)
    radius = jnp.where(occupied, records[0:1], 1.0)
    dry_radius = records[2:3]
    solute = records[3:4]
    radius_cubed = radius * radius * radius
    squared = jnp.maximum(
        radius * radius
        + GROW
        * (
            excess
            - CURVATURE / radius
            + solute * dry_radius * dry_radius * dry_radius / radius_cubed
        ),
        FLOOR_SQ,
    )
    grown = jnp.sqrt(squared)
    condensed = jnp.where(occupied, records[1:2] * (grown * grown * grown - radius_cubed), 0.0)
    spread = jnp.concatenate([row_hot * piece for piece in split_pieces(condensed)], axis=0)
    heat = lax.dot_general(
        spread, lane_hot, (((1,), (1,)), ((), ())), preferred_element_type=jnp.float32
    )
    heat = heat[:rows] + heat[rows:]
    updated = jnp.concatenate([grown, records[1:]], axis=0)
    updated = jnp.where(occupied, updated, 0.0)
    return (updated, heat)


def resident_kernel(rec_ref, cell_ref, stay_ref, sat_ref, out_ref, heat_ref):
    step = pl.program_id(0)
    updated, heat = condense_chunk(
        rec_ref[...], cell_ref[...], stay_ref[...] > 0.0, stacked_pieces(sat_ref[...])
    )
    out_ref[...] = updated

    @pl.when(step == 0)
    def _():
        heat_ref[...] = heat

    @pl.when(step > 0)
    def _():
        heat_ref[...] += heat


def settle_residents(records, cell_row, staying_row, sat_view):
    record_width, drop_count = records.shape
    rows, lanes = sat_view.shape
    chunk = min(4096, drop_count)
    whole = lambda j: (0, 0)
    by_chunk = lambda j: (0, j)
    return pl.pallas_call(
        resident_kernel,
        grid=(drop_count // chunk,),
        out_shape=(
            jax.ShapeDtypeStruct((record_width, drop_count), jnp.float32),
            jax.ShapeDtypeStruct((rows, lanes), jnp.float32),
        ),
        in_specs=[
            pl.BlockSpec((record_width, chunk), by_chunk),
            pl.BlockSpec((1, chunk), by_chunk),
            pl.BlockSpec((1, chunk), by_chunk),
            pl.BlockSpec((rows, lanes), whole),
        ],
        out_specs=(
            pl.BlockSpec((record_width, chunk), by_chunk),
            pl.BlockSpec((rows, lanes), whole),
        ),
        cost_estimate=pl.CostEstimate(
            flops=12 * rows * lanes * drop_count,
            bytes_accessed=4 * (2 * record_width + 2) * drop_count,
            transcendentals=drop_count,
        ),
    )(records, cell_row, staying_row, sat_view)


def arrivals_into(faces, sat_ref, res_ref, vel_ref, out_ref, force_ref):
    record_width = out_ref.shape[1]
    sat_stack = stacked_pieces(sat_ref[...])
    total = res_ref[...]
    for face, in_ref in enumerate(faces):
        packet = in_ref[...]
        records = packet[:record_width]
        cells = (packet[record_width : record_width + 1] + 0.5).astype(jnp.int32)
        occupied = records[1:2] > 0.0
        updated, heat = condense_chunk(records, cells, occupied, sat_stack)
        out_ref[face] = updated
        total = total + heat
    force_ref[...] = vel_ref[...] + BUOYANCY * total


def solve_into(off_ref, bi_ref, fm_ref, bm_ref, fv_ref, fp_ref, sv_ref, sp_ref, msg_ref, coef_ref, xs_ref):
    rows, lanes = fv_ref.shape
    levels = xs_ref.shape[1]
    per = rows // levels
    off = off_ref[0]
    upper = jnp.where(off > 0, 1.0, 0.0).astype(jnp.float32)
    lower = 1.0 - upper
    zero = jnp.zeros((per, lanes), jnp.float32)

    def forward(k, carry):
        uv, up, x0, x1, x2, x3 = carry
        level = off + k
        b0 = bi_ref[0, level]
        b1 = bi_ref[1, level]
        b2 = bi_ref[2, level]
        b3 = bi_ref[3, level]
        f0 = fm_ref[0, level]
        f1 = fm_ref[1, level]
        f2 = fm_ref[2, level]
        f3 = fm_ref[3, level]
        at = pl.ds(pl.multiple_of(k * per, per), per)
        gv = fv_ref[at, :]
        gp = fp_ref[at, :]
        nuv = (b0 * gv + b1 * gp) + (f0 * uv + f1 * up)
        nup = (b2 * gv + b3 * gp) + (f2 * uv + f3 * up)
        sv_ref[at, :] = nuv
        sp_ref[at, :] = nup
        y0 = f0 * x0 + f1 * x2
        y1 = f0 * x1 + f1 * x3
        y2 = f2 * x0 + f3 * x2
        y3 = f2 * x1 + f3 * x3
        xs_ref[0, k] = y0
        xs_ref[1, k] = y1
        xs_ref[2, k] = y2
        xs_ref[3, k] = y3
        return (nuv, nup, y0, y1, y2, y3)

    uv, up, _, _, _, _ = lax.fori_loop(
        0, levels, forward, (zero, zero, upper, 0.0 * upper, 0.0 * upper, upper), unroll=4
    )

    def backward(step, carry):
        sv, sp, c0, c1, c2, c3 = carry
        k = levels - 1 - step
        level = off + k
        m0 = bm_ref[0, level]
        m1 = bm_ref[1, level]
        m2 = bm_ref[2, level]
        m3 = bm_ref[3, level]
        at = pl.ds(pl.multiple_of(k * per, per), per)
        nsv = sv_ref[at, :] + (m0 * sv + m1 * sp)
        nsp = sp_ref[at, :] + (m2 * sv + m3 * sp)
        sv_ref[at, :] = nsv
        sp_ref[at, :] = nsp
        d0 = xs_ref[0, k] + (m0 * c0 + m1 * c2)
        d1 = xs_ref[1, k] + (m0 * c1 + m1 * c3)
        d2 = xs_ref[2, k] + (m2 * c0 + m3 * c2)
        d3 = xs_ref[3, k] + (m2 * c1 + m3 * c3)
        coef_ref[0, at, :] = jnp.full((per, lanes), d0, jnp.float32)
        coef_ref[1, at, :] = jnp.full((per, lanes), d1, jnp.float32)
        coef_ref[2, at, :] = jnp.full((per, lanes), d2, jnp.float32)
        coef_ref[3, at, :] = jnp.full((per, lanes), d3, jnp.float32)
        return (nsv, nsp, d0, d1, d2, d3)

    sv, sp, d0, d1, d2, d3 = lax.fori_loop(
        0, levels, backward, (zero, zero, lower, 0.0 * lower, 0.0 * lower, lower), unroll=4
    )
    msg_ref[0:per, :] = lower * uv + upper * sv
    msg_ref[per : 2 * per, :] = lower * up + upper * sp
    for index, value in enumerate((d0, d1, d2, d3)):
        msg_ref[2 * per + index : 2 * per + index + 1, :] = jnp.full((1, lanes), upper * value, jnp.float32)


def arrive_solve_kernel(
    off_ref, bi_ref, fm_ref, bm_ref, w_ref, e_ref, s_ref, n_ref, sat_ref, res_ref, vel_ref, pres_ref,
    out_ref, sv_ref, sp_ref, msg_ref, coef_ref, force_ref, xs_ref,
):
    arrivals_into((w_ref, e_ref, s_ref, n_ref), sat_ref, res_ref, vel_ref, out_ref, force_ref)
    solve_into(off_ref, bi_ref, fm_ref, bm_ref, force_ref, pres_ref, sv_ref, sp_ref, msg_ref, coef_ref, xs_ref)


def correct_kernel(coef_ref, own_ref, recv_ref, sv_ref, sp_ref, nv_ref, np_ref):
    rows, lanes = sv_ref.shape
    per = (own_ref.shape[0] - 4) // 2
    own0 = own_ref[0:per, :]
    own1 = own_ref[per : 2 * per, :]
    extra = [recv_ref[2 * per + i : 2 * per + i + 1, :] for i in range(4)]
    v0 = recv_ref[0:per, :] + extra[0] * own0 + extra[1] * own1
    v1 = recv_ref[per : 2 * per, :] + extra[2] * own0 + extra[3] * own1
    phase = lax.broadcasted_iota(jnp.int32, (rows, lanes), 0) % per
    t0 = jnp.zeros((rows, lanes), jnp.float32)
    t1 = jnp.zeros((rows, lanes), jnp.float32)
    for p in range(per):
        t0 = jnp.where(phase == p, v0[p : p + 1], t0)
        t1 = jnp.where(phase == p, v1[p : p + 1], t1)
    nv_ref[...] = sv_ref[...] + (coef_ref[0] * t0 + coef_ref[1] * t1)
    np_ref[...] = sp_ref[...] + (coef_ref[2] * t0 + coef_ref[3] * t1)


def settle_and_solve(faces_in, sat_view, heat_res, vel_view, pres_view, levels, block_inverse, forward_map, backward_map):
    assert lax.axis_size("gz") == 2
    packet_width, slot_count = faces_in[0].shape
    record_width = packet_width - 1
    rows, lanes = sat_view.shape
    per = rows // levels
    offset = jnp.full((1,), lax.axis_index("gz") * levels, jnp.int32)
    smem = pl.BlockSpec(memory_space=pltpu.SMEM)
    vmem = pl.BlockSpec(memory_space=pltpu.VMEM)
    arrived, sv, sp, message, coef = pl.pallas_call(
        arrive_solve_kernel,
        out_shape=(
            jax.ShapeDtypeStruct((len(faces_in), record_width, slot_count), jnp.float32),
            jax.ShapeDtypeStruct((rows, lanes), jnp.float32),
            jax.ShapeDtypeStruct((rows, lanes), jnp.float32),
            jax.ShapeDtypeStruct((2 * per + 4, lanes), jnp.float32),
            jax.ShapeDtypeStruct((4, rows, lanes), jnp.float32),
        ),
        in_specs=[smem] * 4 + [vmem] * (len(faces_in) + 4),
        out_specs=(vmem,) * 5,
        scratch_shapes=[
            pltpu.VMEM((rows, lanes), jnp.float32),
            pltpu.SMEM((4, levels), jnp.float32),
        ],
        cost_estimate=pl.CostEstimate(
            flops=8 * sat_view.size * len(faces_in) * slot_count + 40 * rows * lanes,
            bytes_accessed=4 * (2 * packet_width) * len(faces_in) * slot_count + 40 * rows * lanes,
            transcendentals=len(faces_in) * slot_count,
        ),
    )(offset, block_inverse, forward_map, backward_map, *faces_in, sat_view, heat_res, vel_view, pres_view)
    received = lax.ppermute(message, "gz", [(0, 1), (1, 0)])
    new_v, new_p = pl.pallas_call(
        correct_kernel,
        out_shape=(
            jax.ShapeDtypeStruct((rows, lanes), jnp.float32),
            jax.ShapeDtypeStruct((rows, lanes), jnp.float32),
        ),
        in_specs=[vmem] * 5,
        out_specs=(vmem, vmem),
        cost_estimate=pl.CostEstimate(
            flops=8 * rows * lanes, bytes_accessed=32 * rows * lanes, transcendentals=0
        ),
    )(coef, message, received, sv, sp)
    return arrived, new_v, new_p


def along_x(packet_face, offset):
    return shifted(packet_face, "gx", offset)


def along_y(packet_face, offset):
    return shifted(packet_face, "gy", offset)


def body(
    droplets,
    cell_index,
    crossing,
    crossing_count,
    saturation,
    velocity,
    pressure,
    block_inverse,
    forward_map,
    backward_map,
):
    records = droplets[0, 0, 0]
    cell_ids = cell_index[0, 0, 0]
    levels = saturation.shape[0]
    view = (saturation.size // 128, 128)
    sat_view = saturation.reshape(view)
    packet, staying = emit_packets(
        records, cell_ids, crossing[0, 0, 0], crossing_count[0, 0, 0], CX, CY
    )
    from_west = along_x(packet[0], 1)
    from_east = along_x(packet[1], -1)
    from_south = along_y(packet[2], 1)
    from_north = along_y(packet[3], -1)
    resident, heat_res = settle_residents(
        records,
        cell_index.reshape(1, -1),
        staying.astype(jnp.float32).reshape(1, -1),
        sat_view,
    )
    arrived, solved_v, solved_p = settle_and_solve(
        (from_west, from_east, from_south, from_north),
        sat_view,
        heat_res,
        velocity.reshape(view),
        pressure.reshape(view),
        levels,
        block_inverse,
        forward_map,
        backward_map,
    )
    new_velocity = solved_v.reshape(velocity.shape)
    new_pressure = solved_p.reshape(pressure.shape)
    return (resident[None, None, None], arrived[None, None, None], new_velocity, new_pressure)


def solution(mesh):
    return jax.shard_map(
        body,
        mesh=mesh,
        in_specs=(
            P("gz", "gx", "gy", None, None),
            P("gz", "gx", "gy", None),
            P("gz", "gx", "gy", None, None),
            P("gz", "gx", "gy", None),
            P("gz", "gx", "gy", None),
            P("gz", "gx", "gy", None),
            P("gz", "gx", "gy", None),
            P(),
            P(),
            P(),
        ),
        out_specs=(
            P("gz", "gx", "gy", None, None),
            P("gz", "gx", "gy", None, None, None),
            P("gz", "gx", "gy", None),
            P("gz", "gx", "gy", None),
        ),
        check_vma=False,
    )
```

```python
import math

import jax
import jax.numpy as jnp
from jax import lax
from jax.sharding import PartitionSpec as P
from jax.experimental import pallas as pl
from jax.experimental.pallas import tpu as pltpu

CX = 8
CY = 32


GROW = 0.4
CURVATURE = 0.05
FLOOR_SQ = 0.09
BUOYANCY = 0.5
EXACT = lax.Precision.HIGHEST


def shifted(value, axis, steps):
    count = lax.axis_size(axis)
    pairs = [(source, (source + steps) % count) for source in range(count)]
    return lax.ppermute(value, axis, pairs)


def one_hot_of(index, width, dtype):
    return (index[:, None] == lax.broadcasted_iota(jnp.int32, (1, width), 1)).astype(dtype)


def emit_packets(records, cell_ids, leavers, live_count, width_x, width_y):
    record_width, drop_count = records.shape
    slot_count = leavers.shape[1]
    slot_ids = lax.broadcasted_iota(jnp.int32, (4, slot_count), 1)
    face_ids = lax.broadcasted_iota(jnp.int32, (4, slot_count), 0)
    in_use = slot_ids < live_count[:, None]
    inner = min(128, drop_count)
    outer = drop_count // inner
    table = jnp.concatenate([records, cell_ids.astype(jnp.float32)[None, :]], axis=0).reshape(
        record_width + 1, outer, inner
    )
    flat_leavers = leavers.reshape(-1)
    flat_use = in_use.reshape(-1).astype(jnp.bfloat16)
    block_rows = 4 * slot_count

    def pick_block(inputs):
        ids_block, use_block = inputs
        upper = one_hot_of(ids_block // inner, outer, jnp.float32)
        lower = one_hot_of(ids_block % inner, inner, jnp.float32)
        rows = jnp.einsum(
            "nh,rhl->nrl", upper, table, precision=EXACT, preferred_element_type=jnp.float32
        )
        picked_block = jnp.sum(rows * lower[:, None, :], axis=2)
        upper_used = upper.astype(jnp.bfloat16) * use_block[:, None]
        counts = jnp.einsum(
            "nh,nl->hl", upper_used, lower.astype(jnp.bfloat16), preferred_element_type=jnp.float32
        )
        return (picked_block, counts)

    picked_blocks, count_blocks = lax.map(
        pick_block, (flat_leavers.reshape(-1, block_rows), flat_use.reshape(-1, block_rows))
    )
    picked_all = picked_blocks.reshape(4, slot_count, record_width + 1)
    departed = jnp.sum(count_blocks, axis=0).reshape(-1)
    picked = jnp.moveaxis(picked_all[:, :, :record_width], 2, 1)
    source = (picked_all[:, :, record_width] + 0.5).astype(jnp.int32)
    height = source // (width_x * width_y)
    cell_x = source // width_y % width_x
    cell_y = source % width_y
    new_x = jnp.where(face_ids == 0, 0, jnp.where(face_ids == 1, width_x - 1, cell_x))
    new_y = jnp.where(face_ids == 2, 0, jnp.where(face_ids == 3, width_y - 1, cell_y))
    target = height * (width_x * width_y) + new_x * width_y + new_y
    packet = jnp.concatenate([picked, target.astype(records.dtype)[:, None, :]], axis=1)
    packet = jnp.where(in_use[:, None, :], packet, 0.0)
    return (packet, departed == 0.0)


def emit_kernel(count_ref, view_ref, cells_ref, cross_ref, *outs):
    face_refs = outs[:-1]
    stay_ref = outs[-1]
    view_rows, lanes = view_ref.shape
    outer = cells_ref.shape[0]
    record_width = view_rows // outer
    slot_count = cross_ref.shape[1]
    shift = lanes.bit_length() - 1
    rec_stack = jnp.concatenate(split_pieces3(view_ref[...]), axis=0)
    cell_stack = jnp.concatenate(split_pieces3(cells_ref[...].astype(jnp.float32)), axis=0)
    counted = jnp.zeros((outer, lanes), jnp.float32)
    for face, out_ref in enumerate(face_refs):
        index = cross_ref[face : face + 1, :]
        high = lax.shift_right_logical(index, shift)
        low = jnp.bitwise_and(index, lanes - 1)
        lane_hot = jnp.where(
            lax.broadcasted_iota(jnp.int32, (lanes, slot_count), 0) == low, 1.0, 0.0
        ).astype(jnp.bfloat16)
        high_mask = lax.broadcasted_iota(jnp.int32, (outer, slot_count), 0) == high
        got = jnp.dot(rec_stack, lane_hot, preferred_element_type=jnp.float32)
        got = got[:view_rows] + got[view_rows : 2 * view_rows] + got[2 * view_rows :]
        got = got.reshape(outer, record_width, slot_count)
        picked = jnp.sum(jnp.where(high_mask[:, None, :], got, 0.0), axis=0)
        got_cell = jnp.dot(cell_stack, lane_hot, preferred_element_type=jnp.float32)
        got_cell = got_cell[:outer] + got_cell[outer : 2 * outer] + got_cell[2 * outer :]
        source = (jnp.sum(jnp.where(high_mask, got_cell, 0.0), axis=0, keepdims=True) + 0.5).astype(jnp.int32)
        height = lax.shift_right_logical(source, (CX * CY).bit_length() - 1)
        cell_x = jnp.bitwise_and(lax.shift_right_logical(source, CY.bit_length() - 1), CX - 1)
        cell_y = jnp.bitwise_and(source, CY - 1)
        new_x = 0 if face == 0 else (CX - 1 if face == 1 else cell_x)
        new_y = 0 if face == 2 else (CY - 1 if face == 3 else cell_y)
        target = (height * (CX * CY) + new_x * CY + new_y).astype(jnp.float32)
        in_use = lax.broadcasted_iota(jnp.int32, (1, slot_count), 1) < count_ref[face]
        packet = jnp.concatenate([picked, jnp.broadcast_to(target, (1, slot_count))], axis=0)
        out_ref[...] = jnp.where(in_use, packet, 0.0)
        used_high = jnp.where(high_mask & in_use, 1.0, 0.0).astype(jnp.bfloat16)
        counted = counted + lax.dot_general(
            used_high, lane_hot, (((1,), (1,)), ((), ())), preferred_element_type=jnp.float32
        )
    stay_ref[...] = jnp.where(counted == 0.0, 1.0, 0.0)


def emit_faces(records, cell_index, crossing, crossing_count):
    record_width, drop_count = records.shape
    lanes = 128
    outer = drop_count // lanes
    faces, slot_count = crossing.shape
    view = records.reshape(record_width, outer, lanes).transpose(1, 0, 2).reshape(outer * record_width, lanes)
    smem = pl.BlockSpec(memory_space=pltpu.SMEM)
    vmem = pl.BlockSpec(memory_space=pltpu.VMEM)
    results = pl.pallas_call(
        emit_kernel,
        out_shape=tuple(
            jax.ShapeDtypeStruct((record_width + 1, slot_count), jnp.float32) for _ in range(faces)
        )
        + (jax.ShapeDtypeStruct((outer, lanes), jnp.float32),),
        in_specs=[smem, vmem, vmem, vmem],
        out_specs=(vmem,) * (faces + 1),
        cost_estimate=pl.CostEstimate(
            flops=6 * (record_width + 1) * drop_count * faces * slot_count // outer,
            bytes_accessed=4 * (record_width + 1) * drop_count + 8 * (record_width + 1) * faces * slot_count,
            transcendentals=0,
        ),
    )(crossing_count, view, cell_index.reshape(outer, lanes), crossing)
    return results[:faces], results[faces]


def split_pieces3(value):
    high = value.astype(jnp.bfloat16)
    rest = value - high.astype(jnp.float32)
    middle = rest.astype(jnp.bfloat16)
    low = (rest - middle.astype(jnp.float32)).astype(jnp.bfloat16)
    return (high, middle, low)


def split_pieces(value):
    high = value.astype(jnp.bfloat16)
    low = (value - high.astype(jnp.float32)).astype(jnp.bfloat16)
    return (high, low)


def stacked_pieces(value):
    return jnp.concatenate(split_pieces(value), axis=0)


def condense_chunk(records, cells, occupied, sat_stack):
    rows = sat_stack.shape[0] // 2
    lanes = sat_stack.shape[1]
    width = cells.shape[1]
    shift = lanes.bit_length() - 1
    row_of = lax.shift_right_logical(cells, shift)
    lane_of = jnp.bitwise_and(cells, lanes - 1)
    lane_mask = lax.broadcasted_iota(jnp.int32, (lanes, width), 0) == lane_of
    lane_hot = jnp.where(lane_mask, 1.0, 0.0).astype(jnp.bfloat16)
    row_mask = lax.broadcasted_iota(jnp.int32, (rows, width), 0) == row_of
    row_hot = jnp.where(row_mask, 1.0, 0.0).astype(jnp.bfloat16)
    picked = jnp.dot(sat_stack, lane_hot, preferred_element_type=jnp.float32)
    picked = picked[:rows] + picked[rows:]
    excess = jnp.sum(jnp.where(row_mask, picked, 0.0), axis=0, keepdims=True)
    radius = jnp.where(occupied, records[0:1], 1.0)
    dry_radius = records[2:3]
    solute = records[3:4]
    radius_cubed = radius * radius * radius
    squared = jnp.maximum(
        radius * radius
        + GROW
        * (
            excess
            - CURVATURE / radius
            + solute * dry_radius * dry_radius * dry_radius / radius_cubed
        ),
        FLOOR_SQ,
    )
    grown = jnp.sqrt(squared)
    condensed = jnp.where(occupied, records[1:2] * (grown * grown * grown - radius_cubed), 0.0)
    spread = jnp.concatenate([row_hot * piece for piece in split_pieces(condensed)], axis=0)
    heat = lax.dot_general(
        spread, lane_hot, (((1,), (1,)), ((), ())), preferred_element_type=jnp.float32
    )
    heat = heat[:rows] + heat[rows:]
    updated = jnp.concatenate([grown, records[1:]], axis=0)
    updated = jnp.where(occupied, updated, 0.0)
    return (updated, heat)


def resident_kernel(rec_ref, cell_ref, stay_ref, sat_ref, out_ref, heat_ref):
    step = pl.program_id(0)
    updated, heat = condense_chunk(
        rec_ref[...], cell_ref[...], stay_ref[...] > 0.0, stacked_pieces(sat_ref[...])
    )
    out_ref[...] = updated

    @pl.when(step == 0)
    def _():
        heat_ref[...] = heat

    @pl.when(step > 0)
    def _():
        heat_ref[...] += heat


def settle_residents(records, cell_row, staying_row, sat_view):
    record_width, drop_count = records.shape
    rows, lanes = sat_view.shape
    chunk = min(4096, drop_count)
    whole = lambda j: (0, 0)
    by_chunk = lambda j: (0, j)
    return pl.pallas_call(
        resident_kernel,
        grid=(drop_count // chunk,),
        out_shape=(
            jax.ShapeDtypeStruct((record_width, drop_count), jnp.float32),
            jax.ShapeDtypeStruct((rows, lanes), jnp.float32),
        ),
        in_specs=[
            pl.BlockSpec((record_width, chunk), by_chunk),
            pl.BlockSpec((1, chunk), by_chunk),
            pl.BlockSpec((1, chunk), by_chunk),
            pl.BlockSpec((rows, lanes), whole),
        ],
        out_specs=(
            pl.BlockSpec((record_width, chunk), by_chunk),
            pl.BlockSpec((rows, lanes), whole),
        ),
        cost_estimate=pl.CostEstimate(
            flops=12 * rows * lanes * drop_count,
            bytes_accessed=4 * (2 * record_width + 2) * drop_count,
            transcendentals=drop_count,
        ),
    )(records, cell_row, staying_row, sat_view)


def arrivals_into(faces, sat_ref, res_ref, vel_ref, out_ref, force_ref):
    record_width = out_ref.shape[1]
    sat_stack = stacked_pieces(sat_ref[...])
    total = res_ref[...]
    for face, in_ref in enumerate(faces):
        packet = in_ref[...]
        records = packet[:record_width]
        cells = (packet[record_width : record_width + 1] + 0.5).astype(jnp.int32)
        occupied = records[1:2] > 0.0
        updated, heat = condense_chunk(records, cells, occupied, sat_stack)
        out_ref[face] = updated
        total = total + heat
    force_ref[...] = vel_ref[...] + BUOYANCY * total


def solve_into(off_ref, bi_ref, fm_ref, bm_ref, fv_ref, fp_ref, sv_ref, sp_ref, msg_ref, coef_ref, xs_ref):
    rows, lanes = fv_ref.shape
    levels = xs_ref.shape[1]
    per = rows // levels
    off = off_ref[0]
    upper = jnp.where(off > 0, 1.0, 0.0).astype(jnp.float32)
    lower = 1.0 - upper
    zero = jnp.zeros((per, lanes), jnp.float32)

    def forward(k, carry):
        uv, up, x0, x1, x2, x3 = carry
        level = off + k
        b0 = bi_ref[0, level]
        b1 = bi_ref[1, level]
        b2 = bi_ref[2, level]
        b3 = bi_ref[3, level]
        f0 = fm_ref[0, level]
        f1 = fm_ref[1, level]
        f2 = fm_ref[2, level]
        f3 = fm_ref[3, level]
        at = pl.ds(pl.multiple_of(k * per, per), per)
        gv = fv_ref[at, :]
        gp = fp_ref[at, :]
        nuv = (b0 * gv + b1 * gp) + (f0 * uv + f1 * up)
        nup = (b2 * gv + b3 * gp) + (f2 * uv + f3 * up)
        sv_ref[at, :] = nuv
        sp_ref[at, :] = nup
        y0 = f0 * x0 + f1 * x2
        y1 = f0 * x1 + f1 * x3
        y2 = f2 * x0 + f3 * x2
        y3 = f2 * x1 + f3 * x3
        xs_ref[0, k] = y0
        xs_ref[1, k] = y1
        xs_ref[2, k] = y2
        xs_ref[3, k] = y3
        return (nuv, nup, y0, y1, y2, y3)

    uv, up, _, _, _, _ = lax.fori_loop(
        0, levels, forward, (zero, zero, upper, 0.0 * upper, 0.0 * upper, upper), unroll=4
    )

    def backward(step, carry):
        sv, sp, c0, c1, c2, c3 = carry
        k = levels - 1 - step
        level = off + k
        m0 = bm_ref[0, level]
        m1 = bm_ref[1, level]
        m2 = bm_ref[2, level]
        m3 = bm_ref[3, level]
        at = pl.ds(pl.multiple_of(k * per, per), per)
        nsv = sv_ref[at, :] + (m0 * sv + m1 * sp)
        nsp = sp_ref[at, :] + (m2 * sv + m3 * sp)
        sv_ref[at, :] = nsv
        sp_ref[at, :] = nsp
        d0 = xs_ref[0, k] + (m0 * c0 + m1 * c2)
        d1 = xs_ref[1, k] + (m0 * c1 + m1 * c3)
        d2 = xs_ref[2, k] + (m2 * c0 + m3 * c2)
        d3 = xs_ref[3, k] + (m2 * c1 + m3 * c3)
        coef_ref[0, at, :] = jnp.full((per, lanes), d0, jnp.float32)
        coef_ref[1, at, :] = jnp.full((per, lanes), d1, jnp.float32)
        coef_ref[2, at, :] = jnp.full((per, lanes), d2, jnp.float32)
        coef_ref[3, at, :] = jnp.full((per, lanes), d3, jnp.float32)
        return (nsv, nsp, d0, d1, d2, d3)

    sv, sp, d0, d1, d2, d3 = lax.fori_loop(
        0, levels, backward, (zero, zero, lower, 0.0 * lower, 0.0 * lower, lower), unroll=4
    )
    msg_ref[0:per, :] = lower * uv + upper * sv
    msg_ref[per : 2 * per, :] = lower * up + upper * sp
    for index, value in enumerate((d0, d1, d2, d3)):
        msg_ref[2 * per + index : 2 * per + index + 1, :] = jnp.full((1, lanes), upper * value, jnp.float32)


def arrive_solve_kernel(
    off_ref, bi_ref, fm_ref, bm_ref, w_ref, e_ref, s_ref, n_ref, sat_ref, res_ref, vel_ref, pres_ref,
    out_ref, sv_ref, sp_ref, msg_ref, coef_ref, force_ref, xs_ref,
):
    arrivals_into((w_ref, e_ref, s_ref, n_ref), sat_ref, res_ref, vel_ref, out_ref, force_ref)
    solve_into(off_ref, bi_ref, fm_ref, bm_ref, force_ref, pres_ref, sv_ref, sp_ref, msg_ref, coef_ref, xs_ref)


def correct_kernel(coef_ref, own_ref, recv_ref, sv_ref, sp_ref, nv_ref, np_ref):
    rows, lanes = sv_ref.shape
    per = (own_ref.shape[0] - 4) // 2
    own0 = own_ref[0:per, :]
    own1 = own_ref[per : 2 * per, :]
    extra = [recv_ref[2 * per + i : 2 * per + i + 1, :] for i in range(4)]
    v0 = recv_ref[0:per, :] + extra[0] * own0 + extra[1] * own1
    v1 = recv_ref[per : 2 * per, :] + extra[2] * own0 + extra[3] * own1
    phase = lax.broadcasted_iota(jnp.int32, (rows, lanes), 0) % per
    t0 = jnp.zeros((rows, lanes), jnp.float32)
    t1 = jnp.zeros((rows, lanes), jnp.float32)
    for p in range(per):
        t0 = jnp.where(phase == p, v0[p : p + 1], t0)
        t1 = jnp.where(phase == p, v1[p : p + 1], t1)
    nv_ref[...] = sv_ref[...] + (coef_ref[0] * t0 + coef_ref[1] * t1)
    np_ref[...] = sp_ref[...] + (coef_ref[2] * t0 + coef_ref[3] * t1)


def settle_and_solve(faces_in, sat_view, heat_res, vel_view, pres_view, levels, block_inverse, forward_map, backward_map):
    assert lax.axis_size("gz") == 2
    packet_width, slot_count = faces_in[0].shape
    record_width = packet_width - 1
    rows, lanes = sat_view.shape
    per = rows // levels
    offset = jnp.full((1,), lax.axis_index("gz") * levels, jnp.int32)
    smem = pl.BlockSpec(memory_space=pltpu.SMEM)
    vmem = pl.BlockSpec(memory_space=pltpu.VMEM)
    arrived, sv, sp, message, coef = pl.pallas_call(
        arrive_solve_kernel,
        out_shape=(
            jax.ShapeDtypeStruct((len(faces_in), record_width, slot_count), jnp.float32),
            jax.ShapeDtypeStruct((rows, lanes), jnp.float32),
            jax.ShapeDtypeStruct((rows, lanes), jnp.float32),
            jax.ShapeDtypeStruct((2 * per + 4, lanes), jnp.float32),
            jax.ShapeDtypeStruct((4, rows, lanes), jnp.float32),
        ),
        in_specs=[smem] * 4 + [vmem] * (len(faces_in) + 4),
        out_specs=(vmem,) * 5,
        scratch_shapes=[
            pltpu.VMEM((rows, lanes), jnp.float32),
            pltpu.SMEM((4, levels), jnp.float32),
        ],
        cost_estimate=pl.CostEstimate(
            flops=8 * sat_view.size * len(faces_in) * slot_count + 40 * rows * lanes,
            bytes_accessed=4 * (2 * packet_width) * len(faces_in) * slot_count + 40 * rows * lanes,
            transcendentals=len(faces_in) * slot_count,
        ),
    )(offset, block_inverse, forward_map, backward_map, *faces_in, sat_view, heat_res, vel_view, pres_view)
    received = lax.ppermute(message, "gz", [(0, 1), (1, 0)])
    new_v, new_p = pl.pallas_call(
        correct_kernel,
        out_shape=(
            jax.ShapeDtypeStruct((rows, lanes), jnp.float32),
            jax.ShapeDtypeStruct((rows, lanes), jnp.float32),
        ),
        in_specs=[vmem] * 5,
        out_specs=(vmem, vmem),
        cost_estimate=pl.CostEstimate(
            flops=8 * rows * lanes, bytes_accessed=32 * rows * lanes, transcendentals=0
        ),
    )(coef, message, received, sv, sp)
    return arrived, new_v, new_p


def along_x(packet_face, offset):
    return shifted(packet_face, "gx", offset)


def along_y(packet_face, offset):
    return shifted(packet_face, "gy", offset)


def body(
    droplets,
    cell_index,
    crossing,
    crossing_count,
    saturation,
    velocity,
    pressure,
    block_inverse,
    forward_map,
    backward_map,
):
    records = droplets[0, 0, 0]
    cell_ids = cell_index[0, 0, 0]
    levels = saturation.shape[0]
    view = (saturation.size // 128, 128)
    sat_view = saturation.reshape(view)
    faces_out, staying_view = emit_faces(
        records, cell_index, crossing[0, 0, 0], crossing_count[0, 0, 0]
    )
    from_west = along_x(faces_out[0], 1)
    from_east = along_x(faces_out[1], -1)
    from_south = along_y(faces_out[2], 1)
    from_north = along_y(faces_out[3], -1)
    resident, heat_res = settle_residents(
        records,
        cell_index.reshape(1, -1),
        staying_view.reshape(1, -1),
        sat_view,
    )
    arrived, solved_v, solved_p = settle_and_solve(
        (from_west, from_east, from_south, from_north),
        sat_view,
        heat_res,
        velocity.reshape(view),
        pressure.reshape(view),
        levels,
        block_inverse,
        forward_map,
        backward_map,
    )
    new_velocity = solved_v.reshape(velocity.shape)
    new_pressure = solved_p.reshape(pressure.shape)
    return (resident[None, None, None], arrived[None, None, None], new_velocity, new_pressure)


def solution(mesh):
    return jax.shard_map(
        body,
        mesh=mesh,
        in_specs=(
            P("gz", "gx", "gy", None, None),
            P("gz", "gx", "gy", None),
            P("gz", "gx", "gy", None, None),
            P("gz", "gx", "gy", None),
            P("gz", "gx", "gy", None),
            P("gz", "gx", "gy", None),
            P("gz", "gx", "gy", None),
            P(),
            P(),
            P(),
        ),
        out_specs=(
            P("gz", "gx", "gy", None, None),
            P("gz", "gx", "gy", None, None, None),
            P("gz", "gx", "gy", None),
            P("gz", "gx", "gy", None),
        ),
        check_vma=False,
    )
```

```python
import math

import jax
import jax.numpy as jnp
from jax import lax
from jax.sharding import PartitionSpec as P
from jax.experimental import pallas as pl
from jax.experimental.pallas import tpu as pltpu

CX = 8
CY = 32


GROW = 0.4
CURVATURE = 0.05
FLOOR_SQ = 0.09
BUOYANCY = 0.5
EXACT = lax.Precision.HIGHEST


def shifted(value, axis, steps):
    count = lax.axis_size(axis)
    pairs = [(source, (source + steps) % count) for source in range(count)]
    return lax.ppermute(value, axis, pairs)


def one_hot_of(index, width, dtype):
    return (index[:, None] == lax.broadcasted_iota(jnp.int32, (1, width), 1)).astype(dtype)


def emit_packets(records, cell_ids, leavers, live_count, width_x, width_y):
    record_width, drop_count = records.shape
    slot_count = leavers.shape[1]
    slot_ids = lax.broadcasted_iota(jnp.int32, (4, slot_count), 1)
    face_ids = lax.broadcasted_iota(jnp.int32, (4, slot_count), 0)
    in_use = slot_ids < live_count[:, None]
    inner = min(128, drop_count)
    outer = drop_count // inner
    table = jnp.concatenate([records, cell_ids.astype(jnp.float32)[None, :]], axis=0).reshape(
        record_width + 1, outer, inner
    )
    flat_leavers = leavers.reshape(-1)
    flat_use = in_use.reshape(-1).astype(jnp.bfloat16)
    block_rows = 4 * slot_count

    def pick_block(inputs):
        ids_block, use_block = inputs
        upper = one_hot_of(ids_block // inner, outer, jnp.float32)
        lower = one_hot_of(ids_block % inner, inner, jnp.float32)
        rows = jnp.einsum(
            "nh,rhl->nrl", upper, table, precision=EXACT, preferred_element_type=jnp.float32
        )
        picked_block = jnp.sum(rows * lower[:, None, :], axis=2)
        upper_used = upper.astype(jnp.bfloat16) * use_block[:, None]
        counts = jnp.einsum(
            "nh,nl->hl", upper_used, lower.astype(jnp.bfloat16), preferred_element_type=jnp.float32
        )
        return (picked_block, counts)

    picked_blocks, count_blocks = lax.map(
        pick_block, (flat_leavers.reshape(-1, block_rows), flat_use.reshape(-1, block_rows))
    )
    picked_all = picked_blocks.reshape(4, slot_count, record_width + 1)
    departed = jnp.sum(count_blocks, axis=0).reshape(-1)
    picked = jnp.moveaxis(picked_all[:, :, :record_width], 2, 1)
    source = (picked_all[:, :, record_width] + 0.5).astype(jnp.int32)
    height = source // (width_x * width_y)
    cell_x = source // width_y % width_x
    cell_y = source % width_y
    new_x = jnp.where(face_ids == 0, 0, jnp.where(face_ids == 1, width_x - 1, cell_x))
    new_y = jnp.where(face_ids == 2, 0, jnp.where(face_ids == 3, width_y - 1, cell_y))
    target = height * (width_x * width_y) + new_x * width_y + new_y
    packet = jnp.concatenate([picked, target.astype(records.dtype)[:, None, :]], axis=1)
    packet = jnp.where(in_use[:, None, :], packet, 0.0)
    return (packet, departed == 0.0)


def emit_kernel(count_ref, view_ref, cells_ref, cross_ref, *outs):
    face_refs = outs[:-1]
    stay_ref = outs[-1]
    view_rows, lanes = view_ref.shape
    outer = cells_ref.shape[0]
    record_width = view_rows // outer
    slot_count = cross_ref.shape[1]
    shift = lanes.bit_length() - 1
    rec_stack = jnp.concatenate(split_pieces3(view_ref[...]), axis=1)
    cell_stack = jnp.concatenate(split_pieces3(cells_ref[...].astype(jnp.float32)), axis=1)
    counted = jnp.zeros((outer, lanes), jnp.float32)
    for face, out_ref in enumerate(face_refs):
        index = cross_ref[face : face + 1, :]
        high = lax.shift_right_logical(index, shift)
        low = jnp.bitwise_and(index, lanes - 1)
        lane_hot = jnp.where(
            lax.broadcasted_iota(jnp.int32, (lanes, slot_count), 0).astype(jnp.bfloat16)
            == low.astype(jnp.bfloat16),
            jnp.bfloat16(1.0),
            jnp.bfloat16(0.0),
        )
        high_mask = lax.broadcasted_iota(jnp.int32, (outer, slot_count), 0) == high
        lane_hot3 = jnp.concatenate([lane_hot, lane_hot, lane_hot], axis=0)
        got = jnp.dot(rec_stack, lane_hot3, preferred_element_type=jnp.float32)
        got = got.reshape(outer, record_width, slot_count)
        picked = jnp.sum(jnp.where(high_mask[:, None, :], got, 0.0), axis=0)
        got_cell = jnp.dot(cell_stack, lane_hot3, preferred_element_type=jnp.float32)
        source = (jnp.sum(jnp.where(high_mask, got_cell, 0.0), axis=0, keepdims=True) + 0.5).astype(jnp.int32)
        height = lax.shift_right_logical(source, (CX * CY).bit_length() - 1)
        cell_x = jnp.bitwise_and(lax.shift_right_logical(source, CY.bit_length() - 1), CX - 1)
        cell_y = jnp.bitwise_and(source, CY - 1)
        new_x = 0 if face == 0 else (CX - 1 if face == 1 else cell_x)
        new_y = 0 if face == 2 else (CY - 1 if face == 3 else cell_y)
        target = (height * (CX * CY) + new_x * CY + new_y).astype(jnp.float32)
        in_use = lax.broadcasted_iota(jnp.int32, (1, slot_count), 1) < count_ref[face]
        packet = jnp.concatenate([picked, jnp.broadcast_to(target, (1, slot_count))], axis=0)
        out_ref[...] = jnp.where(in_use, packet, 0.0)
        used_high = jnp.where(high_mask & in_use, 1.0, 0.0).astype(jnp.bfloat16)
        counted = counted + lax.dot_general(
            used_high, lane_hot, (((1,), (1,)), ((), ())), preferred_element_type=jnp.float32
        )
    stay_ref[...] = jnp.where(counted == 0.0, 1.0, 0.0)


def emit_faces(records, cell_index, crossing, crossing_count):
    record_width, drop_count = records.shape
    lanes = 128
    outer = drop_count // lanes
    faces, slot_count = crossing.shape
    view = records.reshape(record_width, outer, lanes).transpose(1, 0, 2).reshape(outer * record_width, lanes)
    smem = pl.BlockSpec(memory_space=pltpu.SMEM)
    vmem = pl.BlockSpec(memory_space=pltpu.VMEM)
    results = pl.pallas_call(
        emit_kernel,
        out_shape=tuple(
            jax.ShapeDtypeStruct((record_width + 1, slot_count), jnp.float32) for _ in range(faces)
        )
        + (jax.ShapeDtypeStruct((outer, lanes), jnp.float32),),
        in_specs=[smem, vmem, vmem, vmem],
        out_specs=(vmem,) * (faces + 1),
        cost_estimate=pl.CostEstimate(
            flops=6 * (record_width + 1) * drop_count * faces * slot_count // outer,
            bytes_accessed=4 * (record_width + 1) * drop_count + 8 * (record_width + 1) * faces * slot_count,
            transcendentals=0,
        ),
    )(crossing_count, view, cell_index.reshape(outer, lanes), crossing)
    return results[:faces], results[faces]


def split_pieces3(value):
    high = value.astype(jnp.bfloat16)
    rest = value - high.astype(jnp.float32)
    middle = rest.astype(jnp.bfloat16)
    low = (rest - middle.astype(jnp.float32)).astype(jnp.bfloat16)
    return (high, middle, low)


def split_pieces(value):
    high = value.astype(jnp.bfloat16)
    low = (value - high.astype(jnp.float32)).astype(jnp.bfloat16)
    return (high, low)


def stacked_pieces(value):
    return jnp.concatenate(split_pieces(value), axis=1)


def condense_chunk(records, cells, occupied, sat_stack):
    rows = sat_stack.shape[0]
    lanes = sat_stack.shape[1] // 2
    width = cells.shape[1]
    shift = lanes.bit_length() - 1
    row_of = lax.shift_right_logical(cells, shift)
    lane_of = jnp.bitwise_and(cells, lanes - 1)
    lane_mask = lax.broadcasted_iota(jnp.int32, (lanes, width), 0).astype(jnp.bfloat16) == lane_of.astype(jnp.bfloat16)
    lane_hot = jnp.where(lane_mask, jnp.bfloat16(1.0), jnp.bfloat16(0.0))
    row_mask = lax.broadcasted_iota(jnp.int32, (rows, width), 0) == row_of
    row_hot = jnp.where(lax.broadcasted_iota(jnp.int32, (rows, width), 0).astype(jnp.bfloat16) == row_of.astype(jnp.bfloat16), jnp.bfloat16(1.0), jnp.bfloat16(0.0))
    picked = jnp.dot(sat_stack, jnp.concatenate([lane_hot, lane_hot], axis=0), preferred_element_type=jnp.float32)
    excess = jnp.sum(jnp.where(row_mask, picked, 0.0), axis=0, keepdims=True)
    radius = jnp.where(occupied, records[0:1], 1.0)
    dry_radius = records[2:3]
    solute = records[3:4]
    radius_cubed = radius * radius * radius
    squared = jnp.maximum(
        radius * radius
        + GROW
        * (
            excess
            - CURVATURE / radius
            + solute * dry_radius * dry_radius * dry_radius / radius_cubed
        ),
        FLOOR_SQ,
    )
    grown = jnp.sqrt(squared)
    condensed = jnp.where(occupied, records[1:2] * (grown * grown * grown - radius_cubed), 0.0)
    spread = jnp.concatenate([row_hot * piece for piece in split_pieces(condensed)], axis=0)
    heat = lax.dot_general(
        spread, lane_hot, (((1,), (1,)), ((), ())), preferred_element_type=jnp.float32
    )
    heat = heat[:rows] + heat[rows:]
    updated = jnp.concatenate([grown, records[1:]], axis=0)
    updated = jnp.where(occupied, updated, 0.0)
    return (updated, heat)


def resident_kernel(rec_ref, cell_ref, stay_ref, sat_ref, out_ref, heat_ref):
    step = pl.program_id(0)
    updated, heat = condense_chunk(
        rec_ref[...], cell_ref[...], stay_ref[...] > 0.0, stacked_pieces(sat_ref[...])
    )
    out_ref[...] = updated

    @pl.when(step == 0)
    def _():
        heat_ref[...] = heat

    @pl.when(step > 0)
    def _():
        heat_ref[...] += heat


def settle_residents(records, cell_row, staying_row, sat_view):
    record_width, drop_count = records.shape
    rows, lanes = sat_view.shape
    chunk = min(4096, drop_count)
    whole = lambda j: (0, 0)
    by_chunk = lambda j: (0, j)
    return pl.pallas_call(
        resident_kernel,
        grid=(drop_count // chunk,),
        out_shape=(
            jax.ShapeDtypeStruct((record_width, drop_count), jnp.float32),
            jax.ShapeDtypeStruct((rows, lanes), jnp.float32),
        ),
        in_specs=[
            pl.BlockSpec((record_width, chunk), by_chunk),
            pl.BlockSpec((1, chunk), by_chunk),
            pl.BlockSpec((1, chunk), by_chunk),
            pl.BlockSpec((rows, lanes), whole),
        ],
        out_specs=(
            pl.BlockSpec((record_width, chunk), by_chunk),
            pl.BlockSpec((rows, lanes), whole),
        ),
        cost_estimate=pl.CostEstimate(
            flops=12 * rows * lanes * drop_count,
            bytes_accessed=4 * (2 * record_width + 2) * drop_count,
            transcendentals=drop_count,
        ),
    )(records, cell_row, staying_row, sat_view)


def arrivals_into(faces, sat_ref, res_ref, vel_ref, out_ref, force_ref):
    record_width = out_ref.shape[1]
    sat_stack = stacked_pieces(sat_ref[...])
    total = res_ref[...]
    for face, in_ref in enumerate(faces):
        packet = in_ref[...]
        records = packet[:record_width]
        cells = (packet[record_width : record_width + 1] + 0.5).astype(jnp.int32)
        occupied = records[1:2] > 0.0
        updated, heat = condense_chunk(records, cells, occupied, sat_stack)
        out_ref[face] = updated
        total = total + heat
    force_ref[...] = vel_ref[...] + BUOYANCY * total


def solve_into(off_ref, bi_ref, fm_ref, bm_ref, fv_ref, fp_ref, sv_ref, sp_ref, msg_ref, coef_ref, xs_ref):
    rows, lanes = fv_ref.shape
    levels = xs_ref.shape[1]
    per = rows // levels
    off = off_ref[0]
    upper = jnp.where(off > 0, 1.0, 0.0).astype(jnp.float32)
    lower = 1.0 - upper
    zero = jnp.zeros((per, lanes), jnp.float32)

    def forward(k, carry):
        uv, up, x0, x1, x2, x3 = carry
        level = off + k
        b0 = bi_ref[0, level]
        b1 = bi_ref[1, level]
        b2 = bi_ref[2, level]
        b3 = bi_ref[3, level]
        f0 = fm_ref[0, level]
        f1 = fm_ref[1, level]
        f2 = fm_ref[2, level]
        f3 = fm_ref[3, level]
        at = pl.ds(pl.multiple_of(k * per, per), per)
        gv = fv_ref[at, :]
        gp = fp_ref[at, :]
        nuv = (b0 * gv + b1 * gp) + (f0 * uv + f1 * up)
        nup = (b2 * gv + b3 * gp) + (f2 * uv + f3 * up)
        sv_ref[at, :] = nuv
        sp_ref[at, :] = nup
        y0 = f0 * x0 + f1 * x2
        y1 = f0 * x1 + f1 * x3
        y2 = f2 * x0 + f3 * x2
        y3 = f2 * x1 + f3 * x3
        xs_ref[0, k] = y0
        xs_ref[1, k] = y1
        xs_ref[2, k] = y2
        xs_ref[3, k] = y3
        return (nuv, nup, y0, y1, y2, y3)

    uv, up, _, _, _, _ = lax.fori_loop(
        0, levels, forward, (zero, zero, upper, 0.0 * upper, 0.0 * upper, upper), unroll=4
    )

    def backward(step, carry):
        sv, sp, c0, c1, c2, c3 = carry
        k = levels - 1 - step
        level = off + k
        m0 = bm_ref[0, level]
        m1 = bm_ref[1, level]
        m2 = bm_ref[2, level]
        m3 = bm_ref[3, level]
        at = pl.ds(pl.multiple_of(k * per, per), per)
        nsv = sv_ref[at, :] + (m0 * sv + m1 * sp)
        nsp = sp_ref[at, :] + (m2 * sv + m3 * sp)
        sv_ref[at, :] = nsv
        sp_ref[at, :] = nsp
        d0 = xs_ref[0, k] + (m0 * c0 + m1 * c2)
        d1 = xs_ref[1, k] + (m0 * c1 + m1 * c3)
        d2 = xs_ref[2, k] + (m2 * c0 + m3 * c2)
        d3 = xs_ref[3, k] + (m2 * c1 + m3 * c3)
        coef_ref[0, at, :] = jnp.full((per, lanes), d0, jnp.float32)
        coef_ref[1, at, :] = jnp.full((per, lanes), d1, jnp.float32)
        coef_ref[2, at, :] = jnp.full((per, lanes), d2, jnp.float32)
        coef_ref[3, at, :] = jnp.full((per, lanes), d3, jnp.float32)
        return (nsv, nsp, d0, d1, d2, d3)

    sv, sp, d0, d1, d2, d3 = lax.fori_loop(
        0, levels, backward, (zero, zero, lower, 0.0 * lower, 0.0 * lower, lower), unroll=4
    )
    msg_ref[0:per, :] = lower * uv + upper * sv
    msg_ref[per : 2 * per, :] = lower * up + upper * sp
    for index, value in enumerate((d0, d1, d2, d3)):
        msg_ref[2 * per + index : 2 * per + index + 1, :] = jnp.full((1, lanes), upper * value, jnp.float32)


def arrive_solve_kernel(
    off_ref, bi_ref, fm_ref, bm_ref, w_ref, e_ref, s_ref, n_ref, sat_ref, res_ref, vel_ref, pres_ref,
    out_ref, sv_ref, sp_ref, msg_ref, coef_ref, force_ref, xs_ref,
):
    arrivals_into((w_ref, e_ref, s_ref, n_ref), sat_ref, res_ref, vel_ref, out_ref, force_ref)
    solve_into(off_ref, bi_ref, fm_ref, bm_ref, force_ref, pres_ref, sv_ref, sp_ref, msg_ref, coef_ref, xs_ref)


def correct_kernel(coef_ref, own_ref, recv_ref, sv_ref, sp_ref, nv_ref, np_ref):
    rows, lanes = sv_ref.shape
    per = (own_ref.shape[0] - 4) // 2
    own0 = own_ref[0:per, :]
    own1 = own_ref[per : 2 * per, :]
    extra = [recv_ref[2 * per + i : 2 * per + i + 1, :] for i in range(4)]
    v0 = recv_ref[0:per, :] + extra[0] * own0 + extra[1] * own1
    v1 = recv_ref[per : 2 * per, :] + extra[2] * own0 + extra[3] * own1
    phase = lax.broadcasted_iota(jnp.int32, (rows, lanes), 0) % per
    t0 = jnp.zeros((rows, lanes), jnp.float32)
    t1 = jnp.zeros((rows, lanes), jnp.float32)
    for p in range(per):
        t0 = jnp.where(phase == p, v0[p : p + 1], t0)
        t1 = jnp.where(phase == p, v1[p : p + 1], t1)
    nv_ref[...] = sv_ref[...] + (coef_ref[0] * t0 + coef_ref[1] * t1)
    np_ref[...] = sp_ref[...] + (coef_ref[2] * t0 + coef_ref[3] * t1)


def settle_and_solve(faces_in, sat_view, heat_res, vel_view, pres_view, levels, block_inverse, forward_map, backward_map):
    assert lax.axis_size("gz") == 2
    packet_width, slot_count = faces_in[0].shape
    record_width = packet_width - 1
    rows, lanes = sat_view.shape
    per = rows // levels
    offset = jnp.full((1,), lax.axis_index("gz") * levels, jnp.int32)
    smem = pl.BlockSpec(memory_space=pltpu.SMEM)
    vmem = pl.BlockSpec(memory_space=pltpu.VMEM)
    arrived, sv, sp, message, coef = pl.pallas_call(
        arrive_solve_kernel,
        out_shape=(
            jax.ShapeDtypeStruct((len(faces_in), record_width, slot_count), jnp.float32),
            jax.ShapeDtypeStruct((rows, lanes), jnp.float32),
            jax.ShapeDtypeStruct((rows, lanes), jnp.float32),
            jax.ShapeDtypeStruct((2 * per + 4, lanes), jnp.float32),
            jax.ShapeDtypeStruct((4, rows, lanes), jnp.float32),
        ),
        in_specs=[smem] * 4 + [vmem] * (len(faces_in) + 4),
        out_specs=(vmem,) * 5,
        scratch_shapes=[
            pltpu.VMEM((rows, lanes), jnp.float32),
            pltpu.SMEM((4, levels), jnp.float32),
        ],
        cost_estimate=pl.CostEstimate(
            flops=8 * sat_view.size * len(faces_in) * slot_count + 40 * rows * lanes,
            bytes_accessed=4 * (2 * packet_width) * len(faces_in) * slot_count + 40 * rows * lanes,
            transcendentals=len(faces_in) * slot_count,
        ),
    )(offset, block_inverse, forward_map, backward_map, *faces_in, sat_view, heat_res, vel_view, pres_view)
    received = lax.ppermute(message, "gz", [(0, 1), (1, 0)])
    new_v, new_p = pl.pallas_call(
        correct_kernel,
        out_shape=(
            jax.ShapeDtypeStruct((rows, lanes), jnp.float32),
            jax.ShapeDtypeStruct((rows, lanes), jnp.float32),
        ),
        in_specs=[vmem] * 5,
        out_specs=(vmem, vmem),
        cost_estimate=pl.CostEstimate(
            flops=8 * rows * lanes, bytes_accessed=32 * rows * lanes, transcendentals=0
        ),
    )(coef, message, received, sv, sp)
    return arrived, new_v, new_p


def along_x(packet_face, offset):
    return shifted(packet_face, "gx", offset)


def along_y(packet_face, offset):
    return shifted(packet_face, "gy", offset)


def body(
    droplets,
    cell_index,
    crossing,
    crossing_count,
    saturation,
    velocity,
    pressure,
    block_inverse,
    forward_map,
    backward_map,
):
    records = droplets[0, 0, 0]
    cell_ids = cell_index[0, 0, 0]
    levels = saturation.shape[0]
    view = (saturation.size // 128, 128)
    sat_view = saturation.reshape(view)
    faces_out, staying_view = emit_faces(
        records, cell_index, crossing[0, 0, 0], crossing_count[0, 0, 0]
    )
    from_west = along_x(faces_out[0], 1)
    from_east = along_x(faces_out[1], -1)
    from_south = along_y(faces_out[2], 1)
    from_north = along_y(faces_out[3], -1)
    resident, heat_res = settle_residents(
        records,
        cell_index.reshape(1, -1),
        staying_view.reshape(1, -1),
        sat_view,
    )
    arrived, solved_v, solved_p = settle_and_solve(
        (from_west, from_east, from_south, from_north),
        sat_view,
        heat_res,
        velocity.reshape(view),
        pressure.reshape(view),
        levels,
        block_inverse,
        forward_map,
        backward_map,
    )
    new_velocity = solved_v.reshape(velocity.shape)
    new_pressure = solved_p.reshape(pressure.shape)
    return (resident[None, None, None], arrived[None, None, None], new_velocity, new_pressure)


def solution(mesh):
    return jax.shard_map(
        body,
        mesh=mesh,
        in_specs=(
            P("gz", "gx", "gy", None, None),
            P("gz", "gx", "gy", None),
            P("gz", "gx", "gy", None, None),
            P("gz", "gx", "gy", None),
            P("gz", "gx", "gy", None),
            P("gz", "gx", "gy", None),
            P("gz", "gx", "gy", None),
            P(),
            P(),
            P(),
        ),
        out_specs=(
            P("gz", "gx", "gy", None, None),
            P("gz", "gx", "gy", None, None, None),
            P("gz", "gx", "gy", None),
            P("gz", "gx", "gy", None),
        ),
        check_vma=False,
    )
```

```python
import math

import jax
import jax.numpy as jnp
from jax import lax
from jax.sharding import PartitionSpec as P
from jax.experimental import pallas as pl
from jax.experimental.pallas import tpu as pltpu

CX = 8
CY = 32


GROW = 0.4
CURVATURE = 0.05
FLOOR_SQ = 0.09
BUOYANCY = 0.5
EXACT = lax.Precision.HIGHEST


def shifted(value, axis, steps):
    count = lax.axis_size(axis)
    pairs = [(source, (source + steps) % count) for source in range(count)]
    return lax.ppermute(value, axis, pairs)


def one_hot_of(index, width, dtype):
    return (index[:, None] == lax.broadcasted_iota(jnp.int32, (1, width), 1)).astype(dtype)


def emit_packets(records, cell_ids, leavers, live_count, width_x, width_y):
    record_width, drop_count = records.shape
    slot_count = leavers.shape[1]
    slot_ids = lax.broadcasted_iota(jnp.int32, (4, slot_count), 1)
    face_ids = lax.broadcasted_iota(jnp.int32, (4, slot_count), 0)
    in_use = slot_ids < live_count[:, None]
    inner = min(128, drop_count)
    outer = drop_count // inner
    table = jnp.concatenate([records, cell_ids.astype(jnp.float32)[None, :]], axis=0).reshape(
        record_width + 1, outer, inner
    )
    flat_leavers = leavers.reshape(-1)
    flat_use = in_use.reshape(-1).astype(jnp.bfloat16)
    block_rows = 4 * slot_count

    def pick_block(inputs):
        ids_block, use_block = inputs
        upper = one_hot_of(ids_block // inner, outer, jnp.float32)
        lower = one_hot_of(ids_block % inner, inner, jnp.float32)
        rows = jnp.einsum(
            "nh,rhl->nrl", upper, table, precision=EXACT, preferred_element_type=jnp.float32
        )
        picked_block = jnp.sum(rows * lower[:, None, :], axis=2)
        upper_used = upper.astype(jnp.bfloat16) * use_block[:, None]
        counts = jnp.einsum(
            "nh,nl->hl", upper_used, lower.astype(jnp.bfloat16), preferred_element_type=jnp.float32
        )
        return (picked_block, counts)

    picked_blocks, count_blocks = lax.map(
        pick_block, (flat_leavers.reshape(-1, block_rows), flat_use.reshape(-1, block_rows))
    )
    picked_all = picked_blocks.reshape(4, slot_count, record_width + 1)
    departed = jnp.sum(count_blocks, axis=0).reshape(-1)
    picked = jnp.moveaxis(picked_all[:, :, :record_width], 2, 1)
    source = (picked_all[:, :, record_width] + 0.5).astype(jnp.int32)
    height = source // (width_x * width_y)
    cell_x = source // width_y % width_x
    cell_y = source % width_y
    new_x = jnp.where(face_ids == 0, 0, jnp.where(face_ids == 1, width_x - 1, cell_x))
    new_y = jnp.where(face_ids == 2, 0, jnp.where(face_ids == 3, width_y - 1, cell_y))
    target = height * (width_x * width_y) + new_x * width_y + new_y
    packet = jnp.concatenate([picked, target.astype(records.dtype)[:, None, :]], axis=1)
    packet = jnp.where(in_use[:, None, :], packet, 0.0)
    return (packet, departed == 0.0)


def emit_kernel(count_ref, view_ref, cells_ref, cross_ref, *outs):
    face_refs = outs[:-1]
    stay_ref = outs[-1]
    view_rows, lanes = view_ref.shape
    outer = cells_ref.shape[0]
    record_width = view_rows // outer
    slot_count = cross_ref.shape[1]
    shift = lanes.bit_length() - 1
    rec_stack = jnp.concatenate(split_pieces3(view_ref[...]), axis=1)
    cell_stack = jnp.concatenate(split_pieces3(cells_ref[...].astype(jnp.float32)), axis=1)
    counted = jnp.zeros((outer, lanes), jnp.float32)
    for face, out_ref in enumerate(face_refs):
        index = cross_ref[face : face + 1, :]
        high = lax.shift_right_logical(index, shift)
        low = jnp.bitwise_and(index, lanes - 1)
        lane_hot = jnp.where(
            lax.broadcasted_iota(jnp.int32, (lanes, slot_count), 0).astype(jnp.bfloat16)
            == low.astype(jnp.bfloat16),
            jnp.bfloat16(1.0),
            jnp.bfloat16(0.0),
        )
        high_mask = lax.broadcasted_iota(jnp.int32, (outer, slot_count), 0) == high
        lane_hot3 = jnp.concatenate([lane_hot, lane_hot, lane_hot], axis=0)
        got = jnp.dot(rec_stack, lane_hot3, preferred_element_type=jnp.float32)
        got = got.reshape(outer, record_width, slot_count)
        picked = jnp.sum(jnp.where(high_mask[:, None, :], got, 0.0), axis=0)
        got_cell = jnp.dot(cell_stack, lane_hot3, preferred_element_type=jnp.float32)
        source = (jnp.sum(jnp.where(high_mask, got_cell, 0.0), axis=0, keepdims=True) + 0.5).astype(jnp.int32)
        height = lax.shift_right_logical(source, (CX * CY).bit_length() - 1)
        cell_x = jnp.bitwise_and(lax.shift_right_logical(source, CY.bit_length() - 1), CX - 1)
        cell_y = jnp.bitwise_and(source, CY - 1)
        new_x = 0 if face == 0 else (CX - 1 if face == 1 else cell_x)
        new_y = 0 if face == 2 else (CY - 1 if face == 3 else cell_y)
        target = (height * (CX * CY) + new_x * CY + new_y).astype(jnp.float32)
        in_use = lax.broadcasted_iota(jnp.int32, (1, slot_count), 1) < count_ref[face]
        packet = jnp.concatenate([picked, jnp.broadcast_to(target, (1, slot_count))], axis=0)
        out_ref[...] = jnp.where(in_use, packet, 0.0)
        used_high = jnp.where(high_mask & in_use, 1.0, 0.0).astype(jnp.bfloat16)
        counted = counted + lax.dot_general(
            used_high, lane_hot, (((1,), (1,)), ((), ())), preferred_element_type=jnp.float32
        )
    stay_ref[...] = jnp.where(counted == 0.0, 1.0, 0.0)


def emit_faces(records, cell_index, crossing, crossing_count):
    record_width, drop_count = records.shape
    lanes = 128
    outer = drop_count // lanes
    faces, slot_count = crossing.shape
    view = records.reshape(record_width, outer, lanes).transpose(1, 0, 2).reshape(outer * record_width, lanes)
    smem = pl.BlockSpec(memory_space=pltpu.SMEM)
    vmem = pl.BlockSpec(memory_space=pltpu.VMEM)
    results = pl.pallas_call(
        emit_kernel,
        out_shape=tuple(
            jax.ShapeDtypeStruct((record_width + 1, slot_count), jnp.float32) for _ in range(faces)
        )
        + (jax.ShapeDtypeStruct((outer, lanes), jnp.float32),),
        in_specs=[smem, vmem, vmem, vmem],
        out_specs=(vmem,) * (faces + 1),
        cost_estimate=pl.CostEstimate(
            flops=6 * (record_width + 1) * drop_count * faces * slot_count // outer,
            bytes_accessed=4 * (record_width + 1) * drop_count + 8 * (record_width + 1) * faces * slot_count,
            transcendentals=0,
        ),
    )(crossing_count, view, cell_index.reshape(outer, lanes), crossing)
    return results[:faces], results[faces]


def split_pieces3(value):
    high = value.astype(jnp.bfloat16)
    rest = value - high.astype(jnp.float32)
    middle = rest.astype(jnp.bfloat16)
    low = (rest - middle.astype(jnp.float32)).astype(jnp.bfloat16)
    return (high, middle, low)


def split_pieces(value):
    high = value.astype(jnp.bfloat16)
    low = (value - high.astype(jnp.float32)).astype(jnp.bfloat16)
    return (high, low)


def stacked_pieces(value):
    return jnp.concatenate(split_pieces(value), axis=1)


def condense_chunk(records, cells, occupied, sat_stack):
    rows = sat_stack.shape[0]
    lanes = sat_stack.shape[1] // 2
    width = cells.shape[1]
    shift = lanes.bit_length() - 1
    row_of = lax.shift_right_logical(cells, shift)
    lane_of = jnp.bitwise_and(cells, lanes - 1)
    lane_mask = lax.broadcasted_iota(jnp.int32, (lanes, width), 0).astype(jnp.bfloat16) == lane_of.astype(jnp.bfloat16)
    lane_hot = jnp.where(lane_mask, jnp.bfloat16(1.0), jnp.bfloat16(0.0))
    row_mask = lax.broadcasted_iota(jnp.int32, (rows, width), 0) == row_of
    row_hot = jnp.where(lax.broadcasted_iota(jnp.int32, (rows, width), 0).astype(jnp.bfloat16) == row_of.astype(jnp.bfloat16), jnp.bfloat16(1.0), jnp.bfloat16(0.0))
    picked = jnp.dot(sat_stack, jnp.concatenate([lane_hot, lane_hot], axis=0), preferred_element_type=jnp.float32)
    excess = jnp.sum(jnp.where(row_mask, picked, 0.0), axis=0, keepdims=True)
    radius = jnp.where(occupied, records[0:1], 1.0)
    dry_radius = records[2:3]
    solute = records[3:4]
    radius_cubed = radius * radius * radius
    squared = jnp.maximum(
        radius * radius
        + GROW
        * (
            excess
            - CURVATURE / radius
            + solute * dry_radius * dry_radius * dry_radius / radius_cubed
        ),
        FLOOR_SQ,
    )
    grown = jnp.sqrt(squared)
    condensed = jnp.where(occupied, records[1:2] * (grown * grown * grown - radius_cubed), 0.0)
    spread = jnp.concatenate([row_hot * piece for piece in split_pieces(condensed)], axis=0)
    heat = lax.dot_general(
        spread, lane_hot, (((1,), (1,)), ((), ())), preferred_element_type=jnp.float32
    )
    heat = heat[:rows] + heat[rows:]
    updated = jnp.concatenate([grown, records[1:]], axis=0)
    updated = jnp.where(occupied, updated, 0.0)
    return (updated, heat)


def resident_kernel(rec_ref, cell_ref, stay_ref, sat_ref, out_ref, heat_ref):
    step = pl.program_id(0)
    updated, heat = condense_chunk(
        rec_ref[...], cell_ref[...], stay_ref[...] > 0.0, stacked_pieces(sat_ref[...])
    )
    out_ref[...] = updated

    @pl.when(step == 0)
    def _():
        heat_ref[...] = heat

    @pl.when(step > 0)
    def _():
        heat_ref[...] += heat


def settle_residents(records, cell_row, staying_row, sat_view):
    record_width, drop_count = records.shape
    rows, lanes = sat_view.shape
    chunk = min(4096, drop_count)
    whole = lambda j: (0, 0)
    by_chunk = lambda j: (0, j)
    return pl.pallas_call(
        resident_kernel,
        grid=(drop_count // chunk,),
        out_shape=(
            jax.ShapeDtypeStruct((record_width, drop_count), jnp.float32),
            jax.ShapeDtypeStruct((rows, lanes), jnp.float32),
        ),
        in_specs=[
            pl.BlockSpec((record_width, chunk), by_chunk),
            pl.BlockSpec((1, chunk), by_chunk),
            pl.BlockSpec((1, chunk), by_chunk),
            pl.BlockSpec((rows, lanes), whole),
        ],
        out_specs=(
            pl.BlockSpec((record_width, chunk), by_chunk),
            pl.BlockSpec((rows, lanes), whole),
        ),
        cost_estimate=pl.CostEstimate(
            flops=12 * rows * lanes * drop_count,
            bytes_accessed=4 * (2 * record_width + 2) * drop_count,
            transcendentals=drop_count,
        ),
    )(records, cell_row, staying_row, sat_view)


def arrivals_into(faces, sat_ref, res_ref, vel_ref, out_ref, force_ref):
    record_width = out_ref.shape[1]
    sat_stack = stacked_pieces(sat_ref[...])
    total = res_ref[...]
    for face, in_ref in enumerate(faces):
        packet = in_ref[...]
        records = packet[:record_width]
        cells = (packet[record_width : record_width + 1] + 0.5).astype(jnp.int32)
        occupied = records[1:2] > 0.0
        updated, heat = condense_chunk(records, cells, occupied, sat_stack)
        out_ref[face] = updated
        total = total + heat
    force_ref[...] = vel_ref[...] + BUOYANCY * total


def solve_into(off_ref, bi_ref, fm_ref, bm_ref, fv_ref, fp_ref, sv_ref, sp_ref, msg_ref, coef_ref, xs_ref):
    rows, lanes = fv_ref.shape
    levels = xs_ref.shape[1]
    per = rows // levels
    off = off_ref[0]
    upper = jnp.where(off > 0, 1.0, 0.0).astype(jnp.float32)
    lower = 1.0 - upper
    zero = jnp.zeros((per, lanes), jnp.float32)
    one = jnp.ones((1, lanes), jnp.float32)
    flat = jnp.zeros((1, lanes), jnp.float32)

    def forward(k, carry):
        uv, up, x0, x1, x2, x3 = carry
        level = off + k
        b0 = bi_ref[0, level]
        b1 = bi_ref[1, level]
        b2 = bi_ref[2, level]
        b3 = bi_ref[3, level]
        f0 = fm_ref[0, level]
        f1 = fm_ref[1, level]
        f2 = fm_ref[2, level]
        f3 = fm_ref[3, level]
        at = pl.ds(pl.multiple_of(k * per, per), per)
        gv = fv_ref[at, :]
        gp = fp_ref[at, :]
        nuv = (b0 * gv + b1 * gp) + (f0 * uv + f1 * up)
        nup = (b2 * gv + b3 * gp) + (f2 * uv + f3 * up)
        sv_ref[at, :] = nuv
        sp_ref[at, :] = nup
        y0 = f0 * x0 + f1 * x2
        y1 = f0 * x1 + f1 * x3
        y2 = f2 * x0 + f3 * x2
        y3 = f2 * x1 + f3 * x3
        xs_ref[0, pl.ds(k, 1), :] = y0
        xs_ref[1, pl.ds(k, 1), :] = y1
        xs_ref[2, pl.ds(k, 1), :] = y2
        xs_ref[3, pl.ds(k, 1), :] = y3
        return (nuv, nup, y0, y1, y2, y3)

    uv, up, _, _, _, _ = lax.fori_loop(
        0, levels, forward, (zero, zero, upper * one, flat, flat, upper * one), unroll=True
    )

    def backward(step, carry):
        sv, sp, c0, c1, c2, c3 = carry
        k = levels - 1 - step
        level = off + k
        m0 = bm_ref[0, level]
        m1 = bm_ref[1, level]
        m2 = bm_ref[2, level]
        m3 = bm_ref[3, level]
        at = pl.ds(pl.multiple_of(k * per, per), per)
        nsv = sv_ref[at, :] + (m0 * sv + m1 * sp)
        nsp = sp_ref[at, :] + (m2 * sv + m3 * sp)
        sv_ref[at, :] = nsv
        sp_ref[at, :] = nsp
        d0 = xs_ref[0, pl.ds(k, 1), :] + (m0 * c0 + m1 * c2)
        d1 = xs_ref[1, pl.ds(k, 1), :] + (m0 * c1 + m1 * c3)
        d2 = xs_ref[2, pl.ds(k, 1), :] + (m2 * c0 + m3 * c2)
        d3 = xs_ref[3, pl.ds(k, 1), :] + (m2 * c1 + m3 * c3)
        coef_ref[0, at, :] = jnp.broadcast_to(d0, (per, lanes))
        coef_ref[1, at, :] = jnp.broadcast_to(d1, (per, lanes))
        coef_ref[2, at, :] = jnp.broadcast_to(d2, (per, lanes))
        coef_ref[3, at, :] = jnp.broadcast_to(d3, (per, lanes))
        return (nsv, nsp, d0, d1, d2, d3)

    sv, sp, d0, d1, d2, d3 = lax.fori_loop(
        0, levels, backward, (zero, zero, lower * one, flat, flat, lower * one), unroll=True
    )
    msg_ref[0:per, :] = lower * uv + upper * sv
    msg_ref[per : 2 * per, :] = lower * up + upper * sp
    for index, value in enumerate((d0, d1, d2, d3)):
        msg_ref[2 * per + index : 2 * per + index + 1, :] = upper * value


def arrive_solve_kernel(
    off_ref, bi_ref, fm_ref, bm_ref, w_ref, e_ref, s_ref, n_ref, sat_ref, res_ref, vel_ref, pres_ref,
    out_ref, sv_ref, sp_ref, msg_ref, coef_ref, force_ref, xs_ref,
):
    arrivals_into((w_ref, e_ref, s_ref, n_ref), sat_ref, res_ref, vel_ref, out_ref, force_ref)
    solve_into(off_ref, bi_ref, fm_ref, bm_ref, force_ref, pres_ref, sv_ref, sp_ref, msg_ref, coef_ref, xs_ref)


def correct_kernel(coef_ref, own_ref, recv_ref, sv_ref, sp_ref, nv_ref, np_ref):
    rows, lanes = sv_ref.shape
    per = (own_ref.shape[0] - 4) // 2
    own0 = own_ref[0:per, :]
    own1 = own_ref[per : 2 * per, :]
    extra = [recv_ref[2 * per + i : 2 * per + i + 1, :] for i in range(4)]
    v0 = recv_ref[0:per, :] + extra[0] * own0 + extra[1] * own1
    v1 = recv_ref[per : 2 * per, :] + extra[2] * own0 + extra[3] * own1
    phase = lax.broadcasted_iota(jnp.int32, (rows, lanes), 0) % per
    t0 = jnp.zeros((rows, lanes), jnp.float32)
    t1 = jnp.zeros((rows, lanes), jnp.float32)
    for p in range(per):
        t0 = jnp.where(phase == p, v0[p : p + 1], t0)
        t1 = jnp.where(phase == p, v1[p : p + 1], t1)
    nv_ref[...] = sv_ref[...] + (coef_ref[0] * t0 + coef_ref[1] * t1)
    np_ref[...] = sp_ref[...] + (coef_ref[2] * t0 + coef_ref[3] * t1)


def settle_and_solve(faces_in, sat_view, heat_res, vel_view, pres_view, levels, block_inverse, forward_map, backward_map):
    assert lax.axis_size("gz") == 2
    packet_width, slot_count = faces_in[0].shape
    record_width = packet_width - 1
    rows, lanes = sat_view.shape
    per = rows // levels
    offset = jnp.full((1,), lax.axis_index("gz") * levels, jnp.int32)
    smem = pl.BlockSpec(memory_space=pltpu.SMEM)
    vmem = pl.BlockSpec(memory_space=pltpu.VMEM)
    arrived, sv, sp, message, coef = pl.pallas_call(
        arrive_solve_kernel,
        out_shape=(
            jax.ShapeDtypeStruct((len(faces_in), record_width, slot_count), jnp.float32),
            jax.ShapeDtypeStruct((rows, lanes), jnp.float32),
            jax.ShapeDtypeStruct((rows, lanes), jnp.float32),
            jax.ShapeDtypeStruct((2 * per + 4, lanes), jnp.float32),
            jax.ShapeDtypeStruct((4, rows, lanes), jnp.float32),
        ),
        in_specs=[smem] * 4 + [vmem] * (len(faces_in) + 4),
        out_specs=(vmem,) * 5,
        scratch_shapes=[
            pltpu.VMEM((rows, lanes), jnp.float32),
            pltpu.VMEM((4, levels, lanes), jnp.float32),
        ],
        cost_estimate=pl.CostEstimate(
            flops=8 * sat_view.size * len(faces_in) * slot_count + 40 * rows * lanes,
            bytes_accessed=4 * (2 * packet_width) * len(faces_in) * slot_count + 40 * rows * lanes,
            transcendentals=len(faces_in) * slot_count,
        ),
    )(offset, block_inverse, forward_map, backward_map, *faces_in, sat_view, heat_res, vel_view, pres_view)
    received = lax.ppermute(message, "gz", [(0, 1), (1, 0)])
    new_v, new_p = pl.pallas_call(
        correct_kernel,
        out_shape=(
            jax.ShapeDtypeStruct((rows, lanes), jnp.float32),
            jax.ShapeDtypeStruct((rows, lanes), jnp.float32),
        ),
        in_specs=[vmem] * 5,
        out_specs=(vmem, vmem),
        cost_estimate=pl.CostEstimate(
            flops=8 * rows * lanes, bytes_accessed=32 * rows * lanes, transcendentals=0
        ),
    )(coef, message, received, sv, sp)
    return arrived, new_v, new_p


def along_x(packet_face, offset):
    return shifted(packet_face, "gx", offset)


def along_y(packet_face, offset):
    return shifted(packet_face, "gy", offset)


def body(
    droplets,
    cell_index,
    crossing,
    crossing_count,
    saturation,
    velocity,
    pressure,
    block_inverse,
    forward_map,
    backward_map,
):
    records = droplets[0, 0, 0]
    cell_ids = cell_index[0, 0, 0]
    levels = saturation.shape[0]
    view = (saturation.size // 128, 128)
    sat_view = saturation.reshape(view)
    faces_out, staying_view = emit_faces(
        records, cell_index, crossing[0, 0, 0], crossing_count[0, 0, 0]
    )
    from_west = along_x(faces_out[0], 1)
    from_east = along_x(faces_out[1], -1)
    from_south = along_y(faces_out[2], 1)
    from_north = along_y(faces_out[3], -1)
    resident, heat_res = settle_residents(
        records,
        cell_index.reshape(1, -1),
        staying_view.reshape(1, -1),
        sat_view,
    )
    arrived, solved_v, solved_p = settle_and_solve(
        (from_west, from_east, from_south, from_north),
        sat_view,
        heat_res,
        velocity.reshape(view),
        pressure.reshape(view),
        levels,
        block_inverse,
        forward_map,
        backward_map,
    )
    new_velocity = solved_v.reshape(velocity.shape)
    new_pressure = solved_p.reshape(pressure.shape)
    return (resident[None, None, None], arrived[None, None, None], new_velocity, new_pressure)


def solution(mesh):
    return jax.shard_map(
        body,
        mesh=mesh,
        in_specs=(
            P("gz", "gx", "gy", None, None),
            P("gz", "gx", "gy", None),
            P("gz", "gx", "gy", None, None),
            P("gz", "gx", "gy", None),
            P("gz", "gx", "gy", None),
            P("gz", "gx", "gy", None),
            P("gz", "gx", "gy", None),
            P(),
            P(),
            P(),
        ),
        out_specs=(
            P("gz", "gx", "gy", None, None),
            P("gz", "gx", "gy", None, None, None),
            P("gz", "gx", "gy", None),
            P("gz", "gx", "gy", None),
        ),
        check_vma=False,
    )
```

```python
import math

import jax
import jax.numpy as jnp
from jax import lax
from jax.sharding import PartitionSpec as P
from jax.experimental import pallas as pl
from jax.experimental.pallas import tpu as pltpu

CX = 8
CY = 32


GROW = 0.4
CURVATURE = 0.05
FLOOR_SQ = 0.09
BUOYANCY = 0.5
EXACT = lax.Precision.HIGHEST


def shifted(value, axis, steps):
    count = lax.axis_size(axis)
    pairs = [(source, (source + steps) % count) for source in range(count)]
    return lax.ppermute(value, axis, pairs)


def one_hot_of(index, width, dtype):
    return (index[:, None] == lax.broadcasted_iota(jnp.int32, (1, width), 1)).astype(dtype)


def emit_packets(records, cell_ids, leavers, live_count, width_x, width_y):
    record_width, drop_count = records.shape
    slot_count = leavers.shape[1]
    slot_ids = lax.broadcasted_iota(jnp.int32, (4, slot_count), 1)
    face_ids = lax.broadcasted_iota(jnp.int32, (4, slot_count), 0)
    in_use = slot_ids < live_count[:, None]
    inner = min(128, drop_count)
    outer = drop_count // inner
    table = jnp.concatenate([records, cell_ids.astype(jnp.float32)[None, :]], axis=0).reshape(
        record_width + 1, outer, inner
    )
    flat_leavers = leavers.reshape(-1)
    flat_use = in_use.reshape(-1).astype(jnp.bfloat16)
    block_rows = 4 * slot_count

    def pick_block(inputs):
        ids_block, use_block = inputs
        upper = one_hot_of(ids_block // inner, outer, jnp.float32)
        lower = one_hot_of(ids_block % inner, inner, jnp.float32)
        rows = jnp.einsum(
            "nh,rhl->nrl", upper, table, precision=EXACT, preferred_element_type=jnp.float32
        )
        picked_block = jnp.sum(rows * lower[:, None, :], axis=2)
        upper_used = upper.astype(jnp.bfloat16) * use_block[:, None]
        counts = jnp.einsum(
            "nh,nl->hl", upper_used, lower.astype(jnp.bfloat16), preferred_element_type=jnp.float32
        )
        return (picked_block, counts)

    picked_blocks, count_blocks = lax.map(
        pick_block, (flat_leavers.reshape(-1, block_rows), flat_use.reshape(-1, block_rows))
    )
    picked_all = picked_blocks.reshape(4, slot_count, record_width + 1)
    departed = jnp.sum(count_blocks, axis=0).reshape(-1)
    picked = jnp.moveaxis(picked_all[:, :, :record_width], 2, 1)
    source = (picked_all[:, :, record_width] + 0.5).astype(jnp.int32)
    height = source // (width_x * width_y)
    cell_x = source // width_y % width_x
    cell_y = source % width_y
    new_x = jnp.where(face_ids == 0, 0, jnp.where(face_ids == 1, width_x - 1, cell_x))
    new_y = jnp.where(face_ids == 2, 0, jnp.where(face_ids == 3, width_y - 1, cell_y))
    target = height * (width_x * width_y) + new_x * width_y + new_y
    packet = jnp.concatenate([picked, target.astype(records.dtype)[:, None, :]], axis=1)
    packet = jnp.where(in_use[:, None, :], packet, 0.0)
    return (packet, departed == 0.0)


def emit_kernel(count_ref, view_ref, cells_ref, cross_ref, *outs):
    face_refs = outs[:-1]
    stay_ref = outs[-1]
    view_rows, lanes = view_ref.shape
    outer = cells_ref.shape[0]
    record_width = view_rows // outer
    slot_count = cross_ref.shape[1]
    shift = lanes.bit_length() - 1
    rec_stack = jnp.concatenate(split_pieces3(view_ref[...]), axis=1)
    cell_stack = jnp.concatenate(split_pieces3(cells_ref[...].astype(jnp.float32)), axis=1)
    counted = jnp.zeros((outer, lanes), jnp.float32)
    for face, out_ref in enumerate(face_refs):
        index = cross_ref[face : face + 1, :]
        high = lax.shift_right_logical(index, shift)
        low = jnp.bitwise_and(index, lanes - 1)
        lane_hot = jnp.where(
            lax.broadcasted_iota(jnp.int32, (lanes, slot_count), 0).astype(jnp.bfloat16)
            == low.astype(jnp.bfloat16),
            jnp.bfloat16(1.0),
            jnp.bfloat16(0.0),
        )
        high_mask = lax.broadcasted_iota(jnp.int32, (outer, slot_count), 0) == high
        lane_hot3 = jnp.concatenate([lane_hot, lane_hot, lane_hot], axis=0)
        got = jnp.dot(rec_stack, lane_hot3, preferred_element_type=jnp.float32)
        got = got.reshape(outer, record_width, slot_count)
        picked = jnp.sum(jnp.where(high_mask[:, None, :], got, 0.0), axis=0)
        got_cell = jnp.dot(cell_stack, lane_hot3, preferred_element_type=jnp.float32)
        source = (jnp.sum(jnp.where(high_mask, got_cell, 0.0), axis=0, keepdims=True) + 0.5).astype(jnp.int32)
        height = lax.shift_right_logical(source, (CX * CY).bit_length() - 1)
        cell_x = jnp.bitwise_and(lax.shift_right_logical(source, CY.bit_length() - 1), CX - 1)
        cell_y = jnp.bitwise_and(source, CY - 1)
        new_x = 0 if face == 0 else (CX - 1 if face == 1 else cell_x)
        new_y = 0 if face == 2 else (CY - 1 if face == 3 else cell_y)
        target = (height * (CX * CY) + new_x * CY + new_y).astype(jnp.float32)
        in_use = lax.broadcasted_iota(jnp.int32, (1, slot_count), 1) < count_ref[face]
        packet = jnp.concatenate([picked, jnp.broadcast_to(target, (1, slot_count))], axis=0)
        out_ref[...] = jnp.where(in_use, packet, 0.0)
        used_high = jnp.where(high_mask & in_use, 1.0, 0.0).astype(jnp.bfloat16)
        counted = counted + lax.dot_general(
            used_high, lane_hot, (((1,), (1,)), ((), ())), preferred_element_type=jnp.float32
        )
    stay_ref[...] = jnp.where(counted == 0.0, 1.0, 0.0)


def emit_faces(records, cell_index, crossing, crossing_count):
    record_width, drop_count = records.shape
    lanes = 128
    outer = drop_count // lanes
    faces, slot_count = crossing.shape
    view = records.reshape(record_width, outer, lanes).transpose(1, 0, 2).reshape(outer * record_width, lanes)
    smem = pl.BlockSpec(memory_space=pltpu.SMEM)
    vmem = pl.BlockSpec(memory_space=pltpu.VMEM)
    results = pl.pallas_call(
        emit_kernel,
        out_shape=tuple(
            jax.ShapeDtypeStruct((record_width + 1, slot_count), jnp.float32) for _ in range(faces)
        )
        + (jax.ShapeDtypeStruct((outer, lanes), jnp.float32),),
        in_specs=[smem, vmem, vmem, vmem],
        out_specs=(vmem,) * (faces + 1),
        cost_estimate=pl.CostEstimate(
            flops=6 * (record_width + 1) * drop_count * faces * slot_count // outer,
            bytes_accessed=4 * (record_width + 1) * drop_count + 8 * (record_width + 1) * faces * slot_count,
            transcendentals=0,
        ),
    )(crossing_count, view, cell_index.reshape(outer, lanes), crossing)
    return results[:faces], results[faces]


def split_pieces3(value):
    high = value.astype(jnp.bfloat16)
    rest = value - high.astype(jnp.float32)
    middle = rest.astype(jnp.bfloat16)
    low = (rest - middle.astype(jnp.float32)).astype(jnp.bfloat16)
    return (high, middle, low)


def split_pieces(value):
    high = value.astype(jnp.bfloat16)
    low = (value - high.astype(jnp.float32)).astype(jnp.bfloat16)
    return (high, low)


def stacked_pieces(value):
    return jnp.concatenate(split_pieces(value), axis=1)


def condense_chunk(records, cells, occupied, sat_stack):
    rows = sat_stack.shape[0]
    lanes = sat_stack.shape[1] // 2
    width = cells.shape[1]
    shift = lanes.bit_length() - 1
    row_of = lax.shift_right_logical(cells, shift)
    lane_of = jnp.bitwise_and(cells, lanes - 1)
    lane_mask = lax.broadcasted_iota(jnp.int32, (lanes, width), 0).astype(jnp.bfloat16) == lane_of.astype(jnp.bfloat16)
    lane_hot = jnp.where(lane_mask, jnp.bfloat16(1.0), jnp.bfloat16(0.0))
    row_mask = lax.broadcasted_iota(jnp.int32, (rows, width), 0) == row_of
    row_hot = jnp.where(lax.broadcasted_iota(jnp.int32, (rows, width), 0).astype(jnp.bfloat16) == row_of.astype(jnp.bfloat16), jnp.bfloat16(1.0), jnp.bfloat16(0.0))
    picked = jnp.dot(sat_stack, jnp.concatenate([lane_hot, lane_hot], axis=0), preferred_element_type=jnp.float32)
    excess = jnp.sum(jnp.where(row_mask, picked, 0.0), axis=0, keepdims=True)
    radius = jnp.where(occupied, records[0:1], 1.0)
    dry_radius = records[2:3]
    solute = records[3:4]
    radius_cubed = radius * radius * radius
    squared = jnp.maximum(
        radius * radius
        + GROW
        * (
            excess
            - CURVATURE / radius
            + solute * dry_radius * dry_radius * dry_radius / radius_cubed
        ),
        FLOOR_SQ,
    )
    grown = jnp.sqrt(squared)
    condensed = jnp.where(occupied, records[1:2] * (grown * grown * grown - radius_cubed), 0.0)
    spread = jnp.concatenate([row_hot * piece for piece in split_pieces(condensed)], axis=0)
    heat = lax.dot_general(
        spread, lane_hot, (((1,), (1,)), ((), ())), preferred_element_type=jnp.float32
    )
    heat = heat[:rows] + heat[rows:]
    updated = jnp.concatenate([grown, records[1:]], axis=0)
    updated = jnp.where(occupied, updated, 0.0)
    return (updated, heat)


def resident_kernel(rec_ref, cell_ref, stay_ref, sat_ref, out_ref, heat_ref):
    step = pl.program_id(0)
    updated, heat = condense_chunk(
        rec_ref[...], cell_ref[...], stay_ref[...] > 0.0, stacked_pieces(sat_ref[...])
    )
    out_ref[...] = updated

    @pl.when(step == 0)
    def _():
        heat_ref[...] = heat

    @pl.when(step > 0)
    def _():
        heat_ref[...] += heat


def settle_residents(records, cell_row, staying_row, sat_view):
    record_width, drop_count = records.shape
    rows, lanes = sat_view.shape
    chunk = min(8192, drop_count)
    whole = lambda j: (0, 0)
    by_chunk = lambda j: (0, j)
    return pl.pallas_call(
        resident_kernel,
        grid=(drop_count // chunk,),
        out_shape=(
            jax.ShapeDtypeStruct((record_width, drop_count), jnp.float32),
            jax.ShapeDtypeStruct((rows, lanes), jnp.float32),
        ),
        in_specs=[
            pl.BlockSpec((record_width, chunk), by_chunk),
            pl.BlockSpec((1, chunk), by_chunk),
            pl.BlockSpec((1, chunk), by_chunk),
            pl.BlockSpec((rows, lanes), whole),
        ],
        out_specs=(
            pl.BlockSpec((record_width, chunk), by_chunk),
            pl.BlockSpec((rows, lanes), whole),
        ),
        cost_estimate=pl.CostEstimate(
            flops=12 * rows * lanes * drop_count,
            bytes_accessed=4 * (2 * record_width + 2) * drop_count,
            transcendentals=drop_count,
        ),
    )(records, cell_row, staying_row, sat_view)


def arrivals_into(faces, sat_ref, res_ref, vel_ref, out_ref, force_ref):
    record_width = out_ref.shape[1]
    sat_stack = stacked_pieces(sat_ref[...])
    total = res_ref[...]
    for face, in_ref in enumerate(faces):
        packet = in_ref[...]
        records = packet[:record_width]
        cells = (packet[record_width : record_width + 1] + 0.5).astype(jnp.int32)
        occupied = records[1:2] > 0.0
        updated, heat = condense_chunk(records, cells, occupied, sat_stack)
        out_ref[face] = updated
        total = total + heat
    force_ref[...] = vel_ref[...] + BUOYANCY * total


def solve_into(off_ref, bi_ref, fm_ref, bm_ref, fv_ref, fp_ref, sv_ref, sp_ref, msg_ref, coef_ref, xs_ref):
    rows, lanes = fv_ref.shape
    levels = xs_ref.shape[1]
    per = rows // levels
    off = off_ref[0]
    upper = jnp.where(off > 0, 1.0, 0.0).astype(jnp.float32)
    lower = 1.0 - upper
    zero = jnp.zeros((per, lanes), jnp.float32)
    one = jnp.ones((1, lanes), jnp.float32)
    flat = jnp.zeros((1, lanes), jnp.float32)

    def forward(k, carry):
        uv, up, x0, x1, x2, x3 = carry
        level = off + k
        b0 = bi_ref[0, level]
        b1 = bi_ref[1, level]
        b2 = bi_ref[2, level]
        b3 = bi_ref[3, level]
        f0 = fm_ref[0, level]
        f1 = fm_ref[1, level]
        f2 = fm_ref[2, level]
        f3 = fm_ref[3, level]
        at = pl.ds(pl.multiple_of(k * per, per), per)
        gv = fv_ref[at, :]
        gp = fp_ref[at, :]
        nuv = (b0 * gv + b1 * gp) + (f0 * uv + f1 * up)
        nup = (b2 * gv + b3 * gp) + (f2 * uv + f3 * up)
        sv_ref[at, :] = nuv
        sp_ref[at, :] = nup
        y0 = f0 * x0 + f1 * x2
        y1 = f0 * x1 + f1 * x3
        y2 = f2 * x0 + f3 * x2
        y3 = f2 * x1 + f3 * x3
        xs_ref[0, pl.ds(k, 1), :] = y0
        xs_ref[1, pl.ds(k, 1), :] = y1
        xs_ref[2, pl.ds(k, 1), :] = y2
        xs_ref[3, pl.ds(k, 1), :] = y3
        return (nuv, nup, y0, y1, y2, y3)

    uv, up, _, _, _, _ = lax.fori_loop(
        0, levels, forward, (zero, zero, upper * one, flat, flat, upper * one), unroll=True
    )

    def backward(step, carry):
        sv, sp, c0, c1, c2, c3 = carry
        k = levels - 1 - step
        level = off + k
        m0 = bm_ref[0, level]
        m1 = bm_ref[1, level]
        m2 = bm_ref[2, level]
        m3 = bm_ref[3, level]
        at = pl.ds(pl.multiple_of(k * per, per), per)
        nsv = sv_ref[at, :] + (m0 * sv + m1 * sp)
        nsp = sp_ref[at, :] + (m2 * sv + m3 * sp)
        sv_ref[at, :] = nsv
        sp_ref[at, :] = nsp
        d0 = xs_ref[0, pl.ds(k, 1), :] + (m0 * c0 + m1 * c2)
        d1 = xs_ref[1, pl.ds(k, 1), :] + (m0 * c1 + m1 * c3)
        d2 = xs_ref[2, pl.ds(k, 1), :] + (m2 * c0 + m3 * c2)
        d3 = xs_ref[3, pl.ds(k, 1), :] + (m2 * c1 + m3 * c3)
        coef_ref[0, at, :] = jnp.broadcast_to(d0, (per, lanes))
        coef_ref[1, at, :] = jnp.broadcast_to(d1, (per, lanes))
        coef_ref[2, at, :] = jnp.broadcast_to(d2, (per, lanes))
        coef_ref[3, at, :] = jnp.broadcast_to(d3, (per, lanes))
        return (nsv, nsp, d0, d1, d2, d3)

    sv, sp, d0, d1, d2, d3 = lax.fori_loop(
        0, levels, backward, (zero, zero, lower * one, flat, flat, lower * one), unroll=True
    )
    msg_ref[0:per, :] = lower * uv + upper * sv
    msg_ref[per : 2 * per, :] = lower * up + upper * sp
    for index, value in enumerate((d0, d1, d2, d3)):
        msg_ref[2 * per + index : 2 * per + index + 1, :] = upper * value


def arrive_solve_kernel(
    off_ref, bi_ref, fm_ref, bm_ref, w_ref, e_ref, s_ref, n_ref, sat_ref, res_ref, vel_ref, pres_ref,
    out_ref, sv_ref, sp_ref, msg_ref, coef_ref, force_ref, xs_ref,
):
    arrivals_into((w_ref, e_ref, s_ref, n_ref), sat_ref, res_ref, vel_ref, out_ref, force_ref)
    solve_into(off_ref, bi_ref, fm_ref, bm_ref, force_ref, pres_ref, sv_ref, sp_ref, msg_ref, coef_ref, xs_ref)


def correct_kernel(coef_ref, own_ref, recv_ref, sv_ref, sp_ref, nv_ref, np_ref):
    rows, lanes = sv_ref.shape
    per = (own_ref.shape[0] - 4) // 2
    own0 = own_ref[0:per, :]
    own1 = own_ref[per : 2 * per, :]
    extra = [recv_ref[2 * per + i : 2 * per + i + 1, :] for i in range(4)]
    v0 = recv_ref[0:per, :] + extra[0] * own0 + extra[1] * own1
    v1 = recv_ref[per : 2 * per, :] + extra[2] * own0 + extra[3] * own1
    phase = lax.broadcasted_iota(jnp.int32, (rows, lanes), 0) % per
    t0 = jnp.zeros((rows, lanes), jnp.float32)
    t1 = jnp.zeros((rows, lanes), jnp.float32)
    for p in range(per):
        t0 = jnp.where(phase == p, v0[p : p + 1], t0)
        t1 = jnp.where(phase == p, v1[p : p + 1], t1)
    nv_ref[...] = sv_ref[...] + (coef_ref[0] * t0 + coef_ref[1] * t1)
    np_ref[...] = sp_ref[...] + (coef_ref[2] * t0 + coef_ref[3] * t1)


def settle_and_solve(faces_in, sat_view, heat_res, vel_view, pres_view, levels, block_inverse, forward_map, backward_map):
    assert lax.axis_size("gz") == 2
    packet_width, slot_count = faces_in[0].shape
    record_width = packet_width - 1
    rows, lanes = sat_view.shape
    per = rows // levels
    offset = jnp.full((1,), lax.axis_index("gz") * levels, jnp.int32)
    smem = pl.BlockSpec(memory_space=pltpu.SMEM)
    vmem = pl.BlockSpec(memory_space=pltpu.VMEM)
    arrived, sv, sp, message, coef = pl.pallas_call(
        arrive_solve_kernel,
        out_shape=(
            jax.ShapeDtypeStruct((len(faces_in), record_width, slot_count), jnp.float32),
            jax.ShapeDtypeStruct((rows, lanes), jnp.float32),
            jax.ShapeDtypeStruct((rows, lanes), jnp.float32),
            jax.ShapeDtypeStruct((2 * per + 4, lanes), jnp.float32),
            jax.ShapeDtypeStruct((4, rows, lanes), jnp.float32),
        ),
        in_specs=[smem] * 4 + [vmem] * (len(faces_in) + 4),
        out_specs=(vmem,) * 5,
        scratch_shapes=[
            pltpu.VMEM((rows, lanes), jnp.float32),
            pltpu.VMEM((4, levels, lanes), jnp.float32),
        ],
        cost_estimate=pl.CostEstimate(
            flops=8 * sat_view.size * len(faces_in) * slot_count + 40 * rows * lanes,
            bytes_accessed=4 * (2 * packet_width) * len(faces_in) * slot_count + 40 * rows * lanes,
            transcendentals=len(faces_in) * slot_count,
        ),
    )(offset, block_inverse, forward_map, backward_map, *faces_in, sat_view, heat_res, vel_view, pres_view)
    received = lax.ppermute(message, "gz", [(0, 1), (1, 0)])
    new_v, new_p = pl.pallas_call(
        correct_kernel,
        out_shape=(
            jax.ShapeDtypeStruct((rows, lanes), jnp.float32),
            jax.ShapeDtypeStruct((rows, lanes), jnp.float32),
        ),
        in_specs=[vmem] * 5,
        out_specs=(vmem, vmem),
        cost_estimate=pl.CostEstimate(
            flops=8 * rows * lanes, bytes_accessed=32 * rows * lanes, transcendentals=0
        ),
    )(coef, message, received, sv, sp)
    return arrived, new_v, new_p


def along_x(packet_face, offset):
    return shifted(packet_face, "gx", offset)


def along_y(packet_face, offset):
    return shifted(packet_face, "gy", offset)


def body(
    droplets,
    cell_index,
    crossing,
    crossing_count,
    saturation,
    velocity,
    pressure,
    block_inverse,
    forward_map,
    backward_map,
):
    records = droplets[0, 0, 0]
    cell_ids = cell_index[0, 0, 0]
    levels = saturation.shape[0]
    view = (saturation.size // 128, 128)
    sat_view = saturation.reshape(view)
    faces_out, staying_view = emit_faces(
        records, cell_index, crossing[0, 0, 0], crossing_count[0, 0, 0]
    )
    from_west = along_x(faces_out[0], 1)
    from_east = along_x(faces_out[1], -1)
    from_south = along_y(faces_out[2], 1)
    from_north = along_y(faces_out[3], -1)
    resident, heat_res = settle_residents(
        records,
        cell_index.reshape(1, -1),
        staying_view.reshape(1, -1),
        sat_view,
    )
    arrived, solved_v, solved_p = settle_and_solve(
        (from_west, from_east, from_south, from_north),
        sat_view,
        heat_res,
        velocity.reshape(view),
        pressure.reshape(view),
        levels,
        block_inverse,
        forward_map,
        backward_map,
    )
    new_velocity = solved_v.reshape(velocity.shape)
    new_pressure = solved_p.reshape(pressure.shape)
    return (resident[None, None, None], arrived[None, None, None], new_velocity, new_pressure)


def solution(mesh):
    return jax.shard_map(
        body,
        mesh=mesh,
        in_specs=(
            P("gz", "gx", "gy", None, None),
            P("gz", "gx", "gy", None),
            P("gz", "gx", "gy", None, None),
            P("gz", "gx", "gy", None),
            P("gz", "gx", "gy", None),
            P("gz", "gx", "gy", None),
            P("gz", "gx", "gy", None),
            P(),
            P(),
            P(),
        ),
        out_specs=(
            P("gz", "gx", "gy", None, None),
            P("gz", "gx", "gy", None, None, None),
            P("gz", "gx", "gy", None),
            P("gz", "gx", "gy", None),
        ),
        check_vma=False,
    )
```

```python
import math

import jax
import jax.numpy as jnp
from jax import lax
from jax.sharding import PartitionSpec as P
from jax.experimental import pallas as pl
from jax.experimental.pallas import tpu as pltpu

CX = 8
CY = 32


GROW = 0.4
CURVATURE = 0.05
FLOOR_SQ = 0.09
BUOYANCY = 0.5
EXACT = lax.Precision.HIGHEST


def shifted(value, axis, steps):
    count = lax.axis_size(axis)
    pairs = [(source, (source + steps) % count) for source in range(count)]
    return lax.ppermute(value, axis, pairs)


def one_hot_of(index, width, dtype):
    return (index[:, None] == lax.broadcasted_iota(jnp.int32, (1, width), 1)).astype(dtype)


def emit_packets(records, cell_ids, leavers, live_count, width_x, width_y):
    record_width, drop_count = records.shape
    slot_count = leavers.shape[1]
    slot_ids = lax.broadcasted_iota(jnp.int32, (4, slot_count), 1)
    face_ids = lax.broadcasted_iota(jnp.int32, (4, slot_count), 0)
    in_use = slot_ids < live_count[:, None]
    inner = min(128, drop_count)
    outer = drop_count // inner
    table = jnp.concatenate([records, cell_ids.astype(jnp.float32)[None, :]], axis=0).reshape(
        record_width + 1, outer, inner
    )
    flat_leavers = leavers.reshape(-1)
    flat_use = in_use.reshape(-1).astype(jnp.bfloat16)
    block_rows = 4 * slot_count

    def pick_block(inputs):
        ids_block, use_block = inputs
        upper = one_hot_of(ids_block // inner, outer, jnp.float32)
        lower = one_hot_of(ids_block % inner, inner, jnp.float32)
        rows = jnp.einsum(
            "nh,rhl->nrl", upper, table, precision=EXACT, preferred_element_type=jnp.float32
        )
        picked_block = jnp.sum(rows * lower[:, None, :], axis=2)
        upper_used = upper.astype(jnp.bfloat16) * use_block[:, None]
        counts = jnp.einsum(
            "nh,nl->hl", upper_used, lower.astype(jnp.bfloat16), preferred_element_type=jnp.float32
        )
        return (picked_block, counts)

    picked_blocks, count_blocks = lax.map(
        pick_block, (flat_leavers.reshape(-1, block_rows), flat_use.reshape(-1, block_rows))
    )
    picked_all = picked_blocks.reshape(4, slot_count, record_width + 1)
    departed = jnp.sum(count_blocks, axis=0).reshape(-1)
    picked = jnp.moveaxis(picked_all[:, :, :record_width], 2, 1)
    source = (picked_all[:, :, record_width] + 0.5).astype(jnp.int32)
    height = source // (width_x * width_y)
    cell_x = source // width_y % width_x
    cell_y = source % width_y
    new_x = jnp.where(face_ids == 0, 0, jnp.where(face_ids == 1, width_x - 1, cell_x))
    new_y = jnp.where(face_ids == 2, 0, jnp.where(face_ids == 3, width_y - 1, cell_y))
    target = height * (width_x * width_y) + new_x * width_y + new_y
    packet = jnp.concatenate([picked, target.astype(records.dtype)[:, None, :]], axis=1)
    packet = jnp.where(in_use[:, None, :], packet, 0.0)
    return (packet, departed == 0.0)


def emit_kernel(count_ref, view_ref, cells_ref, cross_ref, *outs):
    face_refs = outs[:-1]
    stay_ref = outs[-1]
    view_rows, lanes = view_ref.shape
    outer = cells_ref.shape[0]
    record_width = view_rows // outer
    slot_count = cross_ref.shape[1]
    shift = lanes.bit_length() - 1
    rec_stack = jnp.concatenate(split_pieces3(view_ref[...]), axis=1)
    cell_stack = jnp.concatenate(split_pieces3(cells_ref[...].astype(jnp.float32)), axis=1)
    faces = len(face_refs)
    width = faces * slot_count
    index = jnp.concatenate([cross_ref[face : face + 1, :] for face in range(faces)], axis=1)
    face_of = lax.broadcasted_iota(jnp.int32, (1, width), 1) // slot_count
    slot_of = lax.broadcasted_iota(jnp.int32, (1, width), 1) % slot_count
    limit = jnp.zeros((1, width), jnp.int32)
    for face in range(faces):
        limit = jnp.where(face_of == face, count_ref[face], limit)
    in_use = slot_of < limit
    high = lax.shift_right_logical(index, shift)
    low = jnp.bitwise_and(index, lanes - 1)
    lane_hot = jnp.where(
        lax.broadcasted_iota(jnp.int32, (lanes, width), 0).astype(jnp.bfloat16)
        == low.astype(jnp.bfloat16),
        jnp.bfloat16(1.0),
        jnp.bfloat16(0.0),
    )
    high_mask = lax.broadcasted_iota(jnp.int32, (outer, width), 0) == high
    lane_hot3 = jnp.concatenate([lane_hot, lane_hot, lane_hot], axis=0)
    got = jnp.dot(rec_stack, lane_hot3, preferred_element_type=jnp.float32)
    got = got.reshape(outer, record_width, width)
    picked = jnp.sum(jnp.where(high_mask[:, None, :], got, 0.0), axis=0)
    got_cell = jnp.dot(cell_stack, lane_hot3, preferred_element_type=jnp.float32)
    source = (jnp.sum(jnp.where(high_mask, got_cell, 0.0), axis=0, keepdims=True) + 0.5).astype(jnp.int32)
    height = lax.shift_right_logical(source, (CX * CY).bit_length() - 1)
    cell_x = jnp.bitwise_and(lax.shift_right_logical(source, CY.bit_length() - 1), CX - 1)
    cell_y = jnp.bitwise_and(source, CY - 1)
    new_x = jnp.where(face_of == 0, 0, jnp.where(face_of == 1, CX - 1, cell_x))
    new_y = jnp.where(face_of == 2, 0, jnp.where(face_of == 3, CY - 1, cell_y))
    target = (height * (CX * CY) + new_x * CY + new_y).astype(jnp.float32)
    packet = jnp.where(in_use, jnp.concatenate([picked, target], axis=0), 0.0)
    for face, out_ref in enumerate(face_refs):
        out_ref[...] = packet[:, face * slot_count : (face + 1) * slot_count]
    used_high = jnp.where(high_mask & in_use, 1.0, 0.0).astype(jnp.bfloat16)
    counted = lax.dot_general(
        used_high, lane_hot, (((1,), (1,)), ((), ())), preferred_element_type=jnp.float32
    )
    stay_ref[...] = jnp.where(counted == 0.0, 1.0, 0.0)


def emit_faces(records, cell_index, crossing, crossing_count):
    record_width, drop_count = records.shape
    lanes = 128
    outer = drop_count // lanes
    faces, slot_count = crossing.shape
    view = records.reshape(record_width, outer, lanes).transpose(1, 0, 2).reshape(outer * record_width, lanes)
    smem = pl.BlockSpec(memory_space=pltpu.SMEM)
    vmem = pl.BlockSpec(memory_space=pltpu.VMEM)
    results = pl.pallas_call(
        emit_kernel,
        out_shape=tuple(
            jax.ShapeDtypeStruct((record_width + 1, slot_count), jnp.float32) for _ in range(faces)
        )
        + (jax.ShapeDtypeStruct((outer, lanes), jnp.float32),),
        in_specs=[smem, vmem, vmem, vmem],
        out_specs=(vmem,) * (faces + 1),
        cost_estimate=pl.CostEstimate(
            flops=6 * (record_width + 1) * drop_count * faces * slot_count // outer,
            bytes_accessed=4 * (record_width + 1) * drop_count + 8 * (record_width + 1) * faces * slot_count,
            transcendentals=0,
        ),
    )(crossing_count, view, cell_index.reshape(outer, lanes), crossing)
    return results[:faces], results[faces]


def split_pieces3(value):
    high = value.astype(jnp.bfloat16)
    rest = value - high.astype(jnp.float32)
    middle = rest.astype(jnp.bfloat16)
    low = (rest - middle.astype(jnp.float32)).astype(jnp.bfloat16)
    return (high, middle, low)


def split_pieces(value):
    high = value.astype(jnp.bfloat16)
    low = (value - high.astype(jnp.float32)).astype(jnp.bfloat16)
    return (high, low)


def stacked_pieces(value):
    return jnp.concatenate(split_pieces(value), axis=1)


def condense_chunk(records, cells, occupied, sat_stack):
    rows = sat_stack.shape[0]
    lanes = sat_stack.shape[1] // 2
    width = cells.shape[1]
    shift = lanes.bit_length() - 1
    row_of = lax.shift_right_logical(cells, shift)
    lane_of = jnp.bitwise_and(cells, lanes - 1)
    lane_mask = lax.broadcasted_iota(jnp.int32, (lanes, width), 0).astype(jnp.bfloat16) == lane_of.astype(jnp.bfloat16)
    lane_hot = jnp.where(lane_mask, jnp.bfloat16(1.0), jnp.bfloat16(0.0))
    row_mask = lax.broadcasted_iota(jnp.int32, (rows, width), 0) == row_of
    row_hot = jnp.where(lax.broadcasted_iota(jnp.int32, (rows, width), 0).astype(jnp.bfloat16) == row_of.astype(jnp.bfloat16), jnp.bfloat16(1.0), jnp.bfloat16(0.0))
    picked = jnp.dot(sat_stack, jnp.concatenate([lane_hot, lane_hot], axis=0), preferred_element_type=jnp.float32)
    excess = jnp.sum(jnp.where(row_mask, picked, 0.0), axis=0, keepdims=True)
    radius = jnp.where(occupied, records[0:1], 1.0)
    dry_radius = records[2:3]
    solute = records[3:4]
    radius_cubed = radius * radius * radius
    squared = jnp.maximum(
        radius * radius
        + GROW
        * (
            excess
            - CURVATURE / radius
            + solute * dry_radius * dry_radius * dry_radius / radius_cubed
        ),
        FLOOR_SQ,
    )
    grown = jnp.sqrt(squared)
    condensed = jnp.where(occupied, records[1:2] * (grown * grown * grown - radius_cubed), 0.0)
    spread = jnp.concatenate([row_hot * piece for piece in split_pieces(condensed)], axis=0)
    heat = lax.dot_general(
        spread, lane_hot, (((1,), (1,)), ((), ())), preferred_element_type=jnp.float32
    )
    heat = heat[:rows] + heat[rows:]
    updated = jnp.concatenate([grown, records[1:]], axis=0)
    updated = jnp.where(occupied, updated, 0.0)
    return (updated, heat)


def resident_kernel(rec_ref, cell_ref, stay_ref, sat_ref, out_ref, heat_ref):
    step = pl.program_id(0)
    updated, heat = condense_chunk(
        rec_ref[...], cell_ref[...], stay_ref[...] > 0.0, stacked_pieces(sat_ref[...])
    )
    out_ref[...] = updated

    @pl.when(step == 0)
    def _():
        heat_ref[...] = heat

    @pl.when(step > 0)
    def _():
        heat_ref[...] += heat


def settle_residents(records, cell_row, staying_row, sat_view):
    record_width, drop_count = records.shape
    rows, lanes = sat_view.shape
    chunk = min(8192, drop_count)
    whole = lambda j: (0, 0)
    by_chunk = lambda j: (0, j)
    return pl.pallas_call(
        resident_kernel,
        grid=(drop_count // chunk,),
        out_shape=(
            jax.ShapeDtypeStruct((record_width, drop_count), jnp.float32),
            jax.ShapeDtypeStruct((rows, lanes), jnp.float32),
        ),
        in_specs=[
            pl.BlockSpec((record_width, chunk), by_chunk),
            pl.BlockSpec((1, chunk), by_chunk),
            pl.BlockSpec((1, chunk), by_chunk),
            pl.BlockSpec((rows, lanes), whole),
        ],
        out_specs=(
            pl.BlockSpec((record_width, chunk), by_chunk),
            pl.BlockSpec((rows, lanes), whole),
        ),
        cost_estimate=pl.CostEstimate(
            flops=12 * rows * lanes * drop_count,
            bytes_accessed=4 * (2 * record_width + 2) * drop_count,
            transcendentals=drop_count,
        ),
    )(records, cell_row, staying_row, sat_view)


def arrivals_into(faces, sat_ref, res_ref, vel_ref, out_ref, force_ref):
    record_width = out_ref.shape[1]
    slot_count = out_ref.shape[2]
    sat_stack = stacked_pieces(sat_ref[...])
    packet = jnp.concatenate([in_ref[...] for in_ref in faces], axis=1)
    records = packet[:record_width]
    cells = (packet[record_width : record_width + 1] + 0.5).astype(jnp.int32)
    occupied = records[1:2] > 0.0
    updated, heat = condense_chunk(records, cells, occupied, sat_stack)
    for face in range(len(faces)):
        out_ref[face] = updated[:, face * slot_count : (face + 1) * slot_count]
    force_ref[...] = vel_ref[...] + BUOYANCY * (res_ref[...] + heat)


def solve_into(off_ref, bi_ref, fm_ref, bm_ref, fv_ref, fp_ref, sv_ref, sp_ref, msg_ref, coef_ref, xs_ref):
    rows, lanes = fv_ref.shape
    levels = xs_ref.shape[1]
    per = rows // levels
    off = off_ref[0]
    upper = jnp.where(off > 0, 1.0, 0.0).astype(jnp.float32)
    lower = 1.0 - upper
    zero = jnp.zeros((per, lanes), jnp.float32)
    one = jnp.ones((1, lanes), jnp.float32)
    flat = jnp.zeros((1, lanes), jnp.float32)

    def forward(k, carry):
        uv, up, x0, x1, x2, x3 = carry
        level = off + k
        b0 = bi_ref[0, level]
        b1 = bi_ref[1, level]
        b2 = bi_ref[2, level]
        b3 = bi_ref[3, level]
        f0 = fm_ref[0, level]
        f1 = fm_ref[1, level]
        f2 = fm_ref[2, level]
        f3 = fm_ref[3, level]
        at = pl.ds(pl.multiple_of(k * per, per), per)
        gv = fv_ref[at, :]
        gp = fp_ref[at, :]
        nuv = (b0 * gv + b1 * gp) + (f0 * uv + f1 * up)
        nup = (b2 * gv + b3 * gp) + (f2 * uv + f3 * up)
        sv_ref[at, :] = nuv
        sp_ref[at, :] = nup
        y0 = f0 * x0 + f1 * x2
        y1 = f0 * x1 + f1 * x3
        y2 = f2 * x0 + f3 * x2
        y3 = f2 * x1 + f3 * x3
        xs_ref[0, pl.ds(k, 1), :] = y0
        xs_ref[1, pl.ds(k, 1), :] = y1
        xs_ref[2, pl.ds(k, 1), :] = y2
        xs_ref[3, pl.ds(k, 1), :] = y3
        return (nuv, nup, y0, y1, y2, y3)

    uv, up, _, _, _, _ = lax.fori_loop(
        0, levels, forward, (zero, zero, upper * one, flat, flat, upper * one), unroll=True
    )

    def backward(step, carry):
        sv, sp, c0, c1, c2, c3 = carry
        k = levels - 1 - step
        level = off + k
        m0 = bm_ref[0, level]
        m1 = bm_ref[1, level]
        m2 = bm_ref[2, level]
        m3 = bm_ref[3, level]
        at = pl.ds(pl.multiple_of(k * per, per), per)
        nsv = sv_ref[at, :] + (m0 * sv + m1 * sp)
        nsp = sp_ref[at, :] + (m2 * sv + m3 * sp)
        sv_ref[at, :] = nsv
        sp_ref[at, :] = nsp
        d0 = xs_ref[0, pl.ds(k, 1), :] + (m0 * c0 + m1 * c2)
        d1 = xs_ref[1, pl.ds(k, 1), :] + (m0 * c1 + m1 * c3)
        d2 = xs_ref[2, pl.ds(k, 1), :] + (m2 * c0 + m3 * c2)
        d3 = xs_ref[3, pl.ds(k, 1), :] + (m2 * c1 + m3 * c3)
        coef_ref[0, at, :] = jnp.broadcast_to(d0, (per, lanes))
        coef_ref[1, at, :] = jnp.broadcast_to(d1, (per, lanes))
        coef_ref[2, at, :] = jnp.broadcast_to(d2, (per, lanes))
        coef_ref[3, at, :] = jnp.broadcast_to(d3, (per, lanes))
        return (nsv, nsp, d0, d1, d2, d3)

    sv, sp, d0, d1, d2, d3 = lax.fori_loop(
        0, levels, backward, (zero, zero, lower * one, flat, flat, lower * one), unroll=True
    )
    msg_ref[0:per, :] = lower * uv + upper * sv
    msg_ref[per : 2 * per, :] = lower * up + upper * sp
    for index, value in enumerate((d0, d1, d2, d3)):
        msg_ref[2 * per + index : 2 * per + index + 1, :] = upper * value


def arrive_solve_kernel(
    off_ref, bi_ref, fm_ref, bm_ref, w_ref, e_ref, s_ref, n_ref, sat_ref, res_ref, vel_ref, pres_ref,
    out_ref, sv_ref, sp_ref, msg_ref, coef_ref, force_ref, xs_ref,
):
    arrivals_into((w_ref, e_ref, s_ref, n_ref), sat_ref, res_ref, vel_ref, out_ref, force_ref)
    solve_into(off_ref, bi_ref, fm_ref, bm_ref, force_ref, pres_ref, sv_ref, sp_ref, msg_ref, coef_ref, xs_ref)


def correct_kernel(coef_ref, own_ref, recv_ref, sv_ref, sp_ref, nv_ref, np_ref):
    rows, lanes = sv_ref.shape
    per = (own_ref.shape[0] - 4) // 2
    own0 = own_ref[0:per, :]
    own1 = own_ref[per : 2 * per, :]
    extra = [recv_ref[2 * per + i : 2 * per + i + 1, :] for i in range(4)]
    v0 = recv_ref[0:per, :] + extra[0] * own0 + extra[1] * own1
    v1 = recv_ref[per : 2 * per, :] + extra[2] * own0 + extra[3] * own1
    phase = lax.broadcasted_iota(jnp.int32, (rows, lanes), 0) % per
    t0 = jnp.zeros((rows, lanes), jnp.float32)
    t1 = jnp.zeros((rows, lanes), jnp.float32)
    for p in range(per):
        t0 = jnp.where(phase == p, v0[p : p + 1], t0)
        t1 = jnp.where(phase == p, v1[p : p + 1], t1)
    nv_ref[...] = sv_ref[...] + (coef_ref[0] * t0 + coef_ref[1] * t1)
    np_ref[...] = sp_ref[...] + (coef_ref[2] * t0 + coef_ref[3] * t1)


def settle_and_solve(faces_in, sat_view, heat_res, vel_view, pres_view, levels, block_inverse, forward_map, backward_map):
    assert lax.axis_size("gz") == 2
    packet_width, slot_count = faces_in[0].shape
    record_width = packet_width - 1
    rows, lanes = sat_view.shape
    per = rows // levels
    offset = jnp.full((1,), lax.axis_index("gz") * levels, jnp.int32)
    smem = pl.BlockSpec(memory_space=pltpu.SMEM)
    vmem = pl.BlockSpec(memory_space=pltpu.VMEM)
    arrived, sv, sp, message, coef = pl.pallas_call(
        arrive_solve_kernel,
        out_shape=(
            jax.ShapeDtypeStruct((len(faces_in), record_width, slot_count), jnp.float32),
            jax.ShapeDtypeStruct((rows, lanes), jnp.float32),
            jax.ShapeDtypeStruct((rows, lanes), jnp.float32),
            jax.ShapeDtypeStruct((2 * per + 4, lanes), jnp.float32),
            jax.ShapeDtypeStruct((4, rows, lanes), jnp.float32),
        ),
        in_specs=[smem] * 4 + [vmem] * (len(faces_in) + 4),
        out_specs=(vmem,) * 5,
        scratch_shapes=[
            pltpu.VMEM((rows, lanes), jnp.float32),
            pltpu.VMEM((4, levels, lanes), jnp.float32),
        ],
        cost_estimate=pl.CostEstimate(
            flops=8 * sat_view.size * len(faces_in) * slot_count + 40 * rows * lanes,
            bytes_accessed=4 * (2 * packet_width) * len(faces_in) * slot_count + 40 * rows * lanes,
            transcendentals=len(faces_in) * slot_count,
        ),
    )(offset, block_inverse, forward_map, backward_map, *faces_in, sat_view, heat_res, vel_view, pres_view)
    received = lax.ppermute(message, "gz", [(0, 1), (1, 0)])
    new_v, new_p = pl.pallas_call(
        correct_kernel,
        out_shape=(
            jax.ShapeDtypeStruct((rows, lanes), jnp.float32),
            jax.ShapeDtypeStruct((rows, lanes), jnp.float32),
        ),
        in_specs=[vmem] * 5,
        out_specs=(vmem, vmem),
        cost_estimate=pl.CostEstimate(
            flops=8 * rows * lanes, bytes_accessed=32 * rows * lanes, transcendentals=0
        ),
    )(coef, message, received, sv, sp)
    return arrived, new_v, new_p


def along_x(packet_face, offset):
    return shifted(packet_face, "gx", offset)


def along_y(packet_face, offset):
    return shifted(packet_face, "gy", offset)


def body(
    droplets,
    cell_index,
    crossing,
    crossing_count,
    saturation,
    velocity,
    pressure,
    block_inverse,
    forward_map,
    backward_map,
):
    records = droplets[0, 0, 0]
    cell_ids = cell_index[0, 0, 0]
    levels = saturation.shape[0]
    view = (saturation.size // 128, 128)
    sat_view = saturation.reshape(view)
    faces_out, staying_view = emit_faces(
        records, cell_index, crossing[0, 0, 0], crossing_count[0, 0, 0]
    )
    from_west = along_x(faces_out[0], 1)
    from_east = along_x(faces_out[1], -1)
    from_south = along_y(faces_out[2], 1)
    from_north = along_y(faces_out[3], -1)
    resident, heat_res = settle_residents(
        records,
        cell_index.reshape(1, -1),
        staying_view.reshape(1, -1),
        sat_view,
    )
    arrived, solved_v, solved_p = settle_and_solve(
        (from_west, from_east, from_south, from_north),
        sat_view,
        heat_res,
        velocity.reshape(view),
        pressure.reshape(view),
        levels,
        block_inverse,
        forward_map,
        backward_map,
    )
    new_velocity = solved_v.reshape(velocity.shape)
    new_pressure = solved_p.reshape(pressure.shape)
    return (resident[None, None, None], arrived[None, None, None], new_velocity, new_pressure)


def solution(mesh):
    return jax.shard_map(
        body,
        mesh=mesh,
        in_specs=(
            P("gz", "gx", "gy", None, None),
            P("gz", "gx", "gy", None),
            P("gz", "gx", "gy", None, None),
            P("gz", "gx", "gy", None),
            P("gz", "gx", "gy", None),
            P("gz", "gx", "gy", None),
            P("gz", "gx", "gy", None),
            P(),
            P(),
            P(),
        ),
        out_specs=(
            P("gz", "gx", "gy", None, None),
            P("gz", "gx", "gy", None, None, None),
            P("gz", "gx", "gy", None),
            P("gz", "gx", "gy", None),
        ),
        check_vma=False,
    )
```

```python
import math

import jax
import jax.numpy as jnp
from jax import lax
from jax.sharding import PartitionSpec as P
from jax.experimental import pallas as pl
from jax.experimental.pallas import tpu as pltpu

CX = 8
CY = 32


GROW = 0.4
CURVATURE = 0.05
FLOOR_SQ = 0.09
BUOYANCY = 0.5
EXACT = lax.Precision.HIGHEST


def shifted(value, axis, steps):
    count = lax.axis_size(axis)
    pairs = [(source, (source + steps) % count) for source in range(count)]
    return lax.ppermute(value, axis, pairs)


def one_hot_of(index, width, dtype):
    return (index[:, None] == lax.broadcasted_iota(jnp.int32, (1, width), 1)).astype(dtype)


def emit_packets(records, cell_ids, leavers, live_count, width_x, width_y):
    record_width, drop_count = records.shape
    slot_count = leavers.shape[1]
    slot_ids = lax.broadcasted_iota(jnp.int32, (4, slot_count), 1)
    face_ids = lax.broadcasted_iota(jnp.int32, (4, slot_count), 0)
    in_use = slot_ids < live_count[:, None]
    inner = min(128, drop_count)
    outer = drop_count // inner
    table = jnp.concatenate([records, cell_ids.astype(jnp.float32)[None, :]], axis=0).reshape(
        record_width + 1, outer, inner
    )
    flat_leavers = leavers.reshape(-1)
    flat_use = in_use.reshape(-1).astype(jnp.bfloat16)
    block_rows = 4 * slot_count

    def pick_block(inputs):
        ids_block, use_block = inputs
        upper = one_hot_of(ids_block // inner, outer, jnp.float32)
        lower = one_hot_of(ids_block % inner, inner, jnp.float32)
        rows = jnp.einsum(
            "nh,rhl->nrl", upper, table, precision=EXACT, preferred_element_type=jnp.float32
        )
        picked_block = jnp.sum(rows * lower[:, None, :], axis=2)
        upper_used = upper.astype(jnp.bfloat16) * use_block[:, None]
        counts = jnp.einsum(
            "nh,nl->hl", upper_used, lower.astype(jnp.bfloat16), preferred_element_type=jnp.float32
        )
        return (picked_block, counts)

    picked_blocks, count_blocks = lax.map(
        pick_block, (flat_leavers.reshape(-1, block_rows), flat_use.reshape(-1, block_rows))
    )
    picked_all = picked_blocks.reshape(4, slot_count, record_width + 1)
    departed = jnp.sum(count_blocks, axis=0).reshape(-1)
    picked = jnp.moveaxis(picked_all[:, :, :record_width], 2, 1)
    source = (picked_all[:, :, record_width] + 0.5).astype(jnp.int32)
    height = source // (width_x * width_y)
    cell_x = source // width_y % width_x
    cell_y = source % width_y
    new_x = jnp.where(face_ids == 0, 0, jnp.where(face_ids == 1, width_x - 1, cell_x))
    new_y = jnp.where(face_ids == 2, 0, jnp.where(face_ids == 3, width_y - 1, cell_y))
    target = height * (width_x * width_y) + new_x * width_y + new_y
    packet = jnp.concatenate([picked, target.astype(records.dtype)[:, None, :]], axis=1)
    packet = jnp.where(in_use[:, None, :], packet, 0.0)
    return (packet, departed == 0.0)


def emit_kernel(count_ref, view_ref, cells_ref, cross_ref, *outs):
    face_refs = outs[:-1]
    stay_ref = outs[-1]
    view_rows, lanes = view_ref.shape
    outer = cells_ref.shape[0]
    record_width = view_rows // outer
    slot_count = cross_ref.shape[1]
    shift = lanes.bit_length() - 1
    rec_stack = jnp.concatenate(split_pieces3(view_ref[...]), axis=1)
    cell_stack = jnp.concatenate(split_pieces(cells_ref[...].astype(jnp.float32)), axis=1)
    faces = len(face_refs)
    width = faces * slot_count
    index = jnp.concatenate([cross_ref[face : face + 1, :] for face in range(faces)], axis=1)
    face_of = lax.broadcasted_iota(jnp.int32, (1, width), 1) // slot_count
    slot_of = lax.broadcasted_iota(jnp.int32, (1, width), 1) % slot_count
    limit = jnp.zeros((1, width), jnp.int32)
    for face in range(faces):
        limit = jnp.where(face_of == face, count_ref[face], limit)
    in_use = slot_of < limit
    high = lax.shift_right_logical(index, shift)
    low = jnp.bitwise_and(index, lanes - 1)
    lane_hot = jnp.where(
        lax.broadcasted_iota(jnp.int32, (lanes, width), 0).astype(jnp.bfloat16)
        == low.astype(jnp.bfloat16),
        jnp.bfloat16(1.0),
        jnp.bfloat16(0.0),
    )
    high_mask = lax.broadcasted_iota(jnp.int32, (outer, width), 0) == high
    lane_hot3 = jnp.concatenate([lane_hot, lane_hot, lane_hot], axis=0)
    got = jnp.dot(rec_stack, lane_hot3, preferred_element_type=jnp.float32)
    got = got.reshape(outer, record_width, width)
    picked = jnp.sum(jnp.where(high_mask[:, None, :], got, 0.0), axis=0)
    got_cell = jnp.dot(
        cell_stack, jnp.concatenate([lane_hot, lane_hot], axis=0), preferred_element_type=jnp.float32
    )
    source = (jnp.sum(jnp.where(high_mask, got_cell, 0.0), axis=0, keepdims=True) + 0.5).astype(jnp.int32)
    height = lax.shift_right_logical(source, (CX * CY).bit_length() - 1)
    cell_x = jnp.bitwise_and(lax.shift_right_logical(source, CY.bit_length() - 1), CX - 1)
    cell_y = jnp.bitwise_and(source, CY - 1)
    new_x = jnp.where(face_of == 0, 0, jnp.where(face_of == 1, CX - 1, cell_x))
    new_y = jnp.where(face_of == 2, 0, jnp.where(face_of == 3, CY - 1, cell_y))
    target = (height * (CX * CY) + new_x * CY + new_y).astype(jnp.float32)
    packet = jnp.where(in_use, jnp.concatenate([picked, target], axis=0), 0.0)
    for face, out_ref in enumerate(face_refs):
        out_ref[...] = packet[:, face * slot_count : (face + 1) * slot_count]
    used_high = jnp.where(high_mask & in_use, 1.0, 0.0).astype(jnp.bfloat16)
    counted = lax.dot_general(
        used_high, lane_hot, (((1,), (1,)), ((), ())), preferred_element_type=jnp.float32
    )
    stay_ref[...] = jnp.where(counted == 0.0, 1.0, 0.0)


def emit_faces(records, cell_index, crossing, crossing_count):
    record_width, drop_count = records.shape
    lanes = 128
    outer = drop_count // lanes
    faces, slot_count = crossing.shape
    view = records.reshape(record_width, outer, lanes).transpose(1, 0, 2).reshape(outer * record_width, lanes)
    smem = pl.BlockSpec(memory_space=pltpu.SMEM)
    vmem = pl.BlockSpec(memory_space=pltpu.VMEM)
    results = pl.pallas_call(
        emit_kernel,
        out_shape=tuple(
            jax.ShapeDtypeStruct((record_width + 1, slot_count), jnp.float32) for _ in range(faces)
        )
        + (jax.ShapeDtypeStruct((outer, lanes), jnp.float32),),
        in_specs=[smem, vmem, vmem, vmem],
        out_specs=(vmem,) * (faces + 1),
        cost_estimate=pl.CostEstimate(
            flops=6 * (record_width + 1) * drop_count * faces * slot_count // outer,
            bytes_accessed=4 * (record_width + 1) * drop_count + 8 * (record_width + 1) * faces * slot_count,
            transcendentals=0,
        ),
    )(crossing_count, view, cell_index.reshape(outer, lanes), crossing)
    return results[:faces], results[faces]


def split_pieces3(value):
    high = value.astype(jnp.bfloat16)
    rest = value - high.astype(jnp.float32)
    middle = rest.astype(jnp.bfloat16)
    low = (rest - middle.astype(jnp.float32)).astype(jnp.bfloat16)
    return (high, middle, low)


def split_pieces(value):
    high = value.astype(jnp.bfloat16)
    low = (value - high.astype(jnp.float32)).astype(jnp.bfloat16)
    return (high, low)


def stacked_pieces(value):
    return jnp.concatenate(split_pieces(value), axis=1)


def condense_chunk(records, cells, occupied, sat_stack):
    rows = sat_stack.shape[0]
    lanes = sat_stack.shape[1] // 2
    width = cells.shape[1]
    shift = lanes.bit_length() - 1
    row_of = lax.shift_right_logical(cells, shift)
    lane_of = jnp.bitwise_and(cells, lanes - 1)
    lane_mask = lax.broadcasted_iota(jnp.int32, (lanes, width), 0).astype(jnp.bfloat16) == lane_of.astype(jnp.bfloat16)
    lane_hot = jnp.where(lane_mask, jnp.bfloat16(1.0), jnp.bfloat16(0.0))
    row_mask = lax.broadcasted_iota(jnp.int32, (rows, width), 0) == row_of
    row_hot = jnp.where(lax.broadcasted_iota(jnp.int32, (rows, width), 0).astype(jnp.bfloat16) == row_of.astype(jnp.bfloat16), jnp.bfloat16(1.0), jnp.bfloat16(0.0))
    picked = jnp.dot(sat_stack, jnp.concatenate([lane_hot, lane_hot], axis=0), preferred_element_type=jnp.float32)
    excess = jnp.sum(jnp.where(row_mask, picked, 0.0), axis=0, keepdims=True)
    radius = jnp.where(occupied, records[0:1], 1.0)
    dry_radius = records[2:3]
    solute = records[3:4]
    radius_cubed = radius * radius * radius
    squared = jnp.maximum(
        radius * radius
        + GROW
        * (
            excess
            - CURVATURE / radius
            + solute * dry_radius * dry_radius * dry_radius / radius_cubed
        ),
        FLOOR_SQ,
    )
    grown = jnp.sqrt(squared)
    condensed = jnp.where(occupied, records[1:2] * (grown * grown * grown - radius_cubed), 0.0)
    spread = jnp.concatenate([row_hot * piece for piece in split_pieces(condensed)], axis=0)
    heat = lax.dot_general(
        spread, lane_hot, (((1,), (1,)), ((), ())), preferred_element_type=jnp.float32
    )
    heat = heat[:rows] + heat[rows:]
    updated = jnp.concatenate([grown, records[1:]], axis=0)
    updated = jnp.where(occupied, updated, 0.0)
    return (updated, heat)


def resident_kernel(rec_ref, cell_ref, stay_ref, sat_ref, out_ref, heat_ref):
    step = pl.program_id(0)
    updated, heat = condense_chunk(
        rec_ref[...], cell_ref[...], stay_ref[...] > 0.0, stacked_pieces(sat_ref[...])
    )
    out_ref[...] = updated

    @pl.when(step == 0)
    def _():
        heat_ref[...] = heat

    @pl.when(step > 0)
    def _():
        heat_ref[...] += heat


def settle_residents(records, cell_row, staying_row, sat_view):
    record_width, drop_count = records.shape
    rows, lanes = sat_view.shape
    chunk = min(8192, drop_count)
    whole = lambda j: (0, 0)
    by_chunk = lambda j: (0, j)
    return pl.pallas_call(
        resident_kernel,
        grid=(drop_count // chunk,),
        out_shape=(
            jax.ShapeDtypeStruct((record_width, drop_count), jnp.float32),
            jax.ShapeDtypeStruct((rows, lanes), jnp.float32),
        ),
        in_specs=[
            pl.BlockSpec((record_width, chunk), by_chunk),
            pl.BlockSpec((1, chunk), by_chunk),
            pl.BlockSpec((1, chunk), by_chunk),
            pl.BlockSpec((rows, lanes), whole),
        ],
        out_specs=(
            pl.BlockSpec((record_width, chunk), by_chunk),
            pl.BlockSpec((rows, lanes), whole),
        ),
        cost_estimate=pl.CostEstimate(
            flops=12 * rows * lanes * drop_count,
            bytes_accessed=4 * (2 * record_width + 2) * drop_count,
            transcendentals=drop_count,
        ),
    )(records, cell_row, staying_row, sat_view)


def arrivals_into(faces, sat_ref, res_ref, vel_ref, out_ref, force_ref):
    record_width = out_ref.shape[1]
    slot_count = out_ref.shape[2]
    sat_stack = stacked_pieces(sat_ref[...])
    packet = jnp.concatenate([in_ref[...] for in_ref in faces], axis=1)
    records = packet[:record_width]
    cells = (packet[record_width : record_width + 1] + 0.5).astype(jnp.int32)
    occupied = records[1:2] > 0.0
    updated, heat = condense_chunk(records, cells, occupied, sat_stack)
    for face in range(len(faces)):
        out_ref[face] = updated[:, face * slot_count : (face + 1) * slot_count]
    force_ref[...] = vel_ref[...] + BUOYANCY * (res_ref[...] + heat)


def solve_into(off_ref, bi_ref, fm_ref, bm_ref, fv_ref, fp_ref, sv_ref, sp_ref, msg_ref, coef_ref, xs_ref):
    rows, lanes = fv_ref.shape
    levels = xs_ref.shape[1]
    per = rows // levels
    off = off_ref[0]
    upper = jnp.where(off > 0, 1.0, 0.0).astype(jnp.float32)
    lower = 1.0 - upper
    zero = jnp.zeros((per, lanes), jnp.float32)
    one = jnp.ones((1, lanes), jnp.float32)
    flat = jnp.zeros((1, lanes), jnp.float32)

    def forward(k, carry):
        uv, up, x0, x1, x2, x3 = carry
        level = off + k
        b0 = bi_ref[0, level]
        b1 = bi_ref[1, level]
        b2 = bi_ref[2, level]
        b3 = bi_ref[3, level]
        f0 = fm_ref[0, level]
        f1 = fm_ref[1, level]
        f2 = fm_ref[2, level]
        f3 = fm_ref[3, level]
        at = pl.ds(pl.multiple_of(k * per, per), per)
        gv = fv_ref[at, :]
        gp = fp_ref[at, :]
        nuv = (b0 * gv + b1 * gp) + (f0 * uv + f1 * up)
        nup = (b2 * gv + b3 * gp) + (f2 * uv + f3 * up)
        sv_ref[at, :] = nuv
        sp_ref[at, :] = nup
        y0 = f0 * x0 + f1 * x2
        y1 = f0 * x1 + f1 * x3
        y2 = f2 * x0 + f3 * x2
        y3 = f2 * x1 + f3 * x3
        xs_ref[0, pl.ds(k, 1), :] = y0
        xs_ref[1, pl.ds(k, 1), :] = y1
        xs_ref[2, pl.ds(k, 1), :] = y2
        xs_ref[3, pl.ds(k, 1), :] = y3
        return (nuv, nup, y0, y1, y2, y3)

    uv, up, _, _, _, _ = lax.fori_loop(
        0, levels, forward, (zero, zero, upper * one, flat, flat, upper * one), unroll=True
    )

    def backward(step, carry):
        sv, sp, c0, c1, c2, c3 = carry
        k = levels - 1 - step
        level = off + k
        m0 = bm_ref[0, level]
        m1 = bm_ref[1, level]
        m2 = bm_ref[2, level]
        m3 = bm_ref[3, level]
        at = pl.ds(pl.multiple_of(k * per, per), per)
        nsv = sv_ref[at, :] + (m0 * sv + m1 * sp)
        nsp = sp_ref[at, :] + (m2 * sv + m3 * sp)
        sv_ref[at, :] = nsv
        sp_ref[at, :] = nsp
        d0 = xs_ref[0, pl.ds(k, 1), :] + (m0 * c0 + m1 * c2)
        d1 = xs_ref[1, pl.ds(k, 1), :] + (m0 * c1 + m1 * c3)
        d2 = xs_ref[2, pl.ds(k, 1), :] + (m2 * c0 + m3 * c2)
        d3 = xs_ref[3, pl.ds(k, 1), :] + (m2 * c1 + m3 * c3)
        coef_ref[0, at, :] = jnp.broadcast_to(d0, (per, lanes))
        coef_ref[1, at, :] = jnp.broadcast_to(d1, (per, lanes))
        coef_ref[2, at, :] = jnp.broadcast_to(d2, (per, lanes))
        coef_ref[3, at, :] = jnp.broadcast_to(d3, (per, lanes))
        return (nsv, nsp, d0, d1, d2, d3)

    sv, sp, d0, d1, d2, d3 = lax.fori_loop(
        0, levels, backward, (zero, zero, lower * one, flat, flat, lower * one), unroll=True
    )
    msg_ref[0:per, :] = lower * uv + upper * sv
    msg_ref[per : 2 * per, :] = lower * up + upper * sp
    for index, value in enumerate((d0, d1, d2, d3)):
        msg_ref[2 * per + index : 2 * per + index + 1, :] = upper * value


def arrive_solve_kernel(
    off_ref, bi_ref, fm_ref, bm_ref, w_ref, e_ref, s_ref, n_ref, sat_ref, res_ref, vel_ref, pres_ref,
    out_ref, sv_ref, sp_ref, msg_ref, coef_ref, force_ref, xs_ref,
):
    arrivals_into((w_ref, e_ref, s_ref, n_ref), sat_ref, res_ref, vel_ref, out_ref, force_ref)
    solve_into(off_ref, bi_ref, fm_ref, bm_ref, force_ref, pres_ref, sv_ref, sp_ref, msg_ref, coef_ref, xs_ref)


def correct_kernel(coef_ref, own_ref, recv_ref, sv_ref, sp_ref, nv_ref, np_ref):
    rows, lanes = sv_ref.shape
    per = (own_ref.shape[0] - 4) // 2
    own0 = own_ref[0:per, :]
    own1 = own_ref[per : 2 * per, :]
    extra = [recv_ref[2 * per + i : 2 * per + i + 1, :] for i in range(4)]
    v0 = recv_ref[0:per, :] + extra[0] * own0 + extra[1] * own1
    v1 = recv_ref[per : 2 * per, :] + extra[2] * own0 + extra[3] * own1
    phase = lax.broadcasted_iota(jnp.int32, (rows, lanes), 0) % per
    t0 = jnp.zeros((rows, lanes), jnp.float32)
    t1 = jnp.zeros((rows, lanes), jnp.float32)
    for p in range(per):
        t0 = jnp.where(phase == p, v0[p : p + 1], t0)
        t1 = jnp.where(phase == p, v1[p : p + 1], t1)
    nv_ref[...] = sv_ref[...] + (coef_ref[0] * t0 + coef_ref[1] * t1)
    np_ref[...] = sp_ref[...] + (coef_ref[2] * t0 + coef_ref[3] * t1)


def settle_and_solve(faces_in, sat_view, heat_res, vel_view, pres_view, levels, block_inverse, forward_map, backward_map):
    assert lax.axis_size("gz") == 2
    packet_width, slot_count = faces_in[0].shape
    record_width = packet_width - 1
    rows, lanes = sat_view.shape
    per = rows // levels
    offset = jnp.full((1,), lax.axis_index("gz") * levels, jnp.int32)
    smem = pl.BlockSpec(memory_space=pltpu.SMEM)
    vmem = pl.BlockSpec(memory_space=pltpu.VMEM)
    arrived, sv, sp, message, coef = pl.pallas_call(
        arrive_solve_kernel,
        out_shape=(
            jax.ShapeDtypeStruct((len(faces_in), record_width, slot_count), jnp.float32),
            jax.ShapeDtypeStruct((rows, lanes), jnp.float32),
            jax.ShapeDtypeStruct((rows, lanes), jnp.float32),
            jax.ShapeDtypeStruct((2 * per + 4, lanes), jnp.float32),
            jax.ShapeDtypeStruct((4, rows, lanes), jnp.float32),
        ),
        in_specs=[smem] * 4 + [vmem] * (len(faces_in) + 4),
        out_specs=(vmem,) * 5,
        scratch_shapes=[
            pltpu.VMEM((rows, lanes), jnp.float32),
            pltpu.VMEM((4, levels, lanes), jnp.float32),
        ],
        cost_estimate=pl.CostEstimate(
            flops=8 * sat_view.size * len(faces_in) * slot_count + 40 * rows * lanes,
            bytes_accessed=4 * (2 * packet_width) * len(faces_in) * slot_count + 40 * rows * lanes,
            transcendentals=len(faces_in) * slot_count,
        ),
    )(offset, block_inverse, forward_map, backward_map, *faces_in, sat_view, heat_res, vel_view, pres_view)
    received = lax.ppermute(message, "gz", [(0, 1), (1, 0)])
    new_v, new_p = pl.pallas_call(
        correct_kernel,
        out_shape=(
            jax.ShapeDtypeStruct((rows, lanes), jnp.float32),
            jax.ShapeDtypeStruct((rows, lanes), jnp.float32),
        ),
        in_specs=[vmem] * 5,
        out_specs=(vmem, vmem),
        cost_estimate=pl.CostEstimate(
            flops=8 * rows * lanes, bytes_accessed=32 * rows * lanes, transcendentals=0
        ),
    )(coef, message, received, sv, sp)
    return arrived, new_v, new_p


def along_x(packet_face, offset):
    return shifted(packet_face, "gx", offset)


def along_y(packet_face, offset):
    return shifted(packet_face, "gy", offset)


def body(
    droplets,
    cell_index,
    crossing,
    crossing_count,
    saturation,
    velocity,
    pressure,
    block_inverse,
    forward_map,
    backward_map,
):
    records = droplets[0, 0, 0]
    cell_ids = cell_index[0, 0, 0]
    levels = saturation.shape[0]
    view = (saturation.size // 128, 128)
    sat_view = saturation.reshape(view)
    faces_out, staying_view = emit_faces(
        records, cell_index, crossing[0, 0, 0], crossing_count[0, 0, 0]
    )
    from_west = along_x(faces_out[0], 1)
    from_east = along_x(faces_out[1], -1)
    from_south = along_y(faces_out[2], 1)
    from_north = along_y(faces_out[3], -1)
    resident, heat_res = settle_residents(
        records,
        cell_index.reshape(1, -1),
        staying_view.reshape(1, -1),
        sat_view,
    )
    arrived, solved_v, solved_p = settle_and_solve(
        (from_west, from_east, from_south, from_north),
        sat_view,
        heat_res,
        velocity.reshape(view),
        pressure.reshape(view),
        levels,
        block_inverse,
        forward_map,
        backward_map,
    )
    new_velocity = solved_v.reshape(velocity.shape)
    new_pressure = solved_p.reshape(pressure.shape)
    return (resident[None, None, None], arrived[None, None, None], new_velocity, new_pressure)


def solution(mesh):
    return jax.shard_map(
        body,
        mesh=mesh,
        in_specs=(
            P("gz", "gx", "gy", None, None),
            P("gz", "gx", "gy", None),
            P("gz", "gx", "gy", None, None),
            P("gz", "gx", "gy", None),
            P("gz", "gx", "gy", None),
            P("gz", "gx", "gy", None),
            P("gz", "gx", "gy", None),
            P(),
            P(),
            P(),
        ),
        out_specs=(
            P("gz", "gx", "gy", None, None),
            P("gz", "gx", "gy", None, None, None),
            P("gz", "gx", "gy", None),
            P("gz", "gx", "gy", None),
        ),
        check_vma=False,
    )
```
